256 devices in a mesh: rhs: 32 (over x, z_lo, y), node: 8 (over z_hi, core).
Axes of the slice: x: 4, y: 4, z: 8 (z_hi: 4, z_lo: 2; z = z_hi * 2 + z_lo), core: 2. Of those that a mesh axis runs over, the one named last changes fastest.
Arguments:
- right_side: float32 [8192, 8192], P('node', 'rhs'), may hold values from -6 to 6
- diag_inv: float32 [32, 256, 256], P('node', 'rhs'), may hold values from -1 to 1
- lower: float32 [32, 256, 256], P('node', 'rhs'), may hold values from -0.4375 to 0.4375
- factor_pattern: int32 [32, 4, 4], P('node'), may hold values 0 or 1
- jacobian: float32 [32, 256, 768], P('node', 'rhs'), may hold values from -0.078125 to 0.078125
- jacobian_pattern: int32 [32, 4, 12], P('node'), may hold values 0 or 1
Outputs:
- solution: float32 [8192, 8192], P('node', 'rhs')
- residual: float32 [8192, 8192], P('node', 'rhs')
The draws below stay inside these ranges and needn't reach their ends.
All inputs are finite; a program needn't handle non-finite values. No bound on the sum of `factor_pattern` or of `jacobian_pattern` on one device may be relied on, other than what follows from the above.
Results may differ from the reference program's by a relative error of at most 0.00021.
Values sent between devices are 32-bit elements; how exact they have to be, the bound alone decides.
A program may use at most 64 MiB of HBM per device.

```python
import jax
import jax.numpy as jnp
from jax import lax

B = 64
SN = 4
PANEL = 256
SUPER = 32
ORDER = 8192
RHS = 8192


def draw_diag_inv(key, part):
    key_diag, key_off = jax.random.split(key)
    diagonal_part = jax.random.uniform(key_diag, (SUPER, PANEL), jnp.float32, 0.75, 1.0)
    spread = jax.random.normal(key_off, (SUPER, PANEL, PANEL), jnp.float32) * (0.3 / PANEL ** 0.5)
    unit_matrix = jnp.eye(PANEL, dtype=jnp.float32)
    return spread * (1.0 - unit_matrix) + diagonal_part[:, :, None] * unit_matrix


def set_ends(values, key, least, high):
    extent = values.shape
    spot = [jax.random.randint(jax.random.fold_in(key, axis), (), 0, extent[axis]) for axis in range(len(extent))]
    values = values.at[tuple(spot)].set(least)
    longest = extent.index(max(extent))
    spot[longest] = (spot[longest] + 1) % extent[longest]
    return values.at[tuple(spot)].set(high)


def level_of(key, extent, cuts, smallest, high):
    loudness = 1.0
    for axis_at, parts in cuts:
        steps = jax.random.uniform(jax.random.fold_in(jax.random.fold_in(key, 6), axis_at), (parts,), jnp.float32, smallest / len(cuts), high / len(cuts))
        loudness = loudness * jnp.repeat(jnp.exp(steps), extent[axis_at] // parts).reshape((-1,) + (1,) * (len(extent) - 1 - axis_at))
    return loudness


def normal_values(rng, extent, scale, bound, cuts=(), held_as=jnp.bfloat16):
    loudness = level_of(rng, extent, cuts, -0.22, 0.18) if cuts else 1.0
    array = jax.random.normal(rng, extent, jnp.float32) * scale * loudness
    return jnp.minimum(jnp.maximum(array, -bound), bound).astype(held_as)


def setup_inputs(seed: int = 0) -> dict:
    seeds = jax.random.split(jax.random.key(seed), 7)
    right_side = normal_values(seeds[0], (ORDER, RHS), 1.0, 6.0, ((0, 8), (1, 32)), jnp.float32)
    diag_inv = draw_diag_inv(jax.random.fold_in(seeds[6], 71), 0)
    lower = normal_values(seeds[2], (SUPER, PANEL, PANEL), (SN * B * 4 // 5) ** -0.5, 0.4375, ((0, 8), (1, 32)), jnp.float32)
    factor_pattern = set_ends((jax.random.randint(seeds[3], (SUPER, SN, SN), 0, 4) < 3).astype(jnp.int32), jax.random.fold_in(seeds[3], 1), 0, 1)
    jacobian = normal_values(seeds[4], (SUPER, PANEL, 3 * PANEL), (24 * SN * B) ** -0.5, 0.078125, ((0, 8), (1, 32)), jnp.float32)
    jacobian_pattern = set_ends((jax.random.randint(seeds[5], (SUPER, SN, 3 * SN), 0, 4) < 3).astype(jnp.int32), jax.random.fold_in(seeds[5], 1), 0, 1)
    return {"right_side": right_side, "diag_inv": diag_inv, "lower": lower, "factor_pattern": factor_pattern, "jacobian": jacobian, "jacobian_pattern": jacobian_pattern}


HIGHEST_PREC = lax.Precision.HIGHEST
TRANSPOSED = (((0,), (0,)), ((), ()))


def expand_pattern(pattern):
    return jnp.repeat(jnp.repeat(pattern, B, axis=1), B, axis=2).astype(jnp.float32)


def reference(right_side, diag_inv, lower, factor_pattern, jacobian, jacobian_pattern):
    columns = right_side.shape[1]
    rhs_blocks = right_side.reshape(SUPER, PANEL, columns)
    masked_lower = lower * expand_pattern(factor_pattern)
    masked_jacobian = jacobian * expand_pattern(jacobian_pattern)

    def advance_down(previous, inputs):
        inv_block, low_block, rhs_block = inputs
        coupled = jnp.dot(low_block, previous, precision=HIGHEST_PREC)
        solved = jnp.dot(inv_block, rhs_block - coupled, precision=HIGHEST_PREC)
        return solved, solved

    zero_state = jnp.zeros((PANEL, columns), jnp.float32)
    unused, forward = lax.scan(advance_down, zero_state, (diag_inv, masked_lower, rhs_blocks))

    def advance_up(incoming, inputs):
        inv_block, low_block, forward_block = inputs
        solved = lax.dot_general(inv_block, forward_block - incoming, TRANSPOSED, precision=HIGHEST_PREC)
        passed = lax.dot_general(low_block, solved, TRANSPOSED, precision=HIGHEST_PREC)
        return passed, solved

    unused, solution = lax.scan(advance_up, zero_state, (diag_inv, masked_lower, forward), reverse=True)

    zero_block = jnp.zeros((1, PANEL, columns), jnp.float32)
    padded = jnp.concatenate([zero_block, solution, zero_block], axis=0)

    def residual_block(position):
        window = lax.dynamic_slice_in_dim(padded, position, 3, 0).reshape(3 * PANEL, columns)
        jac_block = lax.dynamic_index_in_dim(masked_jacobian, position, 0, keepdims=False)
        rhs_block = lax.dynamic_index_in_dim(rhs_blocks, position, 0, keepdims=False)
        return rhs_block - jnp.dot(jac_block, window, precision=HIGHEST_PREC)

    residual = lax.map(residual_block, jnp.arange(SUPER, dtype=jnp.int32))
    return solution.reshape(ORDER, columns), residual.reshape(ORDER, columns)
```

```python
import jax
import jax.numpy as jnp
from jax import lax
from jax.experimental import pallas as pl
from jax.experimental.pallas import tpu as pltpu
from jax.sharding import PartitionSpec as P

MESH_ID = pl.DeviceIdType.MESH
B = 64
W = 256
NODES = 8
HALF = 128


class Sems:
    def __init__(self, send, recv, local):
        self.send, self.recv, self.local = send, recv, local
        self.pairs = self.locals = 0

    def pair(self):
        k = self.pairs
        self.pairs += 1
        return self.send.at[k], self.recv.at[k]

    def one(self):
        k = self.locals
        self.locals += 1
        return self.local.at[k]


class Ring:
    def __init__(self, sems, where, pos, device_at):
        self.where, self.pos = where, pos
        self.up, self.down = device_at(lax.rem(pos + 1, 4)), device_at(lax.rem(pos + 3, 4))
        self.sems = {key: sems.pair() for key in ("u0", "d0", "u1", "d1", "fu", "fd")}
        self.started = []

    def at(self, q, step):
        return self.where(q, lax.rem(self.pos + step, 4))

    def copy(self, key, q, step, device, source=None):
        part = self.at(q, step)
        send, recv = self.sems[key]
        return pltpu.make_async_remote_copy(
            src_ref=part if source is None else source,
            dst_ref=part,
            send_sem=send,
            recv_sem=recv,
            device_id=device,
            device_id_type=MESH_ID,
        )

    def go(self, *args):
        copy = self.copy(*args)
        copy.start()
        self.started.append(copy)

    def direct(self, q, source=None):
        first, second = ("u", "d") if q == 0 else ("d", "u")
        for way in (first, second):
            self.go(f"{way}{q}", q, 0, self.up if way == "u" else self.down, source)

    def forward(self, q):
        if q == 0:
            self.copy("u0", 0, 3, self.up).wait_recv()
            self.go("fu", 0, 3, self.up)
        else:
            self.copy("d1", 1, 1, self.down).wait_recv()
            self.go("fd", 1, 1, self.down)

    def finish(self, q):
        if q == 0:
            self.copy("d0", 0, 1, self.down).wait_recv()
            self.copy("fu", 0, 2, self.up).wait_recv()
        else:
            self.copy("u1", 1, 3, self.up).wait_recv()
            self.copy("fd", 1, 2, self.down).wait_recv()

    def sent(self):
        for copy in self.started:
            copy.wait_send()


class Gather:
    def __init__(self, sems, buf, x, zl, y, device, y_first):
        self.own = buf.at[x, zl, y]

        def layer(q):
            return zl if q == 0 else 1 - zl

        if y_first:
            self.first = Ring(sems, lambda q, p: buf.at[x, layer(q), p], y, lambda p: device(x, zl, p))
            self.second = Ring(sems, lambda q, p: buf.at[p, layer(q)], x, lambda p: device(p, zl, y))
        else:
            self.first = Ring(sems, lambda q, p: buf.at[p, layer(q), y], x, lambda p: device(p, zl, y))
            self.second = Ring(sems, lambda q, p: buf.at[:, layer(q), p], y, lambda p: device(x, zl, p))
        send, recv = sems.pair()
        self.cross_sems = send, recv
        self.partner = device(x, 1 - zl, y)
        self.other = buf.at[x, 1 - zl, y]

    def cross(self, part, source):
        send, recv = self.cross_sems
        return pltpu.make_async_remote_copy(
            src_ref=source, dst_ref=part, send_sem=send, recv_sem=recv, device_id=self.partner, device_id_type=MESH_ID
        )

    def start(self, source=None):
        source = self.own if source is None else source
        self.sent_cross = self.cross(self.own, source)
        self.sent_cross.start()
        self.first.direct(0, source)

    def crossed(self):
        self.cross(self.other, self.other).wait_recv()
        self.first.direct(1)

    def sent(self):
        self.sent_cross.wait_send()
        self.first.sent()
        self.second.sent()


def split(value):
    high = value.astype(jnp.bfloat16)
    return high, (value - high.astype(jnp.float32)).astype(jnp.bfloat16)


def put_left(ref, value, at=0):
    high, low = split(value)
    for k, part in enumerate((high, low, high)):
        ref[:, at + k * W : at + (k + 1) * W] = part


def put_right(ref, value, col=0, row=0):
    high, low = split(value)
    cols = slice(col, col + value.shape[1])
    for k, part in enumerate((high, high, low)):
        ref[row + k * W : row + (k + 1) * W, cols] = part


def dot(left, right):
    return jnp.dot(left, right, preferred_element_type=jnp.float32)


def panel(buf, s):
    return [(buf[x] if s is None else buf[x, :, :, s]).reshape(B, W) for x in range(4)]


def masked_panel(buf, s, weights):
    return jnp.concatenate([part * weights(x) for x, part in enumerate(panel(buf, s))], axis=0)


def kernel(
    r_in, d_in, l_in, ml_in, j_in, mj_in,
    sol_out, res_out,
    gd, gl, gj0, gj1, gn, gp, rv, ml, mj, mn,
    left_d, left_dt, left_a, left_bt, left_p, left_x, left_j, left_e,
    right_rl, right_lt, right_f, right_b, right_ce, right_x,
    u, xl, f3, w0, xs, rs, c_in, e_in, c_out, e_out,
    send_sem, recv_sem, local_sem,
):
    rhs, node = lax.axis_index("rhs"), lax.axis_index("node")
    x, zl, y = rhs // 8, (rhs // 4) % 2, rhs % 4
    after, before = lax.rem(node + 1, NODES), lax.rem(node + NODES - 1, NODES)
    first, last = node == 0, node == NODES - 1

    def device(px, pz, py):
        return (px * 8 + pz * 4 + py, node)

    sems = Sems(send_sem, recv_sem, local_sem)

    def load(source, target):
        copy = pltpu.make_async_copy(source, target, sems.one())
        copy.start()
        return copy

    ml_load = load(ml_in, ml)
    own_d = load(d_in, gd.at[x, zl, y])
    own_l = load(l_in, gl.at[x, zl, y])
    j_loads = []
    for h, gj in enumerate((gj0, gj1)):
        for s in range(2):
            for c in range(3):
                j_loads.append(load(j_in.at[2 * h + s, :, W * c : W * (c + 1)], gj.at[x, zl, y, 3 * s + c]))
    r_load = load(r_in, rv)
    mj_load = load(mj_in, mj)

    barrier = pltpu.get_barrier_semaphore()
    peers = [device(x, 1 - zl, y)]
    peers += [device(x, zl, lax.rem(y + k, 4)) for k in (1, 3)]
    peers += [device(lax.rem(x + k, 4), zl, y) for k in (1, 3)]
    peers += [(rhs, after), (rhs, before)]
    for peer in peers:
        pl.semaphore_signal(barrier, inc=1, device_id=peer, device_id_type=MESH_ID)
    pl.semaphore_wait(barrier, len(peers))

    gathers = [
        Gather(sems, gd, x, zl, y, device, True),
        Gather(sems, gl, x, zl, y, device, False),
    ]
    later = [
        Gather(sems, gj0, x, zl, y, device, True),
        Gather(sems, gj1, x, zl, y, device, False),
    ]

    def remote(source, target, pair, to):
        return pltpu.make_async_remote_copy(
            src_ref=source,
            dst_ref=target,
            send_sem=pair[0],
            recv_sem=pair[1],
            device_id=(rhs, to),
            device_id_type=MESH_ID,
        )

    for g, source in zip(gathers, (d_in, l_in)):
        g.start(source)
    border = [
        remote(ml_in.at[0], mn, sems.pair(), before),
        remote(gl.at[:, :, :, 0], gn, sems.pair(), before),
        remote(gd.at[:, :, :, 3], gp, sems.pair(), after),
    ]
    border[0].start()
    own_d.wait()
    own_l.wait()
    for g in gathers:
        g.crossed()
    for q in (0, 1):
        for g in gathers:
            g.first.forward(q)
    for q in (0, 1):
        for g in gathers:
            g.first.finish(q)
            g.second.direct(q)
    r_load.wait()
    ml_load.wait()
    for copy in j_loads:
        copy.wait()
    mj_load.wait()
    border[0].wait_recv()
    for q in (0, 1):
        for g in gathers:
            g.second.forward(q)
    for q in (0, 1):
        for g in gathers:
            g.second.finish(q)
    for copy in border[1:]:
        copy.start()

    for g in later:
        g.start()

    for s in range(4):
        d = jnp.concatenate(panel(gd, s), axis=0)
        put_left(left_d.at[s], d)
        put_left(left_dt.at[s], d.T)
        low = masked_panel(gl, s, lambda k: ml[s, k : k + 1, :])
        right = right_rl.at[s]
        put_right(right, rv[W * s : W * (s + 1), :])
        put_right(right, low, W)
        if s == 0:
            put_left(left_e.at[0], -low.T)
        else:
            put_right(right_lt.at[s - 1], low.T)
        both = dot(left_d[s], right[...])
        if s == 0:
            put_right(right_f.at[0], both[:, :W])
            put_right(right_f.at[0], -both[:, W:], W)
        else:
            u[s] = both[:, :W]
            put_left(left_a.at[s], -both[:, W:])
    for s in range(1, 4):
        both = dot(left_a[s], right_f[s - 1])
        fs = u[s] + both[:, :W]
        put_right(right_f.at[s], fs)
        put_right(right_f.at[s], both[:, W:], W)
        if s == 3:
            f3[...] = fs
            put_left(left_p, both[:, W:])

    for g in later:
        g.crossed()

    for s in range(3):
        put_left(left_bt.at[s], -dot(left_dt[s], right_lt[s]))
    for s in range(3, -1, -1):
        both = dot(left_dt[s], right_f[s])
        if s < 3:
            both = both + dot(left_bt[s], right_b[...])
        if s > 0:
            put_right(right_b, both)
        xl[s] = both[:, :W]
        put_left(left_x.at[s], both[:, W:])

    for q in (0, 1):
        for g in later:
            g.first.forward(q)
    for q in (0, 1):
        for g in later:
            g.first.finish(q)
            g.second.direct(q)

    down = [(sems.pair(), slice(HALF * k, HALF * (k + 1))) for k in range(2)]
    up = [(sems.pair(), slice(HALF * k, HALF * (k + 1))) for k in range(2)]

    def send_down(k):
        return remote(c_out.at[k], c_in.at[k], down[k][0], after)

    def send_up(k):
        return remote(e_out.at[k], e_in.at[k], up[k][0], before)

    @pl.when(first)
    def _():
        c_in[...] = jnp.zeros_like(c_in)

    @pl.when(last)
    def _():
        e_in[...] = jnp.zeros_like(e_in)

    for k in range(2):
        cols = down[k][1]

        @pl.when(jnp.logical_not(first))
        def _():
            send_down(k).wait_recv()

        put_right(right_ce, c_in[k], HALF * k)

        @pl.when(jnp.logical_not(last))
        def _():
            c_out[k] = f3[:, cols] + dot(left_p[...], right_ce[: 3 * W, cols])
            send_down(k).start()

    for copy in border[1:]:
        copy.wait_recv()
    nxt = masked_panel(gn, None, lambda k: mn[k : k + 1, :])
    put_right(right_lt.at[3], nxt.T)
    for s in range(3, -1, -1):
        xe = -dot(left_dt[3], right_lt[3]) if s == 3 else dot(left_bt[s], right_b[:, :W])
        if s > 0:
            put_right(right_b, xe)
        put_left(left_x.at[s], xe, 3 * W)

    for k in range(2):
        cols = up[k][1]
        w0[k] = xl[0, :, cols] + dot(left_x[0, :, : 3 * W], right_ce[: 3 * W, cols])

        @pl.when(jnp.logical_not(last))
        def _():
            send_up(k).wait_recv()

        put_right(right_ce, e_in[k], HALF * k, 3 * W)

        @pl.when(jnp.logical_not(first))
        def _():
            e_out[k] = w0[k] + dot(left_x[0, :, 3 * W :], right_ce[3 * W :, cols])
            send_up(k).start()

    for q in (0, 1):
        for g in later:
            g.second.forward(q)

    stores = []
    for s in range(4):
        xa = xl[s] + dot(left_x[s], right_ce[...])
        xs[W * s : W * (s + 1), :] = xa
        put_right(right_x, xa, 0, 3 * W * (s + 1))
    stores.append(pltpu.make_async_copy(xs, sol_out, sems.one()))
    stores[0].start()
    for k in range(2):
        put_right(right_x, e_in[k], HALF * k, 3 * W * 5)
    t = dot(left_e[0], right_x[3 * W : 6 * W, :])
    t = t + jnp.concatenate([c_in[0], c_in[1]], axis=1)

    for q in (0, 1):
        for g in later:
            g.second.finish(q)
    prev = jnp.concatenate(panel(gp, None), axis=0)
    put_left(left_e.at[1], prev.T)
    put_right(right_b, t)
    t = dot(left_e[1], right_b[:, :W])
    put_right(right_x, jnp.where(first, 0.0, t))
    for s in range(4):
        gj = (gj0, gj1)[s // 2]
        for c in range(3):
            block = masked_panel(gj, 3 * (s % 2) + c, lambda k: mj[s, k : k + 1, W * c : W * (c + 1)])
            put_left(left_j, block, 3 * W * c)
        rs[W * s : W * (s + 1), :] = rv[W * s : W * (s + 1), :] - dot(
            left_j[...], right_x[3 * W * s : 3 * W * (s + 3), :]
        )
    stores.append(pltpu.make_async_copy(rs, res_out, sems.one()))
    stores[1].start()

    for g in gathers + later:
        g.sent()
    for copy in border:
        copy.wait_send()

    @pl.when(jnp.logical_not(last))
    def _():
        for k in range(2):
            send_down(k).wait_send()

    @pl.when(jnp.logical_not(first))
    def _():
        for k in range(2):
            send_up(k).wait_send()

    for copy in stores:
        copy.wait()


def on_device(right_side, diag_inv, lower, factor_pattern, jacobian, jacobian_pattern):
    weights_l = jnp.repeat(factor_pattern.astype(jnp.float32), B, axis=2)
    weights_j = jnp.repeat(jacobian_pattern.astype(jnp.float32), B, axis=2)
    f32, bf16 = jnp.float32, jnp.bfloat16
    out = jax.ShapeDtypeStruct(right_side.shape, f32)
    anywhere = pl.BlockSpec(memory_space=pl.ANY)
    vmem = pltpu.VMEM
    return pl.pallas_call(
        kernel,
        out_shape=(out, out),
        in_specs=[anywhere] * 6,
        out_specs=(anywhere, anywhere),
        scratch_shapes=[
            vmem((4, 2, 4, 4, 8, W), f32),
            vmem((4, 2, 4, 4, 8, W), f32),
            vmem((4, 2, 4, 6, 8, W), f32),
            vmem((4, 2, 4, 6, 8, W), f32),
            vmem((4, 2, 4, 8, W), f32),
            vmem((4, 2, 4, 8, W), f32),
            vmem((4 * W, W), f32),
            vmem((4, 4, W), f32),
            vmem((4, 4, 3 * W), f32),
            vmem((4, W), f32),
            vmem((4, W, 3 * W), bf16),
            vmem((4, W, 3 * W), bf16),
            vmem((4, W, 3 * W), bf16),
            vmem((3, W, 3 * W), bf16),
            vmem((W, 3 * W), bf16),
            vmem((4, W, 6 * W), bf16),
            vmem((W, 9 * W), bf16),
            vmem((2, W, 3 * W), bf16),
            vmem((4, 3 * W, 2 * W), bf16),
            vmem((4, 3 * W, W), bf16),
            vmem((4, 3 * W, 2 * W), bf16),
            vmem((3 * W, 2 * W), bf16),
            vmem((6 * W, W), bf16),
            vmem((18 * W, W), bf16),
            vmem((4, W, W), f32),
            vmem((4, W, W), f32),
            vmem((W, W), f32),
            vmem((2, W, HALF), f32),
            vmem((4 * W, W), f32),
            vmem((4 * W, W), f32),
            vmem((2, W, HALF), f32),
            vmem((2, W, HALF), f32),
            vmem((2, W, HALF), f32),
            vmem((2, W, HALF), f32),
            pltpu.SemaphoreType.DMA((64,)),
            pltpu.SemaphoreType.DMA((64,)),
            pltpu.SemaphoreType.DMA((24,)),
        ],
        compiler_params=pltpu.CompilerParams(
            collective_id=0, has_side_effects=True, vmem_limit_bytes=60 * 1024 * 1024
        ),
    )(right_side, diag_inv, lower, weights_l, jacobian, weights_j)


def solution(mesh):
    in_specs = (
        P("node", "rhs"),
        P("node", "rhs", None),
        P("node", "rhs", None),
        P("node", None, None),
        P("node", "rhs", None),
        P("node", None, None),
    )
    out_specs = (P("node", "rhs"), P("node", "rhs"))
    return jax.shard_map(on_device, mesh=mesh, in_specs=in_specs, out_specs=out_specs, check_vma=False)
```

```python
import jax
import jax.numpy as jnp
from jax import lax
from jax.experimental import pallas as pl
from jax.experimental.pallas import tpu as pltpu
from jax.sharding import PartitionSpec as P

MESH_ID = pl.DeviceIdType.MESH
B = 64
W = 256
NODES = 8
HALF = 128


class Sems:
    def __init__(self, send, recv, local):
        self.send, self.recv, self.local = send, recv, local
        self.pairs = self.locals = 0

    def pair(self):
        k = self.pairs
        self.pairs += 1
        return self.send.at[k], self.recv.at[k]

    def one(self):
        k = self.locals
        self.locals += 1
        return self.local.at[k]


class Ring:
    def __init__(self, sems, where, pos, device_at):
        self.where, self.pos = where, pos
        self.up, self.down = device_at(lax.rem(pos + 1, 4)), device_at(lax.rem(pos + 3, 4))
        self.sems = {key: sems.pair() for key in ("u0", "d0", "u1", "d1", "fu", "fd")}
        self.started = {}

    def at(self, q, step):
        return self.where(q, lax.rem(self.pos + step, 4))

    def copy(self, key, q, step, device, source=None):
        part = self.at(q, step)
        send, recv = self.sems[key]
        return pltpu.make_async_remote_copy(
            src_ref=part if source is None else source,
            dst_ref=part,
            send_sem=send,
            recv_sem=recv,
            device_id=device,
            device_id_type=MESH_ID,
        )

    def go(self, key, *args):
        self.started[key] = args
        self.copy(key, *args).start()

    def direct(self, q, source=None):
        first, second = ("u", "d") if q == 0 else ("d", "u")
        for way in (first, second):
            self.go(f"{way}{q}", q, 0, self.up if way == "u" else self.down, source)

    def forward(self, q):
        if q == 0:
            self.copy("u0", 0, 3, self.up).wait_recv()
            self.go("fu", 0, 3, self.up)
        else:
            self.copy("d1", 1, 1, self.down).wait_recv()
            self.go("fd", 1, 1, self.down)

    def finish(self, q):
        if q == 0:
            self.copy("d0", 0, 1, self.down).wait_recv()
            self.copy("fu", 0, 2, self.up).wait_recv()
        else:
            self.copy("u1", 1, 3, self.up).wait_recv()
            self.copy("fd", 1, 2, self.down).wait_recv()

    def sent(self):
        for key, args in self.started.items():
            self.copy(key, *args).wait_send()


class Gather:
    def __init__(self, sems, buf, x, zl, y, device, y_first):
        self.own = buf.at[x, zl, y]

        def layer(q):
            return zl if q == 0 else 1 - zl

        if y_first:
            self.first = Ring(sems, lambda q, p: buf.at[x, layer(q), p], y, lambda p: device(x, zl, p))
            self.second = Ring(sems, lambda q, p: buf.at[p, layer(q)], x, lambda p: device(p, zl, y))
        else:
            self.first = Ring(sems, lambda q, p: buf.at[p, layer(q), y], x, lambda p: device(p, zl, y))
            self.second = Ring(sems, lambda q, p: buf.at[:, layer(q), p], y, lambda p: device(x, zl, p))
        send, recv = sems.pair()
        self.cross_sems = send, recv
        self.partner = device(x, 1 - zl, y)
        self.other = buf.at[x, 1 - zl, y]

    def cross(self, part, source):
        send, recv = self.cross_sems
        return pltpu.make_async_remote_copy(
            src_ref=source, dst_ref=part, send_sem=send, recv_sem=recv, device_id=self.partner, device_id_type=MESH_ID
        )

    def start(self, source=None):
        source = self.own if source is None else source
        self.sent_cross = self.cross(self.own, source)
        self.sent_cross.start()
        self.first.direct(0, source)

    def crossed(self):
        self.cross(self.other, self.other).wait_recv()
        self.first.direct(1)

    def sent(self):
        self.sent_cross.wait_send()
        self.first.sent()
        self.second.sent()


def split(value):
    high = value.astype(jnp.bfloat16)
    return high, (value - high.astype(jnp.float32)).astype(jnp.bfloat16)


def put_left(ref, value, at=0):
    high, low = split(value)
    for k, part in enumerate((high, low, high)):
        ref[:, at + k * W : at + (k + 1) * W] = part


def put_right(ref, value, col=0, row=0):
    high, low = split(value)
    cols = slice(col, col + value.shape[1])
    for k, part in enumerate((high, high, low)):
        ref[row + k * W : row + (k + 1) * W, cols] = part


def dot(left, right):
    return jnp.dot(left, right, preferred_element_type=jnp.float32)


def panel(buf, s):
    return [(buf[x] if s is None else buf[x, :, :, s]).reshape(B, W) for x in range(4)]


def masked_panel(buf, s, weights):
    return jnp.concatenate([part * weights(x) for x, part in enumerate(panel(buf, s))], axis=0)


def rows_of(pattern):
    block = lax.broadcasted_iota(jnp.int32, (4, W), 1) // B
    values = pattern.astype(jnp.float32)
    out = jnp.zeros((4, W), jnp.float32)
    for k in range(4):
        out = jnp.where(block == k, values[:, k : k + 1], out)
    return out


def kernel(
    r_in, d_in, l_in, pl_in, j_in, pj_in,
    xs, rs,
    gd, gl, gj0, gj1, gn, gp, rv, pat_l, pat_j, ml, mj, mn,
    left_d, left_dt, left_a, left_bt, left_p, left_x, left_j, left_e,
    right_rl, right_lt, right_f, right_b, right_ce, right_x,
    u, xl, f3, w0, c_in, e_in, c_out, e_out,
    send_sem, recv_sem, local_sem,
):
    rhs, node = lax.axis_index("rhs"), lax.axis_index("node")
    x, zl, y = rhs // 8, (rhs // 4) % 2, rhs % 4
    after, before = lax.rem(node + 1, NODES), lax.rem(node + NODES - 1, NODES)
    first, last = node == 0, node == NODES - 1

    def device(px, pz, py):
        return (px * 8 + pz * 4 + py, node)

    sems = Sems(send_sem, recv_sem, local_sem)

    def load(source, target):
        copy = pltpu.make_async_copy(source, target, sems.one())
        copy.start()
        return copy

    barrier = pltpu.get_barrier_semaphore()
    peers = [device(x, 1 - zl, y)]
    peers += [device(x, zl, lax.rem(y + k, 4)) for k in (1, 3)]
    peers += [device(lax.rem(x + k, 4), zl, y) for k in (1, 3)]
    peers += [(rhs, after), (rhs, before)]
    for peer in peers:
        pl.semaphore_signal(barrier, inc=1, device_id=peer, device_id_type=MESH_ID)
    pl.semaphore_wait(barrier, len(peers))

    gathers = [
        Gather(sems, gd, x, zl, y, device, True),
        Gather(sems, gl, x, zl, y, device, False),
    ]
    later = [
        Gather(sems, gj0, x, zl, y, device, True),
        Gather(sems, gj1, x, zl, y, device, False),
    ]

    def remote(source, target, pair, to):
        return pltpu.make_async_remote_copy(
            src_ref=source,
            dst_ref=target,
            send_sem=pair[0],
            recv_sem=pair[1],
            device_id=(rhs, to),
            device_id_type=MESH_ID,
        )

    for g, source in zip(gathers, (d_in, l_in)):
        g.start(source)
    border = [
        remote(ml.at[0], mn, sems.pair(), before),
        remote(gl.at[:, :, :, 0], gn, sems.pair(), before),
        remote(gd.at[:, :, :, 3], gp, sems.pair(), after),
    ]
    own_d = load(d_in, gd.at[x, zl, y])
    own_l = load(l_in, gl.at[x, zl, y])
    pat_loads = [load(pl_in, pat_l), load(pj_in, pat_j)]
    j_loads = []
    for h, gj in enumerate((gj0, gj1)):
        for s in range(2):
            for c in range(3):
                j_loads.append(load(j_in.at[2 * h + s, :, W * c : W * (c + 1)], gj.at[x, zl, y, 3 * s + c]))
    r_load = load(r_in, rv)
    own_d.wait()
    own_l.wait()
    for g in gathers:
        g.crossed()
    for q in (0, 1):
        for g in gathers:
            g.first.forward(q)
    for q in (0, 1):
        for g in gathers:
            g.first.finish(q)
            g.second.direct(q)
    r_load.wait()
    for copy in pat_loads + j_loads:
        copy.wait()
    for s in range(4):
        ml[s] = rows_of(pat_l[s])
        for c in range(3):
            mj[s, :, W * c : W * (c + 1)] = rows_of(pat_j[s, :, 4 * c : 4 * (c + 1)])
    for q in (0, 1):
        for g in gathers:
            g.second.forward(q)
    for q in (0, 1):
        for g in gathers:
            g.second.finish(q)
    for copy in border[:2]:
        copy.start()

    for g in later:
        g.start()

    for s in range(4):
        d = jnp.concatenate(panel(gd, s), axis=0)
        put_left(left_d.at[s], d)
        put_left(left_dt.at[s], d.T)
        low = masked_panel(gl, s, lambda k: ml[s, k : k + 1, :])
        right = right_rl.at[s]
        put_right(right, rv[W * s : W * (s + 1), :])
        put_right(right, low, W)
        if s == 0:
            put_left(left_e.at[0], -low.T)
        else:
            put_right(right_lt.at[s - 1], low.T)
        both = dot(left_d[s], right[...])
        if s == 0:
            put_right(right_f.at[0], both[:, :W])
            put_right(right_f.at[0], -both[:, W:], W)
        else:
            u[s] = both[:, :W]
            put_left(left_a.at[s], -both[:, W:])
    for s in range(1, 4):
        both = dot(left_a[s], right_f[s - 1])
        fs = u[s] + both[:, :W]
        put_right(right_f.at[s], fs)
        put_right(right_f.at[s], both[:, W:], W)
        if s == 3:
            f3[...] = fs
            put_left(left_p, both[:, W:])

    chunks = [slice(HALF * k, HALF * (k + 1)) for k in range(2)]
    down = [sems.pair() for k in range(2)]
    up = [sems.pair() for k in range(2)]

    def send_down(k):
        return remote(c_out.at[k], c_in.at[k], down[k], after)

    def send_up(k):
        return remote(e_out.at[k], e_in.at[k], up[k], before)

    @pl.when(first)
    def _():
        c_in[...] = jnp.zeros_like(c_in)

    @pl.when(last)
    def _():
        e_in[...] = jnp.zeros_like(e_in)

    def relay_down():
        for k, cols in enumerate(chunks):

            @pl.when(jnp.logical_not(first))
            def _():
                send_down(k).wait_recv()

            put_right(right_ce, c_in[k], HALF * k)

            @pl.when(jnp.logical_not(last))
            def _():
                c_out[k] = f3[:, cols] + dot(left_p[...], right_ce[: 3 * W, cols])
                send_down(k).start()

    pl.when(node < 2)(relay_down)

    for s in range(3):
        put_left(left_bt.at[s], -dot(left_dt[s], right_lt[s]))
    for s in range(3, -1, -1):
        both = dot(left_dt[s], right_f[s])
        if s < 3:
            both = both + dot(left_bt[s], right_b[...])
        if s > 0:
            put_right(right_b, both)
        xl[s] = both[:, :W]
        put_left(left_x.at[s], both[:, W:])

    pl.when((node == 2) | (node == 3))(relay_down)

    for g in later:
        g.crossed()
    for q in (0, 1):
        for g in later:
            g.first.forward(q)
    for q in (0, 1):
        for g in later:
            g.first.finish(q)
            g.second.direct(q)

    pl.when(node > 3)(relay_down)

    border[2].start()
    for copy in border[:2]:
        copy.wait_recv()
    nxt = masked_panel(gn, None, lambda k: mn[k : k + 1, :])
    put_right(right_lt.at[3], nxt.T)
    for s in range(3, -1, -1):
        xe = -dot(left_dt[3], right_lt[3]) if s == 3 else dot(left_bt[s], right_b[:, :W])
        if s > 0:
            put_right(right_b, xe)
        put_left(left_x.at[s], xe, 3 * W)

    def forward_later():
        for q in (0, 1):
            for g in later:
                g.second.forward(q)

    pl.when(jnp.logical_not(last))(forward_later)

    for k, cols in enumerate(chunks):
        w0[k] = xl[0, :, cols] + dot(left_x[0, :, : 3 * W], right_ce[: 3 * W, cols])

        @pl.when(jnp.logical_not(last))
        def _():
            send_up(k).wait_recv()

        put_right(right_ce, e_in[k], HALF * k, 3 * W)

        @pl.when(jnp.logical_not(first))
        def _():
            e_out[k] = w0[k] + dot(left_x[0, :, 3 * W :], right_ce[3 * W :, cols])
            send_up(k).start()

    pl.when(last)(forward_later)

    for s in range(4):
        xa = xl[s] + dot(left_x[s], right_ce[...])
        xs[W * s : W * (s + 1), :] = xa
        put_right(right_x, xa, 0, 3 * W * (s + 1))
    for k in range(2):
        put_right(right_x, e_in[k], HALF * k, 3 * W * 5)
    t = dot(left_e[0], right_x[3 * W : 6 * W, :])
    t = t + jnp.concatenate([c_in[0], c_in[1]], axis=1)

    for q in (0, 1):
        for g in later:
            g.second.finish(q)
    border[2].wait_recv()
    prev = jnp.concatenate(panel(gp, None), axis=0)
    put_left(left_e.at[1], prev.T)
    put_right(right_b, t)
    t = dot(left_e[1], right_b[:, :W])
    put_right(right_x, jnp.where(first, 0.0, t))
    for s in range(4):
        gj = (gj0, gj1)[s // 2]
        for c in range(3):
            block = masked_panel(gj, 3 * (s % 2) + c, lambda k: mj[s, k : k + 1, W * c : W * (c + 1)])
            put_left(left_j, block, 3 * W * c)
        rs[W * s : W * (s + 1), :] = rv[W * s : W * (s + 1), :] - dot(
            left_j[...], right_x[3 * W * s : 3 * W * (s + 3), :]
        )

    for g in gathers + later:
        g.sent()
    for copy in border:
        copy.wait_send()

    @pl.when(jnp.logical_not(last))
    def _():
        for k in range(2):
            send_down(k).wait_send()

    @pl.when(jnp.logical_not(first))
    def _():
        for k in range(2):
            send_up(k).wait_send()


def on_device(*args):
    f32, bf16 = jnp.float32, jnp.bfloat16
    out = jax.ShapeDtypeStruct(args[0].shape, f32)
    hbm = pl.BlockSpec(memory_space=pltpu.HBM)
    vmem = pltpu.VMEM
    return pl.pallas_call(
        kernel,
        out_shape=(out, out),
        in_specs=[hbm] * 6,
        out_specs=(pl.BlockSpec(memory_space=vmem),) * 2,
        scratch_shapes=[
            vmem((4, 2, 4, 4, 8, W), f32),
            vmem((4, 2, 4, 4, 8, W), f32),
            vmem((4, 2, 4, 6, 8, W), f32),
            vmem((4, 2, 4, 6, 8, W), f32),
            vmem((4, 2, 4, 8, W), f32),
            vmem((4, 2, 4, 8, W), f32),
            vmem((4 * W, W), f32),
            vmem((4, 4, 4), jnp.int32),
            vmem((4, 4, 12), jnp.int32),
            vmem((4, 4, W), f32),
            vmem((4, 4, 3 * W), f32),
            vmem((4, W), f32),
            vmem((4, W, 3 * W), bf16),
            vmem((4, W, 3 * W), bf16),
            vmem((4, W, 3 * W), bf16),
            vmem((3, W, 3 * W), bf16),
            vmem((W, 3 * W), bf16),
            vmem((4, W, 6 * W), bf16),
            vmem((W, 9 * W), bf16),
            vmem((2, W, 3 * W), bf16),
            vmem((4, 3 * W, 2 * W), bf16),
            vmem((4, 3 * W, W), bf16),
            vmem((4, 3 * W, 2 * W), bf16),
            vmem((3 * W, 2 * W), bf16),
            vmem((6 * W, W), bf16),
            vmem((18 * W, W), bf16),
            vmem((4, W, W), f32),
            vmem((4, W, W), f32),
            vmem((W, W), f32),
            vmem((2, W, HALF), f32),
            vmem((2, W, HALF), f32),
            vmem((2, W, HALF), f32),
            vmem((2, W, HALF), f32),
            vmem((2, W, HALF), f32),
            pltpu.SemaphoreType.DMA((64,)),
            pltpu.SemaphoreType.DMA((64,)),
            pltpu.SemaphoreType.DMA((24,)),
        ],
        compiler_params=pltpu.CompilerParams(
            collective_id=0, has_side_effects=True, vmem_limit_bytes=48 * 1024 * 1024
        ),
    )(*[pltpu.with_memory_space_constraint(a, pltpu.HBM) for a in args])


def solution(mesh):
    in_specs = (
        P("node", "rhs"),
        P("node", "rhs", None),
        P("node", "rhs", None),
        P("node", None, None),
        P("node", "rhs", None),
        P("node", None, None),
    )
    out_specs = (P("node", "rhs"), P("node", "rhs"))
    return jax.shard_map(on_device, mesh=mesh, in_specs=in_specs, out_specs=out_specs, check_vma=False)
```

```python
import jax
import jax.numpy as jnp
from jax import lax
from jax.experimental import pallas as pl
from jax.experimental.pallas import tpu as pltpu
from jax.sharding import PartitionSpec as P

MESH_ID = pl.DeviceIdType.MESH
B = 64
W = 256
NODES = 8
CHUNKS = 4
PART = W // CHUNKS


class Sems:
    def __init__(self, send, recv, local):
        self.send, self.recv, self.local = send, recv, local
        self.pairs = self.locals = 0

    def pair(self):
        k = self.pairs
        self.pairs += 1
        return self.send.at[k], self.recv.at[k]

    def one(self):
        k = self.locals
        self.locals += 1
        return self.local.at[k]


class Ring:
    def __init__(self, sems, where, pos, device_at):
        self.where, self.pos = where, pos
        self.up, self.down = device_at(lax.rem(pos + 1, 4)), device_at(lax.rem(pos + 3, 4))
        self.sems = {key: sems.pair() for key in ("u0", "d0", "u1", "d1", "fu", "fd")}
        self.started = {}

    def at(self, q, step):
        return self.where(q, lax.rem(self.pos + step, 4))

    def copy(self, key, q, step, device, source=None):
        part = self.at(q, step)
        send, recv = self.sems[key]
        return pltpu.make_async_remote_copy(
            src_ref=part if source is None else source,
            dst_ref=part,
            send_sem=send,
            recv_sem=recv,
            device_id=device,
            device_id_type=MESH_ID,
        )

    def go(self, key, *args):
        self.started[key] = args
        self.copy(key, *args).start()

    def direct(self, q, source=None):
        first, second = ("u", "d") if q == 0 else ("d", "u")
        for way in (first, second):
            self.go(f"{way}{q}", q, 0, self.up if way == "u" else self.down, source)

    def forward(self, q):
        if q == 0:
            self.copy("u0", 0, 3, self.up).wait_recv()
            self.go("fu", 0, 3, self.up)
        else:
            self.copy("d1", 1, 1, self.down).wait_recv()
            self.go("fd", 1, 1, self.down)

    def finish(self, q):
        if q == 0:
            self.copy("d0", 0, 1, self.down).wait_recv()
            self.copy("fu", 0, 2, self.up).wait_recv()
        else:
            self.copy("u1", 1, 3, self.up).wait_recv()
            self.copy("fd", 1, 2, self.down).wait_recv()

    def sent(self):
        for key, args in self.started.items():
            self.copy(key, *args).wait_send()


class Gather:
    def __init__(self, sems, buf, x, zl, y, device, y_first):
        self.own = buf.at[x, zl, y]

        def layer(q):
            return zl if q == 0 else 1 - zl

        if y_first:
            self.first = Ring(sems, lambda q, p: buf.at[x, layer(q), p], y, lambda p: device(x, zl, p))
            self.second = Ring(sems, lambda q, p: buf.at[p, layer(q)], x, lambda p: device(p, zl, y))
        else:
            self.first = Ring(sems, lambda q, p: buf.at[p, layer(q), y], x, lambda p: device(p, zl, y))
            self.second = Ring(sems, lambda q, p: buf.at[:, layer(q), p], y, lambda p: device(x, zl, p))
        send, recv = sems.pair()
        self.cross_sems = send, recv
        self.partner = device(x, 1 - zl, y)
        self.other = buf.at[x, 1 - zl, y]

    def cross(self, part, source):
        send, recv = self.cross_sems
        return pltpu.make_async_remote_copy(
            src_ref=source, dst_ref=part, send_sem=send, recv_sem=recv, device_id=self.partner, device_id_type=MESH_ID
        )

    def start(self, source=None):
        source = self.own if source is None else source
        self.sent_cross = self.cross(self.own, source)
        self.sent_cross.start()
        self.first.direct(0, source)

    def crossed(self):
        self.cross(self.other, self.other).wait_recv()
        self.first.direct(1)

    def sent(self):
        self.sent_cross.wait_send()
        self.first.sent()
        self.second.sent()


def split(value):
    high = value.astype(jnp.bfloat16)
    return high, (value - high.astype(jnp.float32)).astype(jnp.bfloat16)


def put_left(ref, value, at=0):
    high, low = split(value)
    for k, part in enumerate((high, low, high)):
        ref[:, at + k * W : at + (k + 1) * W] = part


def put_right(ref, value, col=0, row=0):
    high, low = split(value)
    cols = slice(col, col + value.shape[1])
    for k, part in enumerate((high, high, low)):
        ref[row + k * W : row + (k + 1) * W, cols] = part


def dot(left, right):
    return jnp.dot(left, right, preferred_element_type=jnp.float32)


def panel(buf, s):
    return [(buf[x] if s is None else buf[x, :, :, s]).reshape(B, W) for x in range(4)]


def masked_panel(buf, s, weights):
    return jnp.concatenate([part * weights(x) for x, part in enumerate(panel(buf, s))], axis=0)


def rows_of(pattern):
    block = lax.broadcasted_iota(jnp.int32, (4, W), 1) // B
    values = pattern.astype(jnp.float32)
    out = jnp.zeros((4, W), jnp.float32)
    for k in range(4):
        out = jnp.where(block == k, values[:, k : k + 1], out)
    return out


def kernel(
    r_in, d_in, l_in, pl_in, j_in, pj_in,
    xs, rs,
    gd, gl, gj0, gj1, gn, gp, rv, pat_l, pat_j, ml, mj, mn,
    left_d, left_dt, left_a, left_bt, left_x, left_j, left_e, left_r, left_m, left_g, left_n,
    right_rl, right_lt, right_f, right_b, right_x, right_p, right_q, right_g, right_u, right_c, right_e,
    u, xl, gt, pt, ga, pa, gg, ct, cn, w0, x0, wb, xb, ht, en, c_in, e_in, c_out, e_out,
    send_sem, recv_sem, local_sem,
):
    rhs, node = lax.axis_index("rhs"), lax.axis_index("node")
    x, zl, y = rhs // 8, (rhs // 4) % 2, rhs % 4
    after, before = lax.rem(node + 1, NODES), lax.rem(node + NODES - 1, NODES)
    first = node == 0
    chip, odd = node // 2, node % 2 == 1
    even = jnp.logical_not(odd)
    partner = node + 1 - 2 * (node % 2)
    two_after, two_before = lax.rem(node + 2, NODES), lax.rem(node + NODES - 2, NODES)

    def device(px, pz, py):
        return (px * 8 + pz * 4 + py, node)

    sems = Sems(send_sem, recv_sem, local_sem)

    def load(source, target):
        copy = pltpu.make_async_copy(source, target, sems.one())
        copy.start()
        return copy

    barrier = pltpu.get_barrier_semaphore()
    peers = [device(x, 1 - zl, y)]
    peers += [device(x, zl, lax.rem(y + k, 4)) for k in (1, 3)]
    peers += [device(lax.rem(x + k, 4), zl, y) for k in (1, 3)]
    peers += [(rhs, to) for to in (after, before, two_after, two_before)]
    for peer in peers:
        pl.semaphore_signal(barrier, inc=1, device_id=peer, device_id_type=MESH_ID)
    pl.semaphore_wait(barrier, len(peers))

    gathers = [
        Gather(sems, gd, x, zl, y, device, True),
        Gather(sems, gl, x, zl, y, device, False),
    ]
    later = [
        Gather(sems, gj0, x, zl, y, device, True),
        Gather(sems, gj1, x, zl, y, device, False),
    ]

    def remote(source, target, pair, to):
        return pltpu.make_async_remote_copy(
            src_ref=source,
            dst_ref=target,
            send_sem=pair[0],
            recv_sem=pair[1],
            device_id=(rhs, to),
            device_id_type=MESH_ID,
        )

    for g, source in zip(gathers, (d_in, l_in)):
        g.start(source)
    border = [
        remote(ml.at[0], mn, sems.pair(), before),
        remote(gl.at[:, :, :, 0], gn, sems.pair(), before),
        remote(gd.at[:, :, :, 3], gp, sems.pair(), after),
    ]
    own_d = load(d_in, gd.at[x, zl, y])
    own_l = load(l_in, gl.at[x, zl, y])
    pat_loads = [load(pl_in, pat_l), load(pj_in, pat_j)]
    j_loads = []
    for h, gj in enumerate((gj0, gj1)):
        for s in range(2):
            for c in range(3):
                j_loads.append(load(j_in.at[2 * h + s, :, W * c : W * (c + 1)], gj.at[x, zl, y, 3 * s + c]))
    r_load = load(r_in, rv)
    own_d.wait()
    own_l.wait()
    for g in gathers:
        g.crossed()
    for q in (0, 1):
        for g in gathers:
            g.first.forward(q)
    for q in (0, 1):
        for g in gathers:
            g.first.finish(q)
            g.second.direct(q)
    r_load.wait()
    for copy in pat_loads + j_loads:
        copy.wait()
    for s in range(4):
        ml[s] = rows_of(pat_l[s])
        for c in range(3):
            mj[s, :, W * c : W * (c + 1)] = rows_of(pat_j[s, :, 4 * c : 4 * (c + 1)])
    for q in (0, 1):
        for g in gathers:
            g.second.forward(q)
    for q in (0, 1):
        for g in gathers:
            g.second.finish(q)
    for copy in border[:2]:
        copy.start()

    for g in later:
        g.start()

    for s in range(4):
        d = jnp.concatenate(panel(gd, s), axis=0)
        put_left(left_d.at[s], d)
        put_left(left_dt.at[s], d.T)
        low = masked_panel(gl, s, lambda k: ml[s, k : k + 1, :])
        right = right_rl.at[s]
        put_right(right, rv[W * s : W * (s + 1), :])
        put_right(right, low, W)
        if s == 0:
            put_left(left_e.at[0], -low.T)
        else:
            put_right(right_lt.at[s - 1], low.T)
        both = dot(left_d[s], right[...])
        if s == 0:
            put_right(right_f.at[0], both[:, :W])
            put_right(right_f.at[0], -both[:, W:], W)
        else:
            u[s] = both[:, :W]
            put_left(left_a.at[s], -both[:, W:])
    for s in range(1, 4):
        both = dot(left_a[s], right_f[s - 1])
        fs = u[s] + both[:, :W]
        put_right(right_f.at[s], fs)
        put_right(right_f.at[s], both[:, W:], W)
        if s == 3:
            gt[...] = fs.T
            pt[...] = both[:, W:].T

    chunks = [slice(PART * k, PART * (k + 1)) for k in range(CHUNKS)]
    down, fan_down, up, fan_up = [[sems.pair() for k in range(CHUNKS)] for _ in range(4)]
    hand = [
        remote(gt, ga, sems.pair(), partner),
        remote(pt, pa, sems.pair(), partner),
        remote(w0, wb, sems.pair(), partner),
        remote(x0, xb, sems.pair(), partner),
    ]

    def send_down(k):
        return remote(c_out.at[k], c_in.at[k], down[k], two_after)

    def share_down(k):
        return remote(c_in.at[k], c_in.at[k], fan_down[k], partner)

    def send_up(k):
        return remote(e_out.at[k], e_in.at[k], up[k], two_before)

    def share_up(k):
        return remote(e_in.at[k], e_in.at[k], fan_up[k], partner)

    @pl.when(even)
    def _():
        hand[0].start()
        hand[1].start()

    @pl.when(chip == 0)
    def _():
        c_in[...] = jnp.zeros_like(c_in)
        left_m[...] = jnp.zeros_like(left_m)

    @pl.when(chip == 3)
    def _():
        e_in[...] = jnp.zeros_like(e_in)

    @pl.when(odd)
    def _():
        put_right(right_p, pt[...])
        hand[0].wait_recv()
        put_left(left_g, ga[...])
        gg[...] = gt[...] + dot(left_g[...], right_p[...])

    @pl.when(odd & (chip == 0))
    def _():
        for k, rows in enumerate(chunks):
            c_out[k] = gg[rows, :]
            send_down(k).start()

    @pl.when(odd)
    def _():
        hand[1].wait_recv()
        put_left(left_g, pa[...])
        put_right(right_g, pa[...])
        put_right(right_q, dot(left_g[...], right_p[...]))

    def relay_down():
        for k, rows in enumerate(chunks):
            send_down(k).wait_recv()
            put_left(left_m.at[rows], c_in[k])

            @pl.when(chip < 3)
            def _():
                c_out[k] = gg[rows, :] + dot(left_m[rows, :], right_q[...])
                send_down(k).start()

            share_down(k).start()

    for s in range(3):
        put_left(left_bt.at[s], -dot(left_dt[s], right_lt[s]))
    for s in range(3, -1, -1):
        both = dot(left_dt[s], right_f[s])
        if s < 3:
            both = both + dot(left_bt[s], right_b[...])
        if s > 0:
            put_right(right_b, both)
        xl[s] = both[:, :W]
        put_left(left_x.at[s], both[:, W:])

    for g in later:
        g.crossed()
    pl.when(odd & (chip == 1))(relay_down)

    for q in (0, 1):
        for g in later:
            g.first.forward(q)
    for q in (0, 1):
        for g in later:
            g.first.finish(q)
            g.second.direct(q)

    for copy in border[:2]:
        copy.wait_recv()
    nxt = masked_panel(gn, None, lambda k: mn[k : k + 1, :])
    put_right(right_lt.at[3], nxt.T)
    for s in range(3, -1, -1):
        if s == 3:
            xe = -dot(left_dt[3], right_lt[3])
        else:
            xe = dot(left_bt[s], right_x[3 * W * (s + 2) : 3 * W * (s + 3), W:])
        put_right(right_x, xe, W, 3 * W * (s + 1))
        put_left(left_x.at[s], xe, 3 * W)
        if s == 0:
            x0[...] = xe

    @pl.when(odd)
    def _():
        hand[3].start()

    @pl.when(even)
    def _():
        hand[3].wait_recv()
        put_left(left_n, xb[...])
        put_right(right_b, xb[...])
        both = dot(left_x[0, :, 3 * W :], right_b[:, :W])
        put_right(right_u, both.T)

    pl.when(odd & (chip > 1))(relay_down)

    @pl.when(odd)
    def _():
        ct[...] = ga[...] + dot(left_m[...], right_g[...])

    @pl.when(even & (chip > 0))
    def _():
        for k in range(CHUNKS):
            share_down(k).wait_recv()

    @pl.when(even)
    def _():
        ct[...] = c_in[...].reshape(W, W)

    cn[...] = ct[...].T
    put_right(right_c, cn[...])
    xl[0] = xl[0] + dot(left_x[0, :, : 3 * W], right_c[...])

    @pl.when(odd)
    def _():
        w0[...] = xl[0]
        hand[2].start()

    border[2].start()

    @pl.when(even)
    def _():
        hand[2].wait_recv()
        put_right(right_b, wb[...])
        both = dot(left_x[0, :, 3 * W :], right_b[:, :W])
        ht[...] = (xl[0] + both).T

    def forward_later():
        for q in (0, 1):
            for g in later:
                g.second.forward(q)

    def prepare():
        for s in range(4):
            if s > 0:
                xl[s] = xl[s] + dot(left_x[s, :, : 3 * W], right_c[...])
            put_right(right_x, xl[s], 0, 3 * W * (s + 1))
        diagonal = lax.broadcasted_iota(jnp.int32, (W, W), 0) == lax.broadcasted_iota(jnp.int32, (W, W), 1)
        put_right(right_x, jnp.zeros((W, W), jnp.float32), 0, 15 * W)
        put_right(right_x, diagonal.astype(jnp.float32), W, 15 * W)
        border[2].wait_recv()
        prev = jnp.concatenate(panel(gp, None), axis=0)
        put_left(left_e.at[1], prev.T)
        both = dot(left_e[0], right_x[3 * W : 6 * W, :])
        put_right(right_b, both[:, :W] + cn[...])
        put_right(right_b, both[:, W:], W)
        both = dot(left_e[1], right_b[...])
        put_right(right_x, jnp.where(first, 0.0, both))
        for q in (0, 1):
            for g in later:
                g.second.finish(q)
        for s in range(4):
            gj = (gj0, gj1)[s // 2]
            for c in range(3):
                block = masked_panel(gj, 3 * (s % 2) + c, lambda k: mj[s, k : k + 1, W * c : W * (c + 1)])
                put_left(left_j, block, 3 * W * c)
            both = dot(left_j[...], right_x[3 * W * s : 3 * W * (s + 3), :])
            rs[W * s : W * (s + 1), :] = rv[W * s : W * (s + 1), :] - both[:, :W]
            put_left(left_r.at[s], -both[:, W:])

    pl.when(chip < 3)(forward_later)
    pl.when(chip < 2)(prepare)

    @pl.when(even)
    def _():
        for k, rows in enumerate(chunks):

            @pl.when(chip < 3)
            def _():
                send_up(k).wait_recv()

            @pl.when(chip > 0)
            def _():
                put_left(left_m.at[rows], e_in[k])
                e_out[k] = ht[rows, :] + dot(left_m[rows, :], right_u[...])
                send_up(k).start()

            @pl.when(chip < 3)
            def _():
                share_up(k).start()

    pl.when(chip == 3)(forward_later)
    pl.when(chip > 1)(prepare)

    @pl.when(odd & (chip < 3))
    def _():
        for k in range(CHUNKS):
            share_up(k).wait_recv()

    en[...] = e_in[...].reshape(W, W).T

    @pl.when(even)
    def _():
        put_right(right_b, en[...])
        en[...] = wb[...] + dot(left_n[...], right_b[:, :W])

    put_right(right_e, en[...])
    for s in range(4):
        rows = slice(W * s, W * (s + 1))
        xs[rows, :] = xl[s] + dot(left_x[s, :, 3 * W :], right_e[...])
        rs[rows, :] = rs[rows, :] + dot(left_r[s], right_e[...])

    for g in gathers + later:
        g.sent()
    for copy in border:
        copy.wait_send()

    def sent(cond, *copies):
        @pl.when(cond)
        def _():
            for copy in copies:
                for k in range(CHUNKS):
                    copy(k).wait_send()

    sent(odd & (chip < 3), send_down)
    sent(odd & (chip > 0), share_down)
    sent(even & (chip > 0), send_up)
    sent(even & (chip < 3), share_up)

    @pl.when(even)
    def _():
        hand[0].wait_send()
        hand[1].wait_send()

    @pl.when(odd)
    def _():
        hand[2].wait_send()
        hand[3].wait_send()


def on_device(*args):
    f32, bf16 = jnp.float32, jnp.bfloat16
    out = jax.ShapeDtypeStruct(args[0].shape, f32)
    hbm = pl.BlockSpec(memory_space=pltpu.HBM)
    vmem = pltpu.VMEM
    return pl.pallas_call(
        kernel,
        out_shape=(out, out),
        in_specs=[hbm] * 6,
        out_specs=(pl.BlockSpec(memory_space=vmem),) * 2,
        scratch_shapes=[
            vmem((4, 2, 4, 4, 8, W), f32),
            vmem((4, 2, 4, 4, 8, W), f32),
            vmem((4, 2, 4, 6, 8, W), f32),
            vmem((4, 2, 4, 6, 8, W), f32),
            vmem((4, 2, 4, 8, W), f32),
            vmem((4, 2, 4, 8, W), f32),
            vmem((4 * W, W), f32),
            vmem((4, 4, 4), jnp.int32),
            vmem((4, 4, 12), jnp.int32),
            vmem((4, 4, W), f32),
            vmem((4, 4, 3 * W), f32),
            vmem((4, W), f32),
            vmem((4, W, 3 * W), bf16),
            vmem((4, W, 3 * W), bf16),
            vmem((4, W, 3 * W), bf16),
            vmem((3, W, 3 * W), bf16),
            vmem((4, W, 6 * W), bf16),
            vmem((W, 9 * W), bf16),
            vmem((2, W, 3 * W), bf16),
            vmem((4, W, 3 * W), bf16),
            vmem((W, 3 * W), bf16),
            vmem((W, 3 * W), bf16),
            vmem((W, 3 * W), bf16),
            vmem((4, 3 * W, 2 * W), bf16),
            vmem((4, 3 * W, W), bf16),
            vmem((4, 3 * W, 2 * W), bf16),
            vmem((3 * W, 2 * W), bf16),
            vmem((18 * W, 2 * W), bf16),
            vmem((3 * W, W), bf16),
            vmem((3 * W, W), bf16),
            vmem((3 * W, W), bf16),
            vmem((3 * W, W), bf16),
            vmem((3 * W, W), bf16),
            vmem((3 * W, W), bf16),
            vmem((4, W, W), f32),
            vmem((4, W, W), f32),
            vmem((W, W), f32),
            vmem((W, W), f32),
            vmem((W, W), f32),
            vmem((W, W), f32),
            vmem((W, W), f32),
            vmem((W, W), f32),
            vmem((W, W), f32),
            vmem((W, W), f32),
            vmem((W, W), f32),
            vmem((W, W), f32),
            vmem((W, W), f32),
            vmem((W, W), f32),
            vmem((W, W), f32),
            vmem((CHUNKS, PART, W), f32),
            vmem((CHUNKS, PART, W), f32),
            vmem((CHUNKS, PART, W), f32),
            vmem((CHUNKS, PART, W), f32),
            pltpu.SemaphoreType.DMA((76,)),
            pltpu.SemaphoreType.DMA((76,)),
            pltpu.SemaphoreType.DMA((24,)),
        ],
        compiler_params=pltpu.CompilerParams(
            collective_id=0, has_side_effects=True, vmem_limit_bytes=48 * 1024 * 1024
        ),
    )(*[pltpu.with_memory_space_constraint(a, pltpu.HBM) for a in args])


def solution(mesh):
    in_specs = (
        P("node", "rhs"),
        P("node", "rhs", None),
        P("node", "rhs", None),
        P("node", None, None),
        P("node", "rhs", None),
        P("node", None, None),
    )
    out_specs = (P("node", "rhs"), P("node", "rhs"))
    return jax.shard_map(on_device, mesh=mesh, in_specs=in_specs, out_specs=out_specs, check_vma=False)
```

```python
import jax
import jax.numpy as jnp
from jax import lax
from jax.experimental import pallas as pl
from jax.experimental.pallas import tpu as pltpu
from jax.sharding import PartitionSpec as P

MESH_ID = pl.DeviceIdType.MESH
B = 64
W = 256
NODES = 8
CHUNKS = 4
PART = W // CHUNKS


class Sems:
    def __init__(self, send, recv, local):
        self.send, self.recv, self.local = send, recv, local
        self.pairs = self.locals = 0

    def pair(self):
        k = self.pairs
        self.pairs += 1
        return self.send.at[k], self.recv.at[k]

    def one(self):
        k = self.locals
        self.locals += 1
        return self.local.at[k]


class Ring:
    def __init__(self, sems, where, pos, device_at):
        self.where, self.pos = where, pos
        self.up, self.down = device_at(lax.rem(pos + 1, 4)), device_at(lax.rem(pos + 3, 4))
        self.sems = {key: sems.pair() for key in ("u0", "d0", "u1", "d1", "fu", "fd")}
        self.started = {}

    def at(self, q, step):
        return self.where(q, lax.rem(self.pos + step, 4))

    def copy(self, key, q, step, device, source=None):
        part = self.at(q, step)
        send, recv = self.sems[key]
        return pltpu.make_async_remote_copy(
            src_ref=part if source is None else source,
            dst_ref=part,
            send_sem=send,
            recv_sem=recv,
            device_id=device,
            device_id_type=MESH_ID,
        )

    def go(self, key, *args):
        self.started[key] = args
        self.copy(key, *args).start()

    def direct(self, q, source=None):
        first, second = ("u", "d") if q == 0 else ("d", "u")
        for way in (first, second):
            self.go(f"{way}{q}", q, 0, self.up if way == "u" else self.down, source)

    def forward(self, q):
        if q == 0:
            self.copy("u0", 0, 3, self.up).wait_recv()
            self.go("fu", 0, 3, self.up)
        else:
            self.copy("d1", 1, 1, self.down).wait_recv()
            self.go("fd", 1, 1, self.down)

    def finish(self, q):
        if q == 0:
            self.copy("d0", 0, 1, self.down).wait_recv()
            self.copy("fu", 0, 2, self.up).wait_recv()
        else:
            self.copy("u1", 1, 3, self.up).wait_recv()
            self.copy("fd", 1, 2, self.down).wait_recv()

    def sent(self):
        for key, args in self.started.items():
            self.copy(key, *args).wait_send()


class Gather:
    def __init__(self, sems, buf, x, zl, y, device, y_first):
        self.own = buf.at[x, zl, y]

        def layer(q):
            return zl if q == 0 else 1 - zl

        if y_first:
            self.first = Ring(sems, lambda q, p: buf.at[x, layer(q), p], y, lambda p: device(x, zl, p))
            self.second = Ring(sems, lambda q, p: buf.at[p, layer(q)], x, lambda p: device(p, zl, y))
        else:
            self.first = Ring(sems, lambda q, p: buf.at[p, layer(q), y], x, lambda p: device(p, zl, y))
            self.second = Ring(sems, lambda q, p: buf.at[:, layer(q), p], y, lambda p: device(x, zl, p))
        send, recv = sems.pair()
        self.cross_sems = send, recv
        self.partner = device(x, 1 - zl, y)
        self.other = buf.at[x, 1 - zl, y]

    def cross(self, part, source):
        send, recv = self.cross_sems
        return pltpu.make_async_remote_copy(
            src_ref=source, dst_ref=part, send_sem=send, recv_sem=recv, device_id=self.partner, device_id_type=MESH_ID
        )

    def start(self, source=None):
        source = self.own if source is None else source
        self.sent_cross = self.cross(self.own, source)
        self.sent_cross.start()
        self.first.direct(0, source)

    def crossed(self):
        self.cross(self.other, self.other).wait_recv()
        self.first.direct(1)

    def sent(self):
        self.sent_cross.wait_send()
        self.first.sent()
        self.second.sent()


def split(value):
    high = value.astype(jnp.bfloat16)
    return high, (value - high.astype(jnp.float32)).astype(jnp.bfloat16)


def put_left(ref, value, at=0):
    high, low = split(value)
    for k, part in enumerate((high, low, high)):
        ref[:, at + k * W : at + (k + 1) * W] = part


def put_right(ref, value, col=0, row=0):
    high, low = split(value)
    cols = slice(col, col + value.shape[1])
    for k, part in enumerate((high, high, low)):
        ref[row + k * W : row + (k + 1) * W, cols] = part


def dot(left, right):
    return jnp.dot(left, right, preferred_element_type=jnp.float32)


def panel(buf, s):
    return [(buf[x] if s is None else buf[x, :, :, s]).reshape(B, W) for x in range(4)]


def masked_panel(buf, s, weights):
    return jnp.concatenate([part * weights(x) for x, part in enumerate(panel(buf, s))], axis=0)


def rows_of(pattern):
    block = lax.broadcasted_iota(jnp.int32, (4, W), 1) // B
    values = pattern.astype(jnp.float32)
    out = jnp.zeros((4, W), jnp.float32)
    for k in range(4):
        out = jnp.where(block == k, values[:, k : k + 1], out)
    return out


def kernel(
    r_in, d_in, l_in, pl_in, j_in, pj_in,
    xs, rs,
    gd, gl, gj0, gj1, gn, gp, rv, pat_l, pat_j, ml, mj, mn,
    left_d, left_dt, left_a, left_bt, left_x, left_j, left_e, left_r, left_m, left_g, left_w,
    right_rl, right_lt, right_f, right_b, right_x, right_p, right_q, right_g, right_u, right_c, right_e, right_n, right_xc, right_xe,
    u, xl, pt, pa, ct, cn, x0, xb, et, xlt, gt, ga, w0, wb, ht, c_in, e_in, c_out, e_out,
    send_sem, recv_sem, local_sem, ready_sem,
):
    rhs, node = lax.axis_index("rhs"), lax.axis_index("node")
    x, zl, y = rhs // 8, (rhs // 4) % 2, rhs % 4
    after, before = node + 1, node - 1
    first, last = node == 0, node == NODES - 1
    chip, odd = node // 2, node % 2 == 1
    even = jnp.logical_not(odd)
    partner = node + 1 - 2 * (node % 2)
    two_after, two_before = node + 2, node - 2

    def device(px, pz, py):
        return (px * 8 + pz * 4 + py, node)

    sems = Sems(send_sem, recv_sem, local_sem)

    def load(source, target):
        copy = pltpu.make_async_copy(source, target, sems.one())
        copy.start()
        return copy

    barrier = pltpu.get_barrier_semaphore()
    peers = [device(x, 1 - zl, y)]
    peers += [device(x, zl, lax.rem(y + k, 4)) for k in (1, 3)]
    peers += [device(lax.rem(x + k, 4), zl, y) for k in (1, 3)]
    for peer in peers:
        pl.semaphore_signal(barrier, inc=1, device_id=peer, device_id_type=MESH_ID)
    for step in (1, 2):

        @pl.when(node + step < NODES)
        def _():
            pl.semaphore_signal(barrier, inc=1, device_id=(rhs, node + step), device_id_type=MESH_ID)

    for least in (0, 1, 2):

        @pl.when(node == least if least < 2 else node >= 2)
        def _():
            pl.semaphore_wait(barrier, len(peers) + least)

    for step in (1, 2):

        @pl.when(node >= step)
        def _():
            pl.semaphore_signal(ready_sem.at[step - 1], inc=1, device_id=(rhs, node - step), device_id_type=MESH_ID)

    gathers = [
        Gather(sems, gd, x, zl, y, device, True),
        Gather(sems, gl, x, zl, y, device, False),
    ]
    later = [
        Gather(sems, gj0, x, zl, y, device, True),
        Gather(sems, gj1, x, zl, y, device, False),
    ]

    def remote(source, target, pair, to):
        return pltpu.make_async_remote_copy(
            src_ref=source,
            dst_ref=target,
            send_sem=pair[0],
            recv_sem=pair[1],
            device_id=(rhs, to),
            device_id_type=MESH_ID,
        )

    for g, source in zip(gathers, (d_in, l_in)):
        g.start(source)
    border = [
        remote(ml.at[0], mn, sems.pair(), before),
        remote(gl.at[:, :, :, 0], gn, sems.pair(), before),
        remote(gd.at[:, :, :, 3], gp, sems.pair(), after),
    ]
    own_d = load(d_in, gd.at[x, zl, y])
    own_l = load(l_in, gl.at[x, zl, y])
    pat_loads = [load(pl_in, pat_l), load(pj_in, pat_j)]
    j_loads = []
    for h, gj in enumerate((gj0, gj1)):
        for s in range(2):
            for c in range(3):
                j_loads.append(load(j_in.at[2 * h + s, :, W * c : W * (c + 1)], gj.at[x, zl, y, 3 * s + c]))
    r_load = load(r_in, rv)
    own_d.wait()
    own_l.wait()
    for g in gathers:
        g.crossed()
    for q in (0, 1):
        for g in gathers:
            g.first.forward(q)
    for q in (0, 1):
        for g in gathers:
            g.first.finish(q)
            g.second.direct(q)
    r_load.wait()
    for copy in pat_loads + j_loads:
        copy.wait()
    for s in range(4):
        ml[s] = rows_of(pat_l[s])
        for c in range(3):
            mj[s, :, W * c : W * (c + 1)] = rows_of(pat_j[s, :, 4 * c : 4 * (c + 1)])
    for q in (0, 1):
        for g in gathers:
            g.second.forward(q)
    for q in (0, 1):
        for g in gathers:
            g.second.finish(q)

    @pl.when(node > 0)
    def _():
        border[0].start()
        border[1].start()

    @pl.when(last)
    def _():
        mn[...] = jnp.zeros_like(mn)
        gn[...] = jnp.zeros_like(gn)

    @pl.when(first)
    def _():
        gp[...] = jnp.zeros_like(gp)


    for g in later:
        g.start()

    for s in range(4):
        d = jnp.concatenate(panel(gd, s), axis=0)
        put_left(left_d.at[s], d)
        put_left(left_dt.at[s], d.T)
        low = masked_panel(gl, s, lambda k: ml[s, k : k + 1, :])
        right = right_rl.at[s]
        put_right(right, rv[W * s : W * (s + 1), :])
        put_right(right, low, W)
        if s == 0:
            put_left(left_e.at[0], -low.T)
        else:
            put_right(right_lt.at[s - 1], low.T)
        both = dot(left_d[s], right[...])
        if s == 0:
            put_right(right_f.at[0], both[:, :W])
            put_right(right_f.at[0], -both[:, W:], W)
        else:
            u[s] = both[:, :W]
            put_left(left_a.at[s], -both[:, W:])
    for s in range(1, 4):
        both = dot(left_a[s], right_f[s - 1])
        fs = u[s] + both[:, :W]
        put_right(right_f.at[s], fs)
        put_right(right_f.at[s], both[:, W:], W)
        if s == 3:
            gt[...] = fs.T.reshape(CHUNKS, PART, W)
            pt[...] = both[:, W:].T

    chunks = [slice(PART * k, PART * (k + 1)) for k in range(CHUNKS)]
    down, fan_down, up, fan_up, join, turn = [[sems.pair() for k in range(CHUNKS)] for _ in range(6)]
    hand = [
        remote(pt, pa, sems.pair(), partner),
        remote(x0, xb, sems.pair(), partner),
    ]

    def send_g(k):
        return remote(gt.at[k], ga.at[k], join[k], partner)

    def send_w(k):
        return remote(w0.at[k], wb.at[k], turn[k], partner)

    def send_down(k):
        return remote(c_out.at[k], c_in.at[k], down[k], two_after)

    def share_down(k):
        return remote(c_in.at[k], c_in.at[k], fan_down[k], partner)

    def send_up(k):
        return remote(e_out.at[k], e_in.at[k], up[k], two_before)

    def share_up(k):
        return remote(e_in.at[k], e_in.at[k], fan_up[k], partner)

    for step in (1, 2):

        @pl.when(node + step < NODES)
        def _():
            pl.semaphore_wait(ready_sem.at[step - 1], 1)

    @pl.when(even)
    def _():
        for k in range(CHUNKS):
            send_g(k).start()
        hand[0].start()

    @pl.when(chip == 0)
    def _():
        c_in[...] = jnp.zeros_like(c_in)
        left_m[...] = jnp.zeros_like(left_m)

    @pl.when(odd)
    def _():
        put_right(right_p, pt[...])
        for k, rows in enumerate(chunks):
            send_g(k).wait_recv()
            put_left(left_w.at[rows], ga[k])
            c_out[k] = gt[k] + dot(left_w[rows, :], right_p[...])

            @pl.when(chip == 0)
            def _():
                send_down(k).start()

        hand[0].wait_recv()
        put_left(left_g, pa[...])
        put_right(right_g, pa[...])
        put_right(right_q, dot(left_g[...], right_p[...]))

    def turn_odd(k):
        rows = chunks[k]
        mine = ga[k] + dot(left_m[rows, :], right_g[...])
        ct[rows, :] = mine
        put_left(left_w.at[rows], mine)
        w0[k] = xlt[rows, :] + dot(left_w[rows, :], right_xc[...])
        send_w(k).start()

    def turn_even(k):
        rows = chunks[k]

        @pl.when(chip > 0)
        def _():
            share_down(k).wait_recv()

        ct[rows, :] = c_in[k]
        put_left(left_m.at[rows], c_in[k])
        mine = xlt[rows, :] + dot(left_m[rows, :], right_xc[...])
        send_w(k).wait_recv()
        put_left(left_w.at[rows], wb[k])
        ht[k] = mine + dot(left_w[rows, :], right_xe[...])

        @pl.when(chip == 3)
        def _():
            e_out[k] = ht[k]
            send_up(k).start()

    def relay_down():
        for k, rows in enumerate(chunks):
            send_down(k).wait_recv()
            put_left(left_m.at[rows], c_in[k])

            @pl.when(chip < 3)
            def _():
                c_out[k] = c_out[k] + dot(left_m[rows, :], right_q[...])
                send_down(k).start()

            share_down(k).start()
            pl.when(chip == 3)(lambda: turn_odd(k))

    for s in range(3):
        put_left(left_bt.at[s], -dot(left_dt[s], right_lt[s]))
    for s in range(3, -1, -1):
        both = dot(left_dt[s], right_f[s])
        if s < 3:
            both = both + dot(left_bt[s], right_b[...])
        if s > 0:
            put_right(right_b, both)
        xl[s] = both[:, :W]
        put_left(left_x.at[s], both[:, W:])
        if s == 0:
            xlt[...] = both[:, :W].T
            put_right(right_xc, both[:, W:].T)

    for g in later:
        g.crossed()
    pl.when(odd & (chip == 1))(relay_down)

    for q in (0, 1):
        for g in later:
            g.first.forward(q)
    for q in (0, 1):
        for g in later:
            g.first.finish(q)
            g.second.direct(q)

    @pl.when(jnp.logical_not(last))
    def _():
        border[0].wait_recv()
        border[1].wait_recv()

    nxt = masked_panel(gn, None, lambda k: mn[k : k + 1, :])
    put_right(right_lt.at[3], nxt.T)
    for s in range(3, -1, -1):
        if s == 3:
            xe = -dot(left_dt[3], right_lt[3])
        else:
            xe = dot(left_bt[s], right_x[3 * W * (s + 2) : 3 * W * (s + 3), W:])
        put_right(right_x, xe, W, 3 * W * (s + 1))
        put_left(left_x.at[s], xe, 3 * W)
        if s == 0:
            x0[...] = xe.T

    @pl.when(odd)
    def _():
        hand[1].start()

    @pl.when(even)
    def _():
        put_right(right_xe, x0[...])
        hand[1].wait_recv()
        put_left(left_g, xb[...])
        put_right(right_n, xb[...])
        put_right(right_u, dot(left_g[...], right_xe[...]))

    pl.when(odd & (chip > 1))(relay_down)

    @pl.when(odd & (chip < 3))
    def _():
        for k in range(CHUNKS):
            turn_odd(k)

    @pl.when(even)
    def _():
        for k in range(CHUNKS):
            turn_even(k)

    @pl.when(jnp.logical_not(last))
    def _():
        border[2].start()

    def forward_later():
        for q in (0, 1):
            for g in later:
                g.second.forward(q)

    def prepare():
        cn[...] = ct[...].T
        put_right(right_c, cn[...])
        for s in range(4):
            xl[s] = xl[s] + dot(left_x[s, :, : 3 * W], right_c[...])
            put_right(right_x, xl[s], 0, 3 * W * (s + 1))
        diagonal = lax.broadcasted_iota(jnp.int32, (W, W), 0) == lax.broadcasted_iota(jnp.int32, (W, W), 1)
        put_right(right_x, jnp.zeros((W, W), jnp.float32), 0, 15 * W)
        put_right(right_x, diagonal.astype(jnp.float32), W, 15 * W)
        pl.when(node > 0)(lambda: border[2].wait_recv())
        prev = jnp.concatenate(panel(gp, None), axis=0)
        put_left(left_e.at[1], prev.T)
        both = dot(left_e[0], right_x[3 * W : 6 * W, :])
        put_right(right_b, both[:, :W] + cn[...])
        put_right(right_b, both[:, W:], W)
        both = dot(left_e[1], right_b[...])
        put_right(right_x, jnp.where(first, 0.0, both))
        for q in (0, 1):
            for g in later:
                g.second.finish(q)
        for s in range(4):
            gj = (gj0, gj1)[s // 2]
            for c in range(3):
                block = masked_panel(gj, 3 * (s % 2) + c, lambda k: mj[s, k : k + 1, W * c : W * (c + 1)])
                put_left(left_j, block, 3 * W * c)
            both = dot(left_j[...], right_x[3 * W * s : 3 * W * (s + 3), :])
            rs[W * s : W * (s + 1), :] = rv[W * s : W * (s + 1), :] - both[:, :W]
            put_left(left_r.at[s], -both[:, W:])

    pl.when(chip < 3)(forward_later)
    pl.when(chip < 2)(prepare)

    @pl.when(even & (chip < 3))
    def _():
        for k, rows in enumerate(chunks):
            send_up(k).wait_recv()
            put_left(left_m.at[rows], e_in[k])

            @pl.when(chip > 0)
            def _():
                e_out[k] = ht[k] + dot(left_m[rows, :], right_u[...])
                send_up(k).start()

            share_up(k).start()
            et[rows, :] = wb[k] + dot(left_m[rows, :], right_n[...])

    @pl.when(even & (chip == 3))
    def _():
        et[...] = wb[...].reshape(W, W)

    pl.when(chip == 3)(forward_later)
    pl.when(chip > 1)(prepare)

    @pl.when(odd & (chip < 3))
    def _():
        for k, rows in enumerate(chunks):
            share_up(k).wait_recv()
            et[rows, :] = e_in[k]

    @pl.when(last)
    def _():
        et[...] = jnp.zeros_like(et)

    put_right(right_e, et[...].T)
    for s in range(4):
        rows = slice(W * s, W * (s + 1))
        xs[rows, :] = xl[s] + dot(left_x[s, :, 3 * W :], right_e[...])
        rs[rows, :] = rs[rows, :] + dot(left_r[s], right_e[...])

    for g in gathers + later:
        g.sent()

    @pl.when(node > 0)
    def _():
        border[0].wait_send()
        border[1].wait_send()

    @pl.when(jnp.logical_not(last))
    def _():
        border[2].wait_send()

    def sent(cond, *copies):
        @pl.when(cond)
        def _():
            for copy in copies:
                for k in range(CHUNKS):
                    copy(k).wait_send()

    sent(odd & (chip < 3), send_down)
    sent(odd & (chip > 0), share_down)
    sent(even & (chip > 0), send_up)
    sent(even & (chip < 3), share_up)
    sent(even, send_g)
    sent(odd, send_w)

    @pl.when(even)
    def _():
        hand[0].wait_send()

    @pl.when(odd)
    def _():
        hand[1].wait_send()


def on_device(*args):
    f32, bf16 = jnp.float32, jnp.bfloat16
    out = jax.ShapeDtypeStruct(args[0].shape, f32)
    hbm = pl.BlockSpec(memory_space=pltpu.HBM)
    vmem = pltpu.VMEM
    return pl.pallas_call(
        kernel,
        out_shape=(out, out),
        in_specs=[hbm] * 6,
        out_specs=(pl.BlockSpec(memory_space=vmem),) * 2,
        scratch_shapes=[
            vmem((4, 2, 4, 4, 8, W), f32),
            vmem((4, 2, 4, 4, 8, W), f32),
            vmem((4, 2, 4, 6, 8, W), f32),
            vmem((4, 2, 4, 6, 8, W), f32),
            vmem((4, 2, 4, 8, W), f32),
            vmem((4, 2, 4, 8, W), f32),
            vmem((4 * W, W), f32),
            vmem((4, 4, 4), jnp.int32),
            vmem((4, 4, 12), jnp.int32),
            vmem((4, 4, W), f32),
            vmem((4, 4, 3 * W), f32),
            vmem((4, W), f32),
            vmem((4, W, 3 * W), bf16),
            vmem((4, W, 3 * W), bf16),
            vmem((4, W, 3 * W), bf16),
            vmem((3, W, 3 * W), bf16),
            vmem((4, W, 6 * W), bf16),
            vmem((W, 9 * W), bf16),
            vmem((2, W, 3 * W), bf16),
            vmem((4, W, 3 * W), bf16),
            vmem((W, 3 * W), bf16),
            vmem((W, 3 * W), bf16),
            vmem((W, 3 * W), bf16),
            vmem((4, 3 * W, 2 * W), bf16),
            vmem((4, 3 * W, W), bf16),
            vmem((4, 3 * W, 2 * W), bf16),
            vmem((3 * W, 2 * W), bf16),
            vmem((18 * W, 2 * W), bf16),
            vmem((3 * W, W), bf16),
            vmem((3 * W, W), bf16),
            vmem((3 * W, W), bf16),
            vmem((3 * W, W), bf16),
            vmem((3 * W, W), bf16),
            vmem((3 * W, W), bf16),
            vmem((3 * W, W), bf16),
            vmem((3 * W, W), bf16),
            vmem((3 * W, W), bf16),
            vmem((4, W, W), f32),
            vmem((4, W, W), f32),
            vmem((W, W), f32),
            vmem((W, W), f32),
            vmem((W, W), f32),
            vmem((W, W), f32),
            vmem((W, W), f32),
            vmem((W, W), f32),
            vmem((W, W), f32),
            vmem((W, W), f32),
            vmem((CHUNKS, PART, W), f32),
            vmem((CHUNKS, PART, W), f32),
            vmem((CHUNKS, PART, W), f32),
            vmem((CHUNKS, PART, W), f32),
            vmem((CHUNKS, PART, W), f32),
            vmem((CHUNKS, PART, W), f32),
            vmem((CHUNKS, PART, W), f32),
            vmem((CHUNKS, PART, W), f32),
            vmem((CHUNKS, PART, W), f32),
            pltpu.SemaphoreType.DMA((84,)),
            pltpu.SemaphoreType.DMA((84,)),
            pltpu.SemaphoreType.DMA((24,)),
            pltpu.SemaphoreType.REGULAR((2,)),
        ],
        compiler_params=pltpu.CompilerParams(
            collective_id=0, has_side_effects=True, vmem_limit_bytes=48 * 1024 * 1024
        ),
    )(*[pltpu.with_memory_space_constraint(a, pltpu.HBM) for a in args])


def solution(mesh):
    in_specs = (
        P("node", "rhs"),
        P("node", "rhs", None),
        P("node", "rhs", None),
        P("node", None, None),
        P("node", "rhs", None),
        P("node", None, None),
    )
    out_specs = (P("node", "rhs"), P("node", "rhs"))
    return jax.shard_map(on_device, mesh=mesh, in_specs=in_specs, out_specs=out_specs, check_vma=False)
```

```python
import jax
import jax.numpy as jnp
from jax import lax
from jax.experimental import pallas as pl
from jax.experimental.pallas import tpu as pltpu
from jax.sharding import PartitionSpec as P

MESH_ID = pl.DeviceIdType.MESH
B = 64
W = 256
NODES = 8
CHUNKS = 4
PART = W // CHUNKS


class Sems:
    def __init__(self, send, recv, local):
        self.send, self.recv, self.local = send, recv, local
        self.pairs = self.locals = 0

    def pair(self):
        k = self.pairs
        self.pairs += 1
        return self.send.at[k], self.recv.at[k]

    def one(self):
        k = self.locals
        self.locals += 1
        return self.local.at[k]


class Ring:
    def __init__(self, sems, where, pos, device_at, near=False):
        self.where, self.pos, self.near = where, pos, near
        self.opposite = device_at(lax.rem(pos + 2, 4))
        self.up, self.down = device_at(lax.rem(pos + 1, 4)), device_at(lax.rem(pos + 3, 4))
        self.sems = {key: sems.pair() for key in ("u0", "d0", "u1", "d1", "f0", "f1")}
        self.started = {}

    def at(self, q, step):
        return self.where(q, lax.rem(self.pos + step, 4))

    def copy(self, key, q, step, device, source=None):
        part = self.at(q, step)
        send, recv = self.sems[key]
        return pltpu.make_async_remote_copy(
            src_ref=part if source is None else source,
            dst_ref=part,
            send_sem=send,
            recv_sem=recv,
            device_id=device,
            device_id_type=MESH_ID,
        )

    def go(self, key, *args):
        self.started[key] = args
        self.copy(key, *args).start()

    def direct(self, q, source=None):
        if self.near and q == 1:
            self.go("f1", 1, 0, self.opposite, source)
        first, second = ("d", "u") if (q == 0) == self.near else ("u", "d")
        for way in (first, second):
            self.go(f"{way}{q}", q, 0, self.up if way == "u" else self.down, source)

    def arrived(self, key, q, step):
        self.copy(key, q, step, self.up).wait_recv()

    def forward(self, q):
        if self.near:
            if q == 0:
                self.arrived("d0", 0, 1)
                self.go("f0", 0, 1, self.down)
        elif q == 0:
            self.arrived("u0", 0, 3)
            self.go("f0", 0, 3, self.up)
        else:
            self.arrived("d1", 1, 1)
            self.go("f1", 1, 1, self.down)

    def finish(self, q):
        if self.near or q == 1:
            self.arrived(f"u{q}", q, 3)
        if (self.near and q == 1) or (not self.near and q == 0):
            self.arrived(f"d{q}", q, 1)
        self.arrived(f"f{q}", q, 2)

    def sent(self):
        for key, args in self.started.items():
            self.copy(key, *args).wait_send()


class Gather:
    def __init__(self, sems, buf, x, zl, y, device, y_first):
        self.own = buf.at[x, zl, y]

        def layer(q):
            return zl if q == 0 else 1 - zl

        if y_first:
            self.first = Ring(sems, lambda q, p: buf.at[x, layer(q), p], y, lambda p: device(x, zl, p), True)
            self.second = Ring(sems, lambda q, p: buf.at[p, layer(q)], x, lambda p: device(p, zl, y))
        else:
            self.first = Ring(sems, lambda q, p: buf.at[p, layer(q), y], x, lambda p: device(p, zl, y), True)
            self.second = Ring(sems, lambda q, p: buf.at[:, layer(q), p], y, lambda p: device(x, zl, p))
        send, recv = sems.pair()
        self.cross_sems = send, recv
        self.partner = device(x, 1 - zl, y)
        self.other = buf.at[x, 1 - zl, y]

    def cross(self, part, source):
        send, recv = self.cross_sems
        return pltpu.make_async_remote_copy(
            src_ref=source, dst_ref=part, send_sem=send, recv_sem=recv, device_id=self.partner, device_id_type=MESH_ID
        )

    def start(self, source=None):
        source = self.own if source is None else source
        self.sent_cross = self.cross(self.own, source)
        self.sent_cross.start()
        self.first.direct(0, source)

    def crossed(self):
        self.cross(self.other, self.other).wait_recv()
        self.first.direct(1)

    def sent(self):
        self.sent_cross.wait_send()
        self.first.sent()
        self.second.sent()


def split(value):
    high = value.astype(jnp.bfloat16)
    return high, (value - high.astype(jnp.float32)).astype(jnp.bfloat16)


def put_left(ref, value, at=0):
    high, low = split(value)
    for k, part in enumerate((high, low, high)):
        ref[:, at + k * W : at + (k + 1) * W] = part


def put_right(ref, value, col=0, row=0):
    high, low = split(value)
    cols = slice(col, col + value.shape[1])
    for k, part in enumerate((high, high, low)):
        ref[row + k * W : row + (k + 1) * W, cols] = part


def dot(left, right):
    return jnp.dot(left, right, preferred_element_type=jnp.float32)


def panel(buf, s):
    return [(buf[x] if s is None else buf[x, :, :, s]).reshape(B, W) for x in range(4)]


def masked_panel(buf, s, weights):
    return jnp.concatenate([part * weights(x) for x, part in enumerate(panel(buf, s))], axis=0)


def rows_of(pattern):
    block = lax.broadcasted_iota(jnp.int32, (4, W), 1) // B
    values = pattern.astype(jnp.float32)
    out = jnp.zeros((4, W), jnp.float32)
    for k in range(4):
        out = jnp.where(block == k, values[:, k : k + 1], out)
    return out


def kernel(
    r_in, d_in, l_in, pl_in, j_in, pj_in,
    xs, rs,
    gd, gl, gj0, gj1, gn, gp, rv, pat_l, pat_j, ml, mj, mn,
    left_d, left_dt, left_a, left_bt, left_x, left_j, left_e, left_r, left_m, left_g, left_w, left_v,
    right_rl, right_lt, right_f, right_b, right_x, right_p, right_q, right_g, right_u, right_c, right_e, right_n, right_xc, right_xe, right_xca,
    u, xl, pt, pa, ct, cn, x0, xea, et, xlt, xct, xla, xca, gt, ga, wb, ht, c_in, e_in, c_out, e_out, ea_out,
    send_sem, recv_sem, local_sem, ready_sem,
):
    rhs, node = lax.axis_index("rhs"), lax.axis_index("node")
    x, zl, y = rhs // 8, (rhs // 4) % 2, rhs % 4
    after, before = node + 1, node - 1
    first, last = node == 0, node == NODES - 1
    chip, odd = node // 2, node % 2 == 1
    even = jnp.logical_not(odd)
    partner = node + 1 - 2 * (node % 2)
    two_after, two_before = node + 2, node - 2

    def device(px, pz, py):
        return (px * 8 + pz * 4 + py, node)

    sems = Sems(send_sem, recv_sem, local_sem)

    def load(source, target):
        copy = pltpu.make_async_copy(source, target, sems.one())
        copy.start()
        return copy

    barrier = pltpu.get_barrier_semaphore()
    peers = [device(x, 1 - zl, y)]
    peers += [device(x, zl, lax.rem(y + k, 4)) for k in (1, 2, 3)]
    peers += [device(lax.rem(x + k, 4), zl, y) for k in (1, 2, 3)]
    for peer in peers:
        pl.semaphore_signal(barrier, inc=1, device_id=peer, device_id_type=MESH_ID)
    for step in (1, 2):

        @pl.when(node + step < NODES)
        def _():
            pl.semaphore_signal(barrier, inc=1, device_id=(rhs, node + step), device_id_type=MESH_ID)

    for least in (0, 1, 2):

        @pl.when(node == least if least < 2 else node >= 2)
        def _():
            pl.semaphore_wait(barrier, len(peers) + least)

    for step in (1, 2):

        @pl.when(node >= step)
        def _():
            pl.semaphore_signal(ready_sem.at[step - 1], inc=1, device_id=(rhs, node - step), device_id_type=MESH_ID)

    gathers = [
        Gather(sems, gd, x, zl, y, device, True),
        Gather(sems, gl, x, zl, y, device, False),
    ]
    later = [
        Gather(sems, gj0, x, zl, y, device, True),
        Gather(sems, gj1, x, zl, y, device, False),
    ]

    def remote(source, target, pair, to):
        return pltpu.make_async_remote_copy(
            src_ref=source,
            dst_ref=target,
            send_sem=pair[0],
            recv_sem=pair[1],
            device_id=(rhs, to),
            device_id_type=MESH_ID,
        )

    for g, source in zip(gathers, (d_in, l_in)):
        g.start(source)
    border = [
        remote(ml.at[0], mn, sems.pair(), before),
        remote(gl.at[:, :, :, 0], gn, sems.pair(), before),
        remote(gd.at[:, :, :, 3], gp, sems.pair(), after),
    ]
    own_d = load(d_in, gd.at[x, zl, y])
    own_l = load(l_in, gl.at[x, zl, y])
    pat_loads = [load(pl_in, pat_l), load(pj_in, pat_j)]
    j_loads = []
    for h, gj in enumerate((gj0, gj1)):
        for s in range(2):
            for c in range(3):
                j_loads.append(load(j_in.at[2 * h + s, :, W * c : W * (c + 1)], gj.at[x, zl, y, 3 * s + c]))
    r_load = load(r_in, rv)
    own_d.wait()
    own_l.wait()
    for g in gathers:
        g.crossed()
    for q in (0, 1):
        for g in gathers:
            g.first.forward(q)
    for q in (0, 1):
        for g in gathers:
            g.first.finish(q)
            g.second.direct(q)
    r_load.wait()
    for copy in pat_loads + j_loads:
        copy.wait()
    for s in range(4):
        ml[s] = rows_of(pat_l[s])
        for c in range(3):
            mj[s, :, W * c : W * (c + 1)] = rows_of(pat_j[s, :, 4 * c : 4 * (c + 1)])
    for q in (0, 1):
        for g in gathers:
            g.second.forward(q)
    for q in (0, 1):
        for g in gathers:
            g.second.finish(q)

    @pl.when(node > 0)
    def _():
        border[0].start()
        border[1].start()

    @pl.when(last)
    def _():
        mn[...] = jnp.zeros_like(mn)
        gn[...] = jnp.zeros_like(gn)

    @pl.when(first)
    def _():
        gp[...] = jnp.zeros_like(gp)


    for g in later:
        g.start()

    for s in range(4):
        d = jnp.concatenate(panel(gd, s), axis=0)
        put_left(left_d.at[s], d)
        put_left(left_dt.at[s], d.T)
        low = masked_panel(gl, s, lambda k: ml[s, k : k + 1, :])
        right = right_rl.at[s]
        put_right(right, rv[W * s : W * (s + 1), :])
        put_right(right, low, W)
        if s == 0:
            put_left(left_e.at[0], -low.T)
        else:
            put_right(right_lt.at[s - 1], low.T)
        both = dot(left_d[s], right[...])
        if s == 0:
            put_right(right_f.at[0], both[:, :W])
            put_right(right_f.at[0], -both[:, W:], W)
        else:
            u[s] = both[:, :W]
            put_left(left_a.at[s], -both[:, W:])
    for s in range(1, 4):
        both = dot(left_a[s], right_f[s - 1])
        fs = u[s] + both[:, :W]
        put_right(right_f.at[s], fs)
        put_right(right_f.at[s], both[:, W:], W)
        if s == 3:
            gt[...] = fs.T.reshape(CHUNKS, PART, W)
            pt[...] = both[:, W:].T

    chunks = [slice(PART * k, PART * (k + 1)) for k in range(CHUNKS)]
    down, fan_down, up, fan_up, join = [[sems.pair() for k in range(CHUNKS)] for _ in range(5)]
    hand = [
        remote(pt, pa, sems.pair(), partner),
        remote(xlt, xla, sems.pair(), partner),
        remote(xct, xca, sems.pair(), partner),
        remote(x0, xea, sems.pair(), partner),
    ]

    def send_g(k):
        return remote(gt.at[k], ga.at[k], join[k], partner)

    def send_down(k):
        return remote(c_out.at[k], c_in.at[k], down[k], two_after)

    def share_down(k):
        return remote(c_in.at[k], c_in.at[k], fan_down[k], partner)

    def send_up(k):
        return remote(e_out.at[k], e_in.at[k], up[k], two_before)

    def share_up(k):
        return remote(ea_out.at[k], e_in.at[k], fan_up[k], partner)

    for step in (1, 2):

        @pl.when(node + step < NODES)
        def _():
            pl.semaphore_wait(ready_sem.at[step - 1], 1)

    @pl.when(even)
    def _():
        for k in range(CHUNKS):
            send_g(k).start()
        hand[0].start()

    @pl.when(chip == 0)
    def _():
        c_in[...] = jnp.zeros_like(c_in)
        left_m[...] = jnp.zeros_like(left_m)

    @pl.when(odd)
    def _():
        put_right(right_p, pt[...])
        for k, rows in enumerate(chunks):
            send_g(k).wait_recv()
            put_left(left_w.at[rows], ga[k])
            c_out[k] = gt[k] + dot(left_w[rows, :], right_p[...])

            @pl.when(chip == 0)
            def _():
                send_down(k).start()

        hand[0].wait_recv()
        put_left(left_g, pa[...])
        put_right(right_g, pa[...])
        put_right(right_q, dot(left_g[...], right_p[...]))

    def turn(k):
        rows = chunks[k]
        mine = ga[k] + dot(left_m[rows, :], right_g[...])
        ct[rows, :] = mine
        put_left(left_w.at[rows], mine)
        wb[k] = xlt[rows, :] + dot(left_w[rows, :], right_xc[...])
        put_left(left_v.at[rows], wb[k])
        head = xla[rows, :] + dot(left_m[rows, :], right_xca[...]) + dot(left_v[rows, :], right_xe[...])

        @pl.when(chip < 3)
        def _():
            ht[k] = head

        @pl.when(chip == 3)
        def _():
            e_out[k] = head
            send_up(k).start()
            ea_out[k] = wb[k]
            share_up(k).start()

    def relay_down():
        for k, rows in enumerate(chunks):
            send_down(k).wait_recv()
            put_left(left_m.at[rows], c_in[k])

            @pl.when(chip < 3)
            def _():
                c_out[k] = c_out[k] + dot(left_m[rows, :], right_q[...])
                send_down(k).start()

            share_down(k).start()
            pl.when(chip == 3)(lambda: turn(k))

    for s in range(3):
        put_left(left_bt.at[s], -dot(left_dt[s], right_lt[s]))
    for s in range(3, -1, -1):
        both = dot(left_dt[s], right_f[s])
        if s < 3:
            both = both + dot(left_bt[s], right_b[...])
        if s > 0:
            put_right(right_b, both)
        xl[s] = both[:, :W]
        put_left(left_x.at[s], both[:, W:])
        if s == 0:
            xlt[...] = both[:, :W].T
            xct[...] = both[:, W:].T

    @pl.when(even)
    def _():
        hand[1].start()
        hand[2].start()

    @pl.when(odd)
    def _():
        put_right(right_xc, xct[...])

    for g in later:
        g.crossed()
    pl.when(odd & (chip > 0) & (chip < 3))(relay_down)

    for q in (0, 1):
        for g in later:
            g.first.forward(q)
    for q in (0, 1):
        for g in later:
            g.first.finish(q)
            g.second.direct(q)

    @pl.when(jnp.logical_not(last))
    def _():
        border[0].wait_recv()
        border[1].wait_recv()

    nxt = masked_panel(gn, None, lambda k: mn[k : k + 1, :])
    put_right(right_lt.at[3], nxt.T)
    for s in range(3, -1, -1):
        if s == 3:
            xe = -dot(left_dt[3], right_lt[3])
        else:
            xe = dot(left_bt[s], right_x[3 * W * (s + 2) : 3 * W * (s + 3), W:])
        put_right(right_x, xe, W, 3 * W * (s + 1))
        put_left(left_x.at[s], xe, 3 * W)
        if s == 0:
            x0[...] = xe.T

    @pl.when(even)
    def _():
        hand[3].start()

    @pl.when(odd)
    def _():
        put_right(right_n, x0[...])
        put_left(left_g, x0[...])
        hand[1].wait_recv()
        hand[2].wait_recv()
        put_right(right_xca, xca[...])
        hand[3].wait_recv()
        put_right(right_xe, xea[...])
        put_right(right_u, dot(left_g[...], right_xe[...]))

    pl.when(odd & (chip == 3))(relay_down)

    @pl.when(odd & (chip < 3))
    def _():
        for k in range(CHUNKS):
            turn(k)

    @pl.when(even)
    def _():
        @pl.when(chip > 0)
        def _():
            for k in range(CHUNKS):
                share_down(k).wait_recv()

        ct[...] = c_in[...].reshape(W, W)

    @pl.when(jnp.logical_not(last))
    def _():
        border[2].start()

    def forward_later():
        for q in (0, 1):
            for g in later:
                g.second.forward(q)

    def prepare():
        cn[...] = ct[...].T
        put_right(right_c, cn[...])
        for s in range(4):
            xl[s] = xl[s] + dot(left_x[s, :, : 3 * W], right_c[...])
            put_right(right_x, xl[s], 0, 3 * W * (s + 1))
        diagonal = lax.broadcasted_iota(jnp.int32, (W, W), 0) == lax.broadcasted_iota(jnp.int32, (W, W), 1)
        put_right(right_x, jnp.zeros((W, W), jnp.float32), 0, 15 * W)
        put_right(right_x, diagonal.astype(jnp.float32), W, 15 * W)
        pl.when(node > 0)(lambda: border[2].wait_recv())
        prev = jnp.concatenate(panel(gp, None), axis=0)
        put_left(left_e.at[1], prev.T)
        both = dot(left_e[0], right_x[3 * W : 6 * W, :])
        put_right(right_b, both[:, :W] + cn[...])
        put_right(right_b, both[:, W:], W)
        both = dot(left_e[1], right_b[...])
        put_right(right_x, jnp.where(first, 0.0, both))
        for q in (0, 1):
            for g in later:
                g.second.finish(q)
        for s in range(4):
            gj = (gj0, gj1)[s // 2]
            for c in range(3):
                block = masked_panel(gj, 3 * (s % 2) + c, lambda k: mj[s, k : k + 1, W * c : W * (c + 1)])
                put_left(left_j, block, 3 * W * c)
            both = dot(left_j[...], right_x[3 * W * s : 3 * W * (s + 3), :])
            rs[W * s : W * (s + 1), :] = rv[W * s : W * (s + 1), :] - both[:, :W]
            put_left(left_r.at[s], -both[:, W:])

    pl.when(even | (chip < 3))(forward_later)
    pl.when(even | (chip == 0))(prepare)

    @pl.when(odd & (chip < 3))
    def _():
        for k, rows in enumerate(chunks):
            send_up(k).wait_recv()
            put_left(left_v.at[rows], e_in[k])

            @pl.when(chip > 0)
            def _():
                e_out[k] = ht[k] + dot(left_v[rows, :], right_u[...])
                send_up(k).start()

            ea_out[k] = wb[k] + dot(left_v[rows, :], right_n[...])
            share_up(k).start()

    pl.when(odd & (chip == 3))(forward_later)
    pl.when(odd & (chip > 0))(prepare)

    @pl.when(even)
    def _():
        for k in range(CHUNKS):
            share_up(k).wait_recv()

    @pl.when(last)
    def _():
        e_in[...] = jnp.zeros_like(e_in)

    put_right(right_e, e_in[...].reshape(W, W).T)
    for s in range(4):
        rows = slice(W * s, W * (s + 1))
        xs[rows, :] = xl[s] + dot(left_x[s, :, 3 * W :], right_e[...])
        rs[rows, :] = rs[rows, :] + dot(left_r[s], right_e[...])

    for g in gathers + later:
        g.sent()

    @pl.when(node > 0)
    def _():
        border[0].wait_send()
        border[1].wait_send()

    @pl.when(jnp.logical_not(last))
    def _():
        border[2].wait_send()

    def sent(cond, *copies):
        @pl.when(cond)
        def _():
            for copy in copies:
                for k in range(CHUNKS):
                    copy(k).wait_send()

    sent(odd & (chip < 3), send_down)
    sent(odd & (chip > 0), share_down)
    sent(odd & (chip > 0), send_up)
    sent(odd, share_up)
    sent(even, send_g)

    @pl.when(even)
    def _():
        for copy in hand:
            copy.wait_send()


def on_device(*args):
    f32, bf16 = jnp.float32, jnp.bfloat16
    out = jax.ShapeDtypeStruct(args[0].shape, f32)
    hbm = pl.BlockSpec(memory_space=pltpu.HBM)
    vmem = pltpu.VMEM
    return pl.pallas_call(
        kernel,
        out_shape=(out, out),
        in_specs=[hbm] * 6,
        out_specs=(pl.BlockSpec(memory_space=vmem),) * 2,
        scratch_shapes=[
            vmem((4, 2, 4, 4, 8, W), f32),
            vmem((4, 2, 4, 4, 8, W), f32),
            vmem((4, 2, 4, 6, 8, W), f32),
            vmem((4, 2, 4, 6, 8, W), f32),
            vmem((4, 2, 4, 8, W), f32),
            vmem((4, 2, 4, 8, W), f32),
            vmem((4 * W, W), f32),
            vmem((4, 4, 4), jnp.int32),
            vmem((4, 4, 12), jnp.int32),
            vmem((4, 4, W), f32),
            vmem((4, 4, 3 * W), f32),
            vmem((4, W), f32),
            vmem((4, W, 3 * W), bf16),
            vmem((4, W, 3 * W), bf16),
            vmem((4, W, 3 * W), bf16),
            vmem((3, W, 3 * W), bf16),
            vmem((4, W, 6 * W), bf16),
            vmem((W, 9 * W), bf16),
            vmem((2, W, 3 * W), bf16),
            vmem((4, W, 3 * W), bf16),
            vmem((W, 3 * W), bf16),
            vmem((W, 3 * W), bf16),
            vmem((W, 3 * W), bf16),
            vmem((W, 3 * W), bf16),
            vmem((4, 3 * W, 2 * W), bf16),
            vmem((4, 3 * W, W), bf16),
            vmem((4, 3 * W, 2 * W), bf16),
            vmem((3 * W, 2 * W), bf16),
            vmem((18 * W, 2 * W), bf16),
            vmem((3 * W, W), bf16),
            vmem((3 * W, W), bf16),
            vmem((3 * W, W), bf16),
            vmem((3 * W, W), bf16),
            vmem((3 * W, W), bf16),
            vmem((3 * W, W), bf16),
            vmem((3 * W, W), bf16),
            vmem((3 * W, W), bf16),
            vmem((3 * W, W), bf16),
            vmem((3 * W, W), bf16),
            vmem((4, W, W), f32),
            vmem((4, W, W), f32),
            vmem((W, W), f32),
            vmem((W, W), f32),
            vmem((W, W), f32),
            vmem((W, W), f32),
            vmem((W, W), f32),
            vmem((W, W), f32),
            vmem((W, W), f32),
            vmem((W, W), f32),
            vmem((W, W), f32),
            vmem((W, W), f32),
            vmem((W, W), f32),
            vmem((CHUNKS, PART, W), f32),
            vmem((CHUNKS, PART, W), f32),
            vmem((CHUNKS, PART, W), f32),
            vmem((CHUNKS, PART, W), f32),
            vmem((CHUNKS, PART, W), f32),
            vmem((CHUNKS, PART, W), f32),
            vmem((CHUNKS, PART, W), f32),
            vmem((CHUNKS, PART, W), f32),
            vmem((CHUNKS, PART, W), f32),
            pltpu.SemaphoreType.DMA((84,)),
            pltpu.SemaphoreType.DMA((84,)),
            pltpu.SemaphoreType.DMA((24,)),
            pltpu.SemaphoreType.REGULAR((2,)),
        ],
        compiler_params=pltpu.CompilerParams(
            collective_id=0, has_side_effects=True, vmem_limit_bytes=48 * 1024 * 1024
        ),
    )(*[pltpu.with_memory_space_constraint(a, pltpu.HBM) for a in args])


def solution(mesh):
    in_specs = (
        P("node", "rhs"),
        P("node", "rhs", None),
        P("node", "rhs", None),
        P("node", None, None),
        P("node", "rhs", None),
        P("node", None, None),
    )
    out_specs = (P("node", "rhs"), P("node", "rhs"))
    return jax.shard_map(on_device, mesh=mesh, in_specs=in_specs, out_specs=out_specs, check_vma=False)
```

```python
import jax
import jax.numpy as jnp
from jax import lax
from jax.experimental import pallas as pl
from jax.experimental.pallas import tpu as pltpu
from jax.sharding import PartitionSpec as P

MESH_ID = pl.DeviceIdType.MESH
B = 64
W = 256
NODES = 8
CHUNKS = 4
PART = W // CHUNKS


class Sems:
    def __init__(self, send, recv, local):
        self.send, self.recv, self.local = send, recv, local
        self.pairs = self.locals = 0

    def pair(self):
        k = self.pairs
        self.pairs += 1
        return self.send.at[k], self.recv.at[k]

    def one(self):
        k = self.locals
        self.locals += 1
        return self.local.at[k]


class Ring:
    def __init__(self, sems, where, pos, device_at, near=False):
        self.where, self.pos, self.near = where, pos, near
        self.opposite = device_at(lax.rem(pos + 2, 4))
        self.up, self.down = device_at(lax.rem(pos + 1, 4)), device_at(lax.rem(pos + 3, 4))
        self.sems = {key: sems.pair() for key in ("u0", "d0", "u1", "d1", "f0", "f1")}
        self.started = {}

    def at(self, q, step):
        return self.where(q, lax.rem(self.pos + step, 4))

    def copy(self, key, q, step, device, source=None):
        part = self.at(q, step)
        send, recv = self.sems[key]
        return pltpu.make_async_remote_copy(
            src_ref=part if source is None else source,
            dst_ref=part,
            send_sem=send,
            recv_sem=recv,
            device_id=device,
            device_id_type=MESH_ID,
        )

    def go(self, key, *args):
        self.started[key] = args
        self.copy(key, *args).start()

    def direct(self, q, source=None):
        if self.near and q == 1:
            self.go("f1", 1, 0, self.opposite, source)
        first, second = ("d", "u") if (q == 0) == self.near else ("u", "d")
        for way in (first, second):
            self.go(f"{way}{q}", q, 0, self.up if way == "u" else self.down, source)

    def arrived(self, key, q, step):
        self.copy(key, q, step, self.up).wait_recv()

    def forward(self, q):
        if self.near:
            if q == 0:
                self.arrived("d0", 0, 1)
                self.go("f0", 0, 1, self.down)
        elif q == 0:
            self.arrived("u0", 0, 3)
            self.go("f0", 0, 3, self.up)
        else:
            self.arrived("d1", 1, 1)
            self.go("f1", 1, 1, self.down)

    def finish(self, q):
        if self.near or q == 1:
            self.arrived(f"u{q}", q, 3)
        if (self.near and q == 1) or (not self.near and q == 0):
            self.arrived(f"d{q}", q, 1)
        self.arrived(f"f{q}", q, 2)

    def sent(self):
        for key, args in self.started.items():
            self.copy(key, *args).wait_send()


class Gather:
    def __init__(self, sems, buf, x, zl, y, device, y_first):
        self.own = buf.at[x, zl, y]

        def layer(q):
            return zl if q == 0 else 1 - zl

        if y_first:
            self.first = Ring(sems, lambda q, p: buf.at[x, layer(q), p], y, lambda p: device(x, zl, p), True)
            self.second = Ring(sems, lambda q, p: buf.at[p, layer(q)], x, lambda p: device(p, zl, y))
        else:
            self.first = Ring(sems, lambda q, p: buf.at[p, layer(q), y], x, lambda p: device(p, zl, y), True)
            self.second = Ring(sems, lambda q, p: buf.at[:, layer(q), p], y, lambda p: device(x, zl, p))
        send, recv = sems.pair()
        self.cross_sems = send, recv
        self.partner = device(x, 1 - zl, y)
        self.other = buf.at[x, 1 - zl, y]

    def cross(self, part, source):
        send, recv = self.cross_sems
        return pltpu.make_async_remote_copy(
            src_ref=source, dst_ref=part, send_sem=send, recv_sem=recv, device_id=self.partner, device_id_type=MESH_ID
        )

    def start(self, source=None):
        source = self.own if source is None else source
        self.sent_cross = self.cross(self.own, source)
        self.sent_cross.start()
        self.first.direct(0, source)

    def crossed(self):
        self.cross(self.other, self.other).wait_recv()
        self.first.direct(1)

    def sent(self):
        self.sent_cross.wait_send()
        self.first.sent()
        self.second.sent()


def split(value):
    high = value.astype(jnp.bfloat16)
    return high, (value - high.astype(jnp.float32)).astype(jnp.bfloat16)


def put_left(ref, value, at=0):
    high, low = split(value)
    for k, part in enumerate((high, low, high)):
        ref[:, at + k * W : at + (k + 1) * W] = part


def put_right(ref, value, col=0, row=0):
    high, low = split(value)
    cols = slice(col, col + value.shape[1])
    for k, part in enumerate((high, high, low)):
        ref[row + k * W : row + (k + 1) * W, cols] = part


def dot(left, right):
    return jnp.dot(left, right, preferred_element_type=jnp.float32)


def panel(buf, s):
    return [(buf[x] if s is None else buf[x, :, :, s]).reshape(B, W) for x in range(4)]


def masked_panel(buf, s, weights):
    return jnp.concatenate([part * weights(x) for x, part in enumerate(panel(buf, s))], axis=0)


def rows_of(pattern):
    block = lax.broadcasted_iota(jnp.int32, (4, W), 1) // B
    values = pattern.astype(jnp.float32)
    out = jnp.zeros((4, W), jnp.float32)
    for k in range(4):
        out = jnp.where(block == k, values[:, k : k + 1], out)
    return out


def kernel(
    r_in, d_in, l_in, pl_in, j_in, pj_in,
    xs, rs,
    gd, gl, gj0, gj1, gn, gp, rv, pat_l, pat_j, ml, mj, mn,
    left_d, left_dt, left_a, left_bt, left_x, left_j, left_e, left_r, left_m, left_g, left_w, left_v,
    right_rl, right_lt, right_f, right_b, right_x, right_p, right_q, right_g, right_u, right_c, right_e, right_n, right_xc, right_xe, right_xca,
    u, xl, pt, pa, ct, cn, x0, xea, et, xlt, xct, xla, xca, gt, ga, wb, ht, c_in, e_in, c_out, e_out, ea_out,
    send_sem, recv_sem, local_sem, ready_sem,
):
    rhs, node = lax.axis_index("rhs"), lax.axis_index("node")
    x, zl, y = rhs // 8, (rhs // 4) % 2, rhs % 4
    after, before = node + 1, node - 1
    first, last = node == 0, node == NODES - 1
    chip, odd = node // 2, node % 2 == 1
    even = jnp.logical_not(odd)
    partner = node + 1 - 2 * (node % 2)
    two_after, two_before = node + 2, node - 2

    def device(px, pz, py):
        return (px * 8 + pz * 4 + py, node)

    sems = Sems(send_sem, recv_sem, local_sem)

    def load(source, target):
        copy = pltpu.make_async_copy(source, target, sems.one())
        copy.start()
        return copy

    barrier = pltpu.get_barrier_semaphore()
    peers = [device(x, 1 - zl, y)]
    peers += [device(x, zl, lax.rem(y + k, 4)) for k in (1, 2, 3)]
    peers += [device(lax.rem(x + k, 4), zl, y) for k in (1, 2, 3)]
    for peer in peers:
        pl.semaphore_signal(barrier, inc=1, device_id=peer, device_id_type=MESH_ID)
    for step in (1, 2):

        @pl.when(node + step < NODES)
        def _():
            pl.semaphore_signal(barrier, inc=1, device_id=(rhs, node + step), device_id_type=MESH_ID)

    for least in (0, 1, 2):

        @pl.when(node == least if least < 2 else node >= 2)
        def _():
            pl.semaphore_wait(barrier, len(peers) + least)

    for step in (1, 2):

        @pl.when(node >= step)
        def _():
            pl.semaphore_signal(ready_sem.at[step - 1], inc=1, device_id=(rhs, node - step), device_id_type=MESH_ID)

    gathers = [
        Gather(sems, gd, x, zl, y, device, True),
        Gather(sems, gl, x, zl, y, device, False),
    ]
    later = [
        Gather(sems, gj0, x, zl, y, device, True),
        Gather(sems, gj1, x, zl, y, device, False),
    ]

    def remote(source, target, pair, to):
        return pltpu.make_async_remote_copy(
            src_ref=source,
            dst_ref=target,
            send_sem=pair[0],
            recv_sem=pair[1],
            device_id=(rhs, to),
            device_id_type=MESH_ID,
        )

    for g, source in zip(gathers, (d_in, l_in)):
        g.start(source)
    border = [
        remote(ml.at[0], mn, sems.pair(), before),
        remote(gl.at[:, :, :, 0], gn, sems.pair(), before),
        remote(gd.at[:, :, :, 3], gp, sems.pair(), after),
    ]
    own_d = load(d_in, gd.at[x, zl, y])
    own_l = load(l_in, gl.at[x, zl, y])
    pat_loads = [load(pl_in, pat_l), load(pj_in, pat_j)]
    j_loads = []
    for h, gj in enumerate((gj0, gj1)):
        for s in range(2):
            for c in range(3):
                j_loads.append(load(j_in.at[2 * h + s, :, W * c : W * (c + 1)], gj.at[x, zl, y, 3 * s + c]))
    r_load = load(r_in, rv)
    own_d.wait()
    own_l.wait()
    for g in gathers:
        g.crossed()
    for q in (0, 1):
        for g in gathers:
            g.first.forward(q)
    for q in (0, 1):
        for g in gathers:
            g.first.finish(q)
            g.second.direct(q)
    r_load.wait()
    for copy in pat_loads + j_loads:
        copy.wait()
    for s in range(4):
        ml[s] = rows_of(pat_l[s])
        for c in range(3):
            mj[s, :, W * c : W * (c + 1)] = rows_of(pat_j[s, :, 4 * c : 4 * (c + 1)])
    def stage(number):
        def run():
            if number < 2:
                for g in later:
                    (g.start, g.crossed)[number]()
                return
            for q in (0, 1):
                for g in later:
                    if number == 2:
                        g.first.forward(q)
                    elif number == 3:
                        g.first.finish(q)
                        g.second.direct(q)
                    else:
                        g.second.forward(q)

        return run

    early = chip > 1
    slow = chip < 2
    pl.when(early)(stage(0))
    for q in (0, 1):
        for g in gathers:
            g.second.forward(q)
    pl.when(early)(stage(1))
    for q in (0, 1):
        for g in gathers:
            g.second.finish(q)

    @pl.when(node > 0)
    def _():
        border[0].start()
        border[1].start()

    @pl.when(last)
    def _():
        mn[...] = jnp.zeros_like(mn)
        gn[...] = jnp.zeros_like(gn)

    @pl.when(first)
    def _():
        gp[...] = jnp.zeros_like(gp)


    pl.when(slow)(stage(0))
    pl.when(early)(stage(2))

    for s in range(4):
        d = jnp.concatenate(panel(gd, s), axis=0)
        put_left(left_d.at[s], d)
        put_left(left_dt.at[s], d.T)
        low = masked_panel(gl, s, lambda k: ml[s, k : k + 1, :])
        right = right_rl.at[s]
        put_right(right, rv[W * s : W * (s + 1), :])
        put_right(right, low, W)
        if s == 0:
            put_left(left_e.at[0], -low.T)
        else:
            put_right(right_lt.at[s - 1], low.T)
        both = dot(left_d[s], right[...])
        if s == 0:
            put_right(right_f.at[0], both[:, :W])
            put_right(right_f.at[0], -both[:, W:], W)
        else:
            u[s] = both[:, :W]
            put_left(left_a.at[s], -both[:, W:])
    for s in range(1, 4):
        both = dot(left_a[s], right_f[s - 1])
        fs = u[s] + both[:, :W]
        put_right(right_f.at[s], fs)
        put_right(right_f.at[s], both[:, W:], W)
        if s == 3:
            gt[...] = fs.T.reshape(CHUNKS, PART, W)
            pt[...] = both[:, W:].T

    chunks = [slice(PART * k, PART * (k + 1)) for k in range(CHUNKS)]
    down, fan_down, up, fan_up, join = [[sems.pair() for k in range(CHUNKS)] for _ in range(5)]
    hand = [
        remote(pt, pa, sems.pair(), partner),
        remote(xlt, xla, sems.pair(), partner),
        remote(xct, xca, sems.pair(), partner),
        remote(x0, xea, sems.pair(), partner),
    ]

    def send_g(k):
        return remote(gt.at[k], ga.at[k], join[k], partner)

    def send_down(k):
        return remote(c_out.at[k], c_in.at[k], down[k], two_after)

    def share_down(k):
        return remote(c_in.at[k], c_in.at[k], fan_down[k], partner)

    def send_up(k):
        return remote(e_out.at[k], e_in.at[k], up[k], two_before)

    def share_up(k):
        return remote(ea_out.at[k], e_in.at[k], fan_up[k], partner)

    for step in (1, 2):

        @pl.when(node + step < NODES)
        def _():
            pl.semaphore_wait(ready_sem.at[step - 1], 1)

    @pl.when(even)
    def _():
        for k in range(CHUNKS):
            send_g(k).start()
        hand[0].start()

    @pl.when(chip == 0)
    def _():
        c_in[...] = jnp.zeros_like(c_in)
        left_m[...] = jnp.zeros_like(left_m)

    @pl.when(slow)
    def _():
        stage(1)()
        stage(2)()

    pl.when(early)(stage(3))

    @pl.when(odd)
    def _():
        put_right(right_p, pt[...])
        for k, rows in enumerate(chunks):
            send_g(k).wait_recv()
            put_left(left_w.at[rows], ga[k])
            c_out[k] = gt[k] + dot(left_w[rows, :], right_p[...])

            @pl.when(chip == 0)
            def _():
                send_down(k).start()

        hand[0].wait_recv()
        put_left(left_g, pa[...])
        put_right(right_g, pa[...])
        put_right(right_q, dot(left_g[...], right_p[...]))

    def turn(k):
        rows = chunks[k]
        mine = ga[k] + dot(left_m[rows, :], right_g[...])
        ct[rows, :] = mine
        put_left(left_w.at[rows], mine)
        wb[k] = xlt[rows, :] + dot(left_w[rows, :], right_xc[...])
        put_left(left_v.at[rows], wb[k])
        head = xla[rows, :] + dot(left_m[rows, :], right_xca[...]) + dot(left_v[rows, :], right_xe[...])

        @pl.when(chip < 3)
        def _():
            ht[k] = head

        @pl.when(chip == 3)
        def _():
            e_out[k] = head
            send_up(k).start()
            ea_out[k] = wb[k]
            share_up(k).start()

    def relay_down():
        for k, rows in enumerate(chunks):
            send_down(k).wait_recv()
            put_left(left_m.at[rows], c_in[k])

            @pl.when(chip < 3)
            def _():
                c_out[k] = c_out[k] + dot(left_m[rows, :], right_q[...])
                send_down(k).start()

            share_down(k).start()
            pl.when(chip == 3)(lambda: turn(k))

    pl.when(odd & (chip == 0))(stage(3))
    for s in range(3):
        put_left(left_bt.at[s], -dot(left_dt[s], right_lt[s]))
    for s in range(3, -1, -1):
        both = dot(left_dt[s], right_f[s])
        if s < 3:
            both = both + dot(left_bt[s], right_b[...])
        if s > 0:
            put_right(right_b, both)
        xl[s] = both[:, :W]
        put_left(left_x.at[s], both[:, W:])
        if s == 0:
            xlt[...] = both[:, :W].T
            xct[...] = both[:, W:].T

    @pl.when(even)
    def _():
        hand[1].start()
        hand[2].start()

    @pl.when(odd)
    def _():
        put_right(right_xc, xct[...])

    pl.when(odd & (chip > 0) & (chip < 3))(relay_down)

    pl.when((even & slow) | (node == 3))(stage(3))

    @pl.when(jnp.logical_not(last))
    def _():
        border[0].wait_recv()
        border[1].wait_recv()

    nxt = masked_panel(gn, None, lambda k: mn[k : k + 1, :])
    put_right(right_lt.at[3], nxt.T)
    for s in range(3, -1, -1):
        if s == 3:
            xe = -dot(left_dt[3], right_lt[3])
        else:
            xe = dot(left_bt[s], right_x[3 * W * (s + 2) : 3 * W * (s + 3), W:])
        put_right(right_x, xe, W, 3 * W * (s + 1))
        put_left(left_x.at[s], xe, 3 * W)
        if s == 0:
            x0[...] = xe.T

    @pl.when(even)
    def _():
        hand[3].start()

    @pl.when(odd)
    def _():
        put_right(right_n, x0[...])
        put_left(left_g, x0[...])
        hand[1].wait_recv()
        hand[2].wait_recv()
        put_right(right_xca, xca[...])
        hand[3].wait_recv()
        put_right(right_xe, xea[...])
        put_right(right_u, dot(left_g[...], right_xe[...]))

    pl.when(odd & (chip == 3))(stage(4))
    pl.when(odd & (chip == 3))(relay_down)

    @pl.when(odd & (chip < 3))
    def _():
        for k in range(CHUNKS):
            turn(k)

    @pl.when(even)
    def _():
        @pl.when(chip > 0)
        def _():
            for k in range(CHUNKS):
                share_down(k).wait_recv()

        ct[...] = c_in[...].reshape(W, W)

    @pl.when(jnp.logical_not(last))
    def _():
        border[2].start()

    def prepare():
        cn[...] = ct[...].T
        put_right(right_c, cn[...])
        for s in range(4):
            xl[s] = xl[s] + dot(left_x[s, :, : 3 * W], right_c[...])
            put_right(right_x, xl[s], 0, 3 * W * (s + 1))
        diagonal = lax.broadcasted_iota(jnp.int32, (W, W), 0) == lax.broadcasted_iota(jnp.int32, (W, W), 1)
        put_right(right_x, jnp.zeros((W, W), jnp.float32), 0, 15 * W)
        put_right(right_x, diagonal.astype(jnp.float32), W, 15 * W)
        pl.when(node > 0)(lambda: border[2].wait_recv())
        prev = jnp.concatenate(panel(gp, None), axis=0)
        put_left(left_e.at[1], prev.T)
        both = dot(left_e[0], right_x[3 * W : 6 * W, :])
        put_right(right_b, both[:, :W] + cn[...])
        put_right(right_b, both[:, W:], W)
        both = dot(left_e[1], right_b[...])
        put_right(right_x, jnp.where(first, 0.0, both))
        for q in (0, 1):
            for g in later:
                g.second.finish(q)
        for s in range(4):
            gj = (gj0, gj1)[s // 2]
            for c in range(3):
                block = masked_panel(gj, 3 * (s % 2) + c, lambda k: mj[s, k : k + 1, W * c : W * (c + 1)])
                put_left(left_j, block, 3 * W * c)
            both = dot(left_j[...], right_x[3 * W * s : 3 * W * (s + 3), :])
            rs[W * s : W * (s + 1), :] = rv[W * s : W * (s + 1), :] - both[:, :W]
            put_left(left_r.at[s], -both[:, W:])

    pl.when(even | (chip < 3))(stage(4))
    pl.when(even | (chip == 0))(prepare)

    @pl.when(odd & (chip < 3))
    def _():
        for k, rows in enumerate(chunks):
            send_up(k).wait_recv()
            put_left(left_v.at[rows], e_in[k])

            @pl.when(chip > 0)
            def _():
                e_out[k] = ht[k] + dot(left_v[rows, :], right_u[...])
                send_up(k).start()

            ea_out[k] = wb[k] + dot(left_v[rows, :], right_n[...])
            share_up(k).start()

    pl.when(odd & (chip > 0))(prepare)

    @pl.when(even)
    def _():
        for k in range(CHUNKS):
            share_up(k).wait_recv()

    @pl.when(last)
    def _():
        e_in[...] = jnp.zeros_like(e_in)

    put_right(right_e, e_in[...].reshape(W, W).T)
    for s in range(4):
        rows = slice(W * s, W * (s + 1))
        xs[rows, :] = xl[s] + dot(left_x[s, :, 3 * W :], right_e[...])
        rs[rows, :] = rs[rows, :] + dot(left_r[s], right_e[...])

    for g in gathers + later:
        g.sent()

    @pl.when(node > 0)
    def _():
        border[0].wait_send()
        border[1].wait_send()

    @pl.when(jnp.logical_not(last))
    def _():
        border[2].wait_send()

    def sent(cond, *copies):
        @pl.when(cond)
        def _():
            for copy in copies:
                for k in range(CHUNKS):
                    copy(k).wait_send()

    sent(odd & (chip < 3), send_down)
    sent(odd & (chip > 0), share_down)
    sent(odd & (chip > 0), send_up)
    sent(odd, share_up)
    sent(even, send_g)

    @pl.when(even)
    def _():
        for copy in hand:
            copy.wait_send()


def on_device(*args):
    f32, bf16 = jnp.float32, jnp.bfloat16
    out = jax.ShapeDtypeStruct(args[0].shape, f32)
    hbm = pl.BlockSpec(memory_space=pltpu.HBM)
    vmem = pltpu.VMEM
    return pl.pallas_call(
        kernel,
        out_shape=(out, out),
        in_specs=[hbm] * 6,
        out_specs=(pl.BlockSpec(memory_space=vmem),) * 2,
        scratch_shapes=[
            vmem((4, 2, 4, 4, 8, W), f32),
            vmem((4, 2, 4, 4, 8, W), f32),
            vmem((4, 2, 4, 6, 8, W), f32),
            vmem((4, 2, 4, 6, 8, W), f32),
            vmem((4, 2, 4, 8, W), f32),
            vmem((4, 2, 4, 8, W), f32),
            vmem((4 * W, W), f32),
            vmem((4, 4, 4), jnp.int32),
            vmem((4, 4, 12), jnp.int32),
            vmem((4, 4, W), f32),
            vmem((4, 4, 3 * W), f32),
            vmem((4, W), f32),
            vmem((4, W, 3 * W), bf16),
            vmem((4, W, 3 * W), bf16),
            vmem((4, W, 3 * W), bf16),
            vmem((3, W, 3 * W), bf16),
            vmem((4, W, 6 * W), bf16),
            vmem((W, 9 * W), bf16),
            vmem((2, W, 3 * W), bf16),
            vmem((4, W, 3 * W), bf16),
            vmem((W, 3 * W), bf16),
            vmem((W, 3 * W), bf16),
            vmem((W, 3 * W), bf16),
            vmem((W, 3 * W), bf16),
            vmem((4, 3 * W, 2 * W), bf16),
            vmem((4, 3 * W, W), bf16),
            vmem((4, 3 * W, 2 * W), bf16),
            vmem((3 * W, 2 * W), bf16),
            vmem((18 * W, 2 * W), bf16),
            vmem((3 * W, W), bf16),
            vmem((3 * W, W), bf16),
            vmem((3 * W, W), bf16),
            vmem((3 * W, W), bf16),
            vmem((3 * W, W), bf16),
            vmem((3 * W, W), bf16),
            vmem((3 * W, W), bf16),
            vmem((3 * W, W), bf16),
            vmem((3 * W, W), bf16),
            vmem((3 * W, W), bf16),
            vmem((4, W, W), f32),
            vmem((4, W, W), f32),
            vmem((W, W), f32),
            vmem((W, W), f32),
            vmem((W, W), f32),
            vmem((W, W), f32),
            vmem((W, W), f32),
            vmem((W, W), f32),
            vmem((W, W), f32),
            vmem((W, W), f32),
            vmem((W, W), f32),
            vmem((W, W), f32),
            vmem((W, W), f32),
            vmem((CHUNKS, PART, W), f32),
            vmem((CHUNKS, PART, W), f32),
            vmem((CHUNKS, PART, W), f32),
            vmem((CHUNKS, PART, W), f32),
            vmem((CHUNKS, PART, W), f32),
            vmem((CHUNKS, PART, W), f32),
            vmem((CHUNKS, PART, W), f32),
            vmem((CHUNKS, PART, W), f32),
            vmem((CHUNKS, PART, W), f32),
            pltpu.SemaphoreType.DMA((84,)),
            pltpu.SemaphoreType.DMA((84,)),
            pltpu.SemaphoreType.DMA((24,)),
            pltpu.SemaphoreType.REGULAR((2,)),
        ],
        compiler_params=pltpu.CompilerParams(
            collective_id=0, has_side_effects=True, vmem_limit_bytes=48 * 1024 * 1024
        ),
    )(*[pltpu.with_memory_space_constraint(a, pltpu.HBM) for a in args])


def solution(mesh):
    in_specs = (
        P("node", "rhs"),
        P("node", "rhs", None),
        P("node", "rhs", None),
        P("node", None, None),
        P("node", "rhs", None),
        P("node", None, None),
    )
    out_specs = (P("node", "rhs"), P("node", "rhs"))
    return jax.shard_map(on_device, mesh=mesh, in_specs=in_specs, out_specs=out_specs, check_vma=False)
```

```python
import jax
import jax.numpy as jnp
from jax import lax
from jax.experimental import pallas as pl
from jax.experimental.pallas import tpu as pltpu
from jax.sharding import PartitionSpec as P

MESH_ID = pl.DeviceIdType.MESH
B = 64
W = 256
NODES = 8
CHUNKS = 4
PART = W // CHUNKS


class Sems:
    def __init__(self, send, recv, local):
        self.send, self.recv, self.local = send, recv, local
        self.pairs = self.locals = 0

    def pair(self):
        k = self.pairs
        self.pairs += 1
        return self.send.at[k], self.recv.at[k]

    def one(self):
        k = self.locals
        self.locals += 1
        return self.local.at[k]


class Ring:
    def __init__(self, sems, where, pos, device_at, near=False):
        self.where, self.pos, self.near = where, pos, near
        self.opposite = device_at(lax.rem(pos + 2, 4))
        self.up, self.down = device_at(lax.rem(pos + 1, 4)), device_at(lax.rem(pos + 3, 4))
        self.sems = {key: sems.pair() for key in ("u0", "d0", "u1", "d1", "f0", "f1")}
        self.started = {}

    def at(self, q, step):
        return self.where(q, lax.rem(self.pos + step, 4))

    def copy(self, key, q, step, device, source=None):
        part = self.at(q, step)
        send, recv = self.sems[key]
        return pltpu.make_async_remote_copy(
            src_ref=part if source is None else source,
            dst_ref=part,
            send_sem=send,
            recv_sem=recv,
            device_id=device,
            device_id_type=MESH_ID,
        )

    def go(self, key, *args):
        self.started[key] = args
        self.copy(key, *args).start()

    def direct(self, q, source=None):
        if self.near and q == 1:
            self.go("f1", 1, 0, self.opposite, source)
        first, second = ("d", "u") if (q == 0) == self.near else ("u", "d")
        for way in (first, second):
            self.go(f"{way}{q}", q, 0, self.up if way == "u" else self.down, source)

    def arrived(self, key, q, step):
        self.copy(key, q, step, self.up).wait_recv()

    def forward(self, q):
        if self.near:
            if q == 0:
                self.arrived("d0", 0, 1)
                self.go("f0", 0, 1, self.down)
        elif q == 0:
            self.arrived("u0", 0, 3)
            self.go("f0", 0, 3, self.up)
        else:
            self.arrived("d1", 1, 1)
            self.go("f1", 1, 1, self.down)

    def finish(self, q):
        if self.near or q == 1:
            self.arrived(f"u{q}", q, 3)
        if (self.near and q == 1) or (not self.near and q == 0):
            self.arrived(f"d{q}", q, 1)
        self.arrived(f"f{q}", q, 2)

    def sent(self):
        for key, args in self.started.items():
            self.copy(key, *args).wait_send()


class Gather:
    def __init__(self, sems, buf, x, zl, y, device, y_first):
        self.own = buf.at[x, zl, y]

        def layer(q):
            return zl if q == 0 else 1 - zl

        if y_first:
            self.first = Ring(sems, lambda q, p: buf.at[x, layer(q), p], y, lambda p: device(x, zl, p), True)
            self.second = Ring(sems, lambda q, p: buf.at[p, layer(q)], x, lambda p: device(p, zl, y))
        else:
            self.first = Ring(sems, lambda q, p: buf.at[p, layer(q), y], x, lambda p: device(p, zl, y), True)
            self.second = Ring(sems, lambda q, p: buf.at[:, layer(q), p], y, lambda p: device(x, zl, p))
        send, recv = sems.pair()
        self.cross_sems = send, recv
        self.partner = device(x, 1 - zl, y)
        self.other = buf.at[x, 1 - zl, y]

    def cross(self, part, source):
        send, recv = self.cross_sems
        return pltpu.make_async_remote_copy(
            src_ref=source, dst_ref=part, send_sem=send, recv_sem=recv, device_id=self.partner, device_id_type=MESH_ID
        )

    def start(self, source=None):
        source = self.own if source is None else source
        self.sent_cross = self.cross(self.own, source)
        self.sent_cross.start()
        self.first.direct(0, source)

    def crossed(self):
        self.cross(self.other, self.other).wait_recv()
        self.first.direct(1)

    def sent(self):
        self.sent_cross.wait_send()
        self.first.sent()
        self.second.sent()


def split(value):
    high = value.astype(jnp.bfloat16)
    return high, (value - high.astype(jnp.float32)).astype(jnp.bfloat16)


def put_left(ref, value, at=0):
    high, low = split(value)
    for k, part in enumerate((high, low, high)):
        ref[:, at + k * W : at + (k + 1) * W] = part


def put_right(ref, value, col=0, row=0):
    high, low = split(value)
    cols = slice(col, col + value.shape[1])
    for k, part in enumerate((high, high, low)):
        ref[row + k * W : row + (k + 1) * W, cols] = part


def dot(left, right):
    return jnp.dot(left, right, preferred_element_type=jnp.float32)


def panel(buf, s):
    return [(buf[x] if s is None else buf[x, :, :, s]).reshape(B, W) for x in range(4)]


def masked_panel(buf, s, weights):
    return jnp.concatenate([part * weights(x) for x, part in enumerate(panel(buf, s))], axis=0)


def rows_of(pattern):
    block = lax.broadcasted_iota(jnp.int32, (4, W), 1) // B
    values = pattern.astype(jnp.float32)
    out = jnp.zeros((4, W), jnp.float32)
    for k in range(4):
        out = jnp.where(block == k, values[:, k : k + 1], out)
    return out


def kernel(
    r_in, d_in, l_in, pl_in, j_in, pj_in,
    xl, rs, left_x, left_r, right_e,
    gd, gl, gj0, gj1, gn, gp, rv, pat_l, pat_j, ml, mj, mn,
    left_d, left_dt, left_a, left_bt, left_c, left_j, left_e, left_m, left_g, left_w, left_v,
    right_rl, right_lt, right_f, right_b, right_x, right_p, right_q, right_g, right_u, right_c, right_n, right_xc, right_xe, right_xca,
    u, pt, pa, ct, cn, x0, xea, et, xlt, xct, xla, xca, gt, ga, wb, ht, c_in, e_in, c_out, e_out, ea_out,
    send_sem, recv_sem, local_sem, ready_sem,
):
    rhs, node = lax.axis_index("rhs"), lax.axis_index("node")
    x, zl, y = rhs // 8, (rhs // 4) % 2, rhs % 4
    after, before = node + 1, node - 1
    first, last = node == 0, node == NODES - 1
    chip, odd = node // 2, node % 2 == 1
    even = jnp.logical_not(odd)
    partner = node + 1 - 2 * (node % 2)
    two_after, two_before = node + 2, node - 2

    def device(px, pz, py):
        return (px * 8 + pz * 4 + py, node)

    sems = Sems(send_sem, recv_sem, local_sem)

    def load(source, target):
        copy = pltpu.make_async_copy(source, target, sems.one())
        copy.start()
        return copy

    barrier = pltpu.get_barrier_semaphore()
    peers = [device(x, 1 - zl, y)]
    peers += [device(x, zl, lax.rem(y + k, 4)) for k in (1, 2, 3)]
    peers += [device(lax.rem(x + k, 4), zl, y) for k in (1, 2, 3)]
    for peer in peers:
        pl.semaphore_signal(barrier, inc=1, device_id=peer, device_id_type=MESH_ID)
    for step in (1, 2):

        @pl.when(node + step < NODES)
        def _():
            pl.semaphore_signal(barrier, inc=1, device_id=(rhs, node + step), device_id_type=MESH_ID)

    for least in (0, 1, 2):

        @pl.when(node == least if least < 2 else node >= 2)
        def _():
            pl.semaphore_wait(barrier, len(peers) + least)

    for step in (1, 2):

        @pl.when(node >= step)
        def _():
            pl.semaphore_signal(ready_sem.at[step - 1], inc=1, device_id=(rhs, node - step), device_id_type=MESH_ID)

    gathers = [
        Gather(sems, gd, x, zl, y, device, True),
        Gather(sems, gl, x, zl, y, device, False),
    ]
    later = [
        Gather(sems, gj0, x, zl, y, device, True),
        Gather(sems, gj1, x, zl, y, device, False),
    ]

    def remote(source, target, pair, to):
        return pltpu.make_async_remote_copy(
            src_ref=source,
            dst_ref=target,
            send_sem=pair[0],
            recv_sem=pair[1],
            device_id=(rhs, to),
            device_id_type=MESH_ID,
        )

    for g, source in zip(gathers, (d_in, l_in)):
        g.start(source)
    border = [
        remote(ml.at[0], mn, sems.pair(), before),
        remote(gl.at[:, :, :, 0], gn, sems.pair(), before),
        remote(gd.at[:, :, :, 3], gp, sems.pair(), after),
    ]
    own_d = load(d_in, gd.at[x, zl, y])
    own_l = load(l_in, gl.at[x, zl, y])
    pat_loads = [load(pl_in, pat_l), load(pj_in, pat_j)]
    j_loads = []
    for h, gj in enumerate((gj0, gj1)):
        for s in range(2):
            for c in range(3):
                j_loads.append(load(j_in.at[2 * h + s, :, W * c : W * (c + 1)], gj.at[x, zl, y, 3 * s + c]))
    r_load = load(r_in, rv)
    own_d.wait()
    own_l.wait()
    for g in gathers:
        g.crossed()
    for q in (0, 1):
        for g in gathers:
            g.first.forward(q)
    def second_pieces():
        for g in gathers:
            g.second.direct(1)

    for q in (0, 1):
        for g in gathers:
            g.first.finish(q)
            if q == 0:
                g.second.direct(0)
    pl.when(even)(second_pieces)
    r_load.wait()
    for copy in pat_loads + j_loads:
        copy.wait()
    for s in range(4):
        ml[s] = rows_of(pat_l[s])
        for c in range(3):
            mj[s, :, W * c : W * (c + 1)] = rows_of(pat_j[s, :, 4 * c : 4 * (c + 1)])
    def stage(number):
        def run():
            if number < 2:
                for g in later:
                    (g.start, g.crossed)[number]()
                return
            for q in (0, 1):
                for g in later:
                    if number == 2:
                        g.first.forward(q)
                    elif number == 3:
                        g.first.finish(q)
                        g.second.direct(q)
                    else:
                        g.second.forward(q)

        return run

    early = chip > 1
    slow = chip < 2
    pl.when(early)(stage(0))
    for g in gathers:
        g.second.forward(0)
    pl.when(odd)(second_pieces)
    for g in gathers:
        g.second.forward(1)
    pl.when(early)(stage(1))
    for q in (0, 1):
        for g in gathers:
            g.second.finish(q)

    @pl.when(node > 0)
    def _():
        border[0].start()
        border[1].start()

    @pl.when(last)
    def _():
        mn[...] = jnp.zeros_like(mn)
        gn[...] = jnp.zeros_like(gn)

    @pl.when(first)
    def _():
        gp[...] = jnp.zeros_like(gp)


    pl.when(slow)(stage(0))
    pl.when(early)(stage(2))

    for s in range(4):
        d = jnp.concatenate(panel(gd, s), axis=0)
        put_left(left_d.at[s], d)
        low = masked_panel(gl, s, lambda k: ml[s, k : k + 1, :])
        right = right_rl.at[s]
        put_right(right, rv[W * s : W * (s + 1), :])
        put_right(right, low, W)
        both = dot(left_d[s], right[...])
        if s == 0:
            put_right(right_f.at[0], both[:, :W])
            put_right(right_f.at[0], -both[:, W:], W)
        else:
            u[s] = both[:, :W]
            put_left(left_a.at[s], -both[:, W:])
    for s in range(1, 4):
        both = dot(left_a[s], right_f[s - 1])
        fs = u[s] + both[:, :W]
        put_right(right_f.at[s], fs)
        put_right(right_f.at[s], both[:, W:], W)
        if s == 3:
            gt[...] = fs.T.reshape(CHUNKS, PART, W)
            pt[...] = both[:, W:].T

    chunks = [slice(PART * k, PART * (k + 1)) for k in range(CHUNKS)]
    down, fan_down, up, fan_up, join = [[sems.pair() for k in range(CHUNKS)] for _ in range(5)]
    hand = [
        remote(pt, pa, sems.pair(), partner),
        remote(xlt, xla, sems.pair(), partner),
        remote(xct, xca, sems.pair(), partner),
        remote(x0, xea, sems.pair(), partner),
    ]

    def send_g(k):
        return remote(gt.at[k], ga.at[k], join[k], partner)

    def send_down(k):
        return remote(c_out.at[k], c_in.at[k], down[k], two_after)

    def share_down(k):
        return remote(c_in.at[k], c_in.at[k], fan_down[k], partner)

    def send_up(k):
        return remote(e_out.at[k], e_in.at[k], up[k], two_before)

    def share_up(k):
        return remote(ea_out.at[k], e_in.at[k], fan_up[k], partner)

    for step in (1, 2):

        @pl.when(node + step < NODES)
        def _():
            pl.semaphore_wait(ready_sem.at[step - 1], 1)

    @pl.when(even)
    def _():
        for k in range(CHUNKS):
            send_g(k).start()
        hand[0].start()

    @pl.when(chip == 0)
    def _():
        c_in[...] = jnp.zeros_like(c_in)
        left_m[...] = jnp.zeros_like(left_m)

    @pl.when(slow)
    def _():
        stage(1)()
        stage(2)()

    pl.when(early)(stage(3))

    @pl.when(odd)
    def _():
        put_right(right_p, pt[...])
        for k, rows in enumerate(chunks):
            send_g(k).wait_recv()
            put_left(left_w.at[rows], ga[k])
            c_out[k] = gt[k] + dot(left_w[rows, :], right_p[...])

            @pl.when(chip == 0)
            def _():
                send_down(k).start()

        hand[0].wait_recv()
        put_left(left_g, pa[...])
        put_right(right_g, pa[...])
        put_right(right_q, dot(left_g[...], right_p[...]))

    def turn(k):
        rows = chunks[k]
        mine = ga[k] + dot(left_m[rows, :], right_g[...])
        ct[rows, :] = mine
        put_left(left_w.at[rows], mine)
        wb[k] = xlt[rows, :] + dot(left_w[rows, :], right_xc[...])
        put_left(left_v.at[rows], wb[k])
        head = xla[rows, :] + dot(left_m[rows, :], right_xca[...]) + dot(left_v[rows, :], right_xe[...])

        @pl.when(chip < 3)
        def _():
            ht[k] = head

        @pl.when(chip == 3)
        def _():
            e_out[k] = head
            send_up(k).start()
            ea_out[k] = wb[k]
            share_up(k).start()

    def relay_down():
        for k, rows in enumerate(chunks):
            send_down(k).wait_recv()
            put_left(left_m.at[rows], c_in[k])

            @pl.when(chip < 3)
            def _():
                c_out[k] = c_out[k] + dot(left_m[rows, :], right_q[...])
                send_down(k).start()

            share_down(k).start()
            pl.when(chip == 3)(lambda: turn(k))

    pl.when(odd & (chip == 0))(stage(3))
    for s in range(4):
        put_left(left_dt.at[s], jnp.concatenate(panel(gd, s), axis=0).T)
        low = masked_panel(gl, s, lambda k: ml[s, k : k + 1, :])
        if s == 0:
            put_left(left_e.at[0], -low.T)
        else:
            put_right(right_lt.at[s - 1], low.T)
    for s in range(3):
        put_left(left_bt.at[s], -dot(left_dt[s], right_lt[s]))
    for s in range(3, -1, -1):
        both = dot(left_dt[s], right_f[s])
        if s < 3:
            both = both + dot(left_bt[s], right_b[...])
        if s > 0:
            put_right(right_b, both)
        xl[s] = both[:, :W]
        put_left(left_c.at[s], both[:, W:])
        if s == 0:
            xlt[...] = both[:, :W].T
            xct[...] = both[:, W:].T

    @pl.when(even)
    def _():
        hand[1].start()
        hand[2].start()

    @pl.when(odd)
    def _():
        put_right(right_xc, xct[...])

    pl.when(odd & (chip > 0) & (chip < 3))(relay_down)

    pl.when((even & slow) | (node == 3))(stage(3))

    @pl.when(jnp.logical_not(last))
    def _():
        border[0].wait_recv()
        border[1].wait_recv()

    nxt = masked_panel(gn, None, lambda k: mn[k : k + 1, :])
    put_right(right_lt.at[3], nxt.T)
    for s in range(3, -1, -1):
        if s == 3:
            xe = -dot(left_dt[3], right_lt[3])
        else:
            xe = dot(left_bt[s], right_x[3 * W * (s + 2) : 3 * W * (s + 3), W:])
        put_right(right_x, xe, W, 3 * W * (s + 1))
        put_left(left_x.at[s], xe)
        if s == 0:
            x0[...] = xe.T

    @pl.when(even)
    def _():
        hand[3].start()

    @pl.when(odd)
    def _():
        put_right(right_n, x0[...])
        put_left(left_g, x0[...])
        hand[1].wait_recv()
        hand[2].wait_recv()
        put_right(right_xca, xca[...])
        hand[3].wait_recv()
        put_right(right_xe, xea[...])
        put_right(right_u, dot(left_g[...], right_xe[...]))

    pl.when(odd & (chip == 3))(stage(4))
    pl.when(odd & (chip == 3))(relay_down)

    @pl.when(odd & (chip < 3))
    def _():
        for k in range(CHUNKS):
            turn(k)

    @pl.when(even)
    def _():
        @pl.when(chip > 0)
        def _():
            for k in range(CHUNKS):
                share_down(k).wait_recv()

        ct[...] = c_in[...].reshape(W, W)

    @pl.when(jnp.logical_not(last))
    def _():
        border[2].start()

    def prepare():
        cn[...] = ct[...].T
        put_right(right_c, cn[...])
        for s in range(4):
            xl[s] = xl[s] + dot(left_c[s], right_c[...])
            put_right(right_x, xl[s], 0, 3 * W * (s + 1))
        diagonal = lax.broadcasted_iota(jnp.int32, (W, W), 0) == lax.broadcasted_iota(jnp.int32, (W, W), 1)
        put_right(right_x, jnp.zeros((W, W), jnp.float32), 0, 15 * W)
        put_right(right_x, diagonal.astype(jnp.float32), W, 15 * W)
        pl.when(node > 0)(lambda: border[2].wait_recv())
        prev = jnp.concatenate(panel(gp, None), axis=0)
        put_left(left_e.at[1], prev.T)
        both = dot(left_e[0], right_x[3 * W : 6 * W, :])
        put_right(right_b, both[:, :W] + cn[...])
        put_right(right_b, both[:, W:], W)
        both = dot(left_e[1], right_b[...])
        put_right(right_x, jnp.where(first, 0.0, both))
        for q in (0, 1):
            for g in later:
                g.second.finish(q)
        for s in range(4):
            gj = (gj0, gj1)[s // 2]
            for c in range(3):
                block = masked_panel(gj, 3 * (s % 2) + c, lambda k: mj[s, k : k + 1, W * c : W * (c + 1)])
                put_left(left_j, block, 3 * W * c)
            both = dot(left_j[...], right_x[3 * W * s : 3 * W * (s + 3), :])
            rs[W * s : W * (s + 1), :] = rv[W * s : W * (s + 1), :] - both[:, :W]
            put_left(left_r.at[s], -both[:, W:])

    pl.when(even | (chip < 3))(stage(4))
    pl.when(even | (chip == 0))(prepare)

    @pl.when(odd & (chip < 3))
    def _():
        for k, rows in enumerate(chunks):
            send_up(k).wait_recv()
            put_left(left_v.at[rows], e_in[k])

            @pl.when(chip > 0)
            def _():
                e_out[k] = ht[k] + dot(left_v[rows, :], right_u[...])
                send_up(k).start()

            ea_out[k] = wb[k] + dot(left_v[rows, :], right_n[...])
            share_up(k).start()

    pl.when(odd & (chip > 0))(prepare)

    @pl.when(even)
    def _():
        for k in range(CHUNKS):
            share_up(k).wait_recv()

    @pl.when(last)
    def _():
        e_in[...] = jnp.zeros_like(e_in)

    put_right(right_e, e_in[...].reshape(W, W).T)
    for g in gathers + later:
        g.sent()

    @pl.when(node > 0)
    def _():
        border[0].wait_send()
        border[1].wait_send()

    @pl.when(jnp.logical_not(last))
    def _():
        border[2].wait_send()

    def sent(cond, *copies):
        @pl.when(cond)
        def _():
            for copy in copies:
                for k in range(CHUNKS):
                    copy(k).wait_send()

    sent(odd & (chip < 3), send_down)
    sent(odd & (chip > 0), share_down)
    sent(odd & (chip > 0), send_up)
    sent(odd, share_up)
    sent(even, send_g)

    @pl.when(even)
    def _():
        for copy in hand:
            copy.wait_send()


def last_kernel(xl, rs, left_x, left_r, right_e, sol_out, res_out, buf, sem):
    copies = []
    for s in range(4):
        rows = slice(W * s, W * (s + 1))
        for k, (base, left, out) in enumerate(((xl[s], left_x, sol_out), (rs[rows, :], left_r, res_out))):
            buf[k, rows, :] = base + dot(left[s], right_e[...])
            copies.append(pltpu.make_async_copy(buf.at[k, rows], out.at[rows], sem.at[k, s]))
            copies[-1].start()
    for copy in copies:
        copy.wait()


def on_device(*args):
    f32, bf16 = jnp.float32, jnp.bfloat16
    rows, columns = args[0].shape
    hbm, vmem = pl.BlockSpec(memory_space=pltpu.HBM), pltpu.VMEM
    held = pl.BlockSpec(memory_space=vmem)
    shape = jax.ShapeDtypeStruct
    parts = pl.pallas_call(
        kernel,
        out_shape=(
            shape((4, W, W), f32),
            shape((4 * W, W), f32),
            shape((4, W, 3 * W), bf16),
            shape((4, W, 3 * W), bf16),
            shape((3 * W, W), bf16),
        ),
        in_specs=[hbm] * 6,
        out_specs=(held,) * 5,
        scratch_shapes=[
            vmem((4, 2, 4, 4, 8, W), f32),
            vmem((4, 2, 4, 4, 8, W), f32),
            vmem((4, 2, 4, 6, 8, W), f32),
            vmem((4, 2, 4, 6, 8, W), f32),
            vmem((4, 2, 4, 8, W), f32),
            vmem((4, 2, 4, 8, W), f32),
            vmem((4 * W, W), f32),
            vmem((4, 4, 4), jnp.int32),
            vmem((4, 4, 12), jnp.int32),
            vmem((4, 4, W), f32),
            vmem((4, 4, 3 * W), f32),
            vmem((4, W), f32),
            vmem((4, W, 3 * W), bf16),
            vmem((4, W, 3 * W), bf16),
            vmem((4, W, 3 * W), bf16),
            vmem((3, W, 3 * W), bf16),
            vmem((4, W, 3 * W), bf16),
            vmem((W, 9 * W), bf16),
            vmem((2, W, 3 * W), bf16),
            vmem((W, 3 * W), bf16),
            vmem((W, 3 * W), bf16),
            vmem((W, 3 * W), bf16),
            vmem((W, 3 * W), bf16),
            vmem((4, 3 * W, 2 * W), bf16),
            vmem((4, 3 * W, W), bf16),
            vmem((4, 3 * W, 2 * W), bf16),
            vmem((3 * W, 2 * W), bf16),
            vmem((18 * W, 2 * W), bf16),
            vmem((3 * W, W), bf16),
            vmem((3 * W, W), bf16),
            vmem((3 * W, W), bf16),
            vmem((3 * W, W), bf16),
            vmem((3 * W, W), bf16),
            vmem((3 * W, W), bf16),
            vmem((3 * W, W), bf16),
            vmem((3 * W, W), bf16),
            vmem((3 * W, W), bf16),
            vmem((4, W, W), f32),
            vmem((W, W), f32),
            vmem((W, W), f32),
            vmem((W, W), f32),
            vmem((W, W), f32),
            vmem((W, W), f32),
            vmem((W, W), f32),
            vmem((W, W), f32),
            vmem((W, W), f32),
            vmem((W, W), f32),
            vmem((W, W), f32),
            vmem((W, W), f32),
            vmem((CHUNKS, PART, W), f32),
            vmem((CHUNKS, PART, W), f32),
            vmem((CHUNKS, PART, W), f32),
            vmem((CHUNKS, PART, W), f32),
            vmem((CHUNKS, PART, W), f32),
            vmem((CHUNKS, PART, W), f32),
            vmem((CHUNKS, PART, W), f32),
            vmem((CHUNKS, PART, W), f32),
            vmem((CHUNKS, PART, W), f32),
            pltpu.SemaphoreType.DMA((84,)),
            pltpu.SemaphoreType.DMA((84,)),
            pltpu.SemaphoreType.DMA((24,)),
            pltpu.SemaphoreType.REGULAR((2,)),
        ],
        compiler_params=pltpu.CompilerParams(
            collective_id=0, has_side_effects=True, vmem_limit_bytes=48 * 1024 * 1024
        ),
    )(*[pltpu.with_memory_space_constraint(a, pltpu.HBM) for a in args])
    out = shape((rows, columns), f32)
    return pl.pallas_call(
        last_kernel,
        out_shape=(out, out),
        in_specs=[held] * 5,
        out_specs=(hbm, hbm),
        scratch_shapes=[vmem((2, rows, columns), f32), pltpu.SemaphoreType.DMA((2, 4))],
        compiler_params=pltpu.CompilerParams(vmem_limit_bytes=16 * 1024 * 1024),
    )(*parts)


def solution(mesh):
    in_specs = (
        P("node", "rhs"),
        P("node", "rhs", None),
        P("node", "rhs", None),
        P("node", None, None),
        P("node", "rhs", None),
        P("node", None, None),
    )
    out_specs = (P("node", "rhs"), P("node", "rhs"))
    return jax.shard_map(on_device, mesh=mesh, in_specs=in_specs, out_specs=out_specs, check_vma=False)
```

```python
import jax
import jax.numpy as jnp
from jax import lax
from jax.experimental import pallas as pl
from jax.experimental.pallas import tpu as pltpu
from jax.sharding import PartitionSpec as P

MESH_ID = pl.DeviceIdType.MESH
B = 64
W = 256
NODES = 8
CHUNKS = 8
PART = W // CHUNKS


class Sems:
    def __init__(self, send, recv, local):
        self.send, self.recv, self.local = send, recv, local
        self.pairs = self.locals = 0

    def pair(self):
        k = self.pairs
        self.pairs += 1
        return self.send.at[k], self.recv.at[k]

    def one(self):
        k = self.locals
        self.locals += 1
        return self.local.at[k]


class Ring:
    def __init__(self, sems, where, pos, device_at, near=False):
        self.where, self.pos, self.near = where, pos, near
        self.opposite = device_at(lax.rem(pos + 2, 4))
        self.up, self.down = device_at(lax.rem(pos + 1, 4)), device_at(lax.rem(pos + 3, 4))
        self.sems = {key: sems.pair() for key in ("u0", "d0", "u1", "d1", "f0", "f1")}
        self.started = {}

    def at(self, q, step):
        return self.where(q, lax.rem(self.pos + step, 4))

    def copy(self, key, q, step, device, source=None):
        part = self.at(q, step)
        send, recv = self.sems[key]
        return pltpu.make_async_remote_copy(
            src_ref=part if source is None else source,
            dst_ref=part,
            send_sem=send,
            recv_sem=recv,
            device_id=device,
            device_id_type=MESH_ID,
        )

    def go(self, key, *args):
        self.started[key] = args
        self.copy(key, *args).start()

    def direct(self, q, source=None):
        if self.near and q == 1:
            self.go("f1", 1, 0, self.opposite, source)
        first, second = ("d", "u") if (q == 0) == self.near else ("u", "d")
        for way in (first, second):
            self.go(f"{way}{q}", q, 0, self.up if way == "u" else self.down, source)

    def arrived(self, key, q, step):
        self.copy(key, q, step, self.up).wait_recv()

    def forward(self, q):
        if self.near:
            if q == 0:
                self.arrived("d0", 0, 1)
                self.go("f0", 0, 1, self.down)
        elif q == 0:
            self.arrived("u0", 0, 3)
            self.go("f0", 0, 3, self.up)
        else:
            self.arrived("d1", 1, 1)
            self.go("f1", 1, 1, self.down)

    def finish(self, q):
        if self.near or q == 1:
            self.arrived(f"u{q}", q, 3)
        if (self.near and q == 1) or (not self.near and q == 0):
            self.arrived(f"d{q}", q, 1)
        self.arrived(f"f{q}", q, 2)

    def sent(self):
        for key, args in self.started.items():
            self.copy(key, *args).wait_send()


class Gather:
    def __init__(self, sems, buf, x, zl, y, device, y_first):
        self.own = buf.at[x, zl, y]

        def layer(q):
            return zl if q == 0 else 1 - zl

        if y_first:
            self.first = Ring(sems, lambda q, p: buf.at[x, layer(q), p], y, lambda p: device(x, zl, p), True)
            self.second = Ring(sems, lambda q, p: buf.at[p, layer(q)], x, lambda p: device(p, zl, y))
        else:
            self.first = Ring(sems, lambda q, p: buf.at[p, layer(q), y], x, lambda p: device(p, zl, y), True)
            self.second = Ring(sems, lambda q, p: buf.at[:, layer(q), p], y, lambda p: device(x, zl, p))
        send, recv = sems.pair()
        self.cross_sems = send, recv
        self.partner = device(x, 1 - zl, y)
        self.other = buf.at[x, 1 - zl, y]

    def cross(self, part, source):
        send, recv = self.cross_sems
        return pltpu.make_async_remote_copy(
            src_ref=source, dst_ref=part, send_sem=send, recv_sem=recv, device_id=self.partner, device_id_type=MESH_ID
        )

    def start(self, source=None):
        source = self.own if source is None else source
        self.sent_cross = self.cross(self.own, source)
        self.sent_cross.start()
        self.first.direct(0, source)

    def crossed(self):
        self.cross(self.other, self.other).wait_recv()
        self.first.direct(1)

    def sent(self):
        self.sent_cross.wait_send()
        self.first.sent()
        self.second.sent()


def split(value):
    high = value.astype(jnp.bfloat16)
    return high, (value - high.astype(jnp.float32)).astype(jnp.bfloat16)


def put_left(ref, value, at=0):
    high, low = split(value)
    for k, part in enumerate((high, low, high)):
        ref[:, at + k * W : at + (k + 1) * W] = part


def put_right(ref, value, col=0, row=0):
    high, low = split(value)
    cols = slice(col, col + value.shape[1])
    for k, part in enumerate((high, high, low)):
        ref[row + k * W : row + (k + 1) * W, cols] = part


def dot(left, right):
    return jnp.dot(left, right, preferred_element_type=jnp.float32)


def panel(buf, s):
    return [(buf[x] if s is None else buf[x, :, :, s]).reshape(B, W) for x in range(4)]


def masked_panel(buf, s, weights):
    return jnp.concatenate([part * weights(x) for x, part in enumerate(panel(buf, s))], axis=0)


def rows_of(pattern):
    block = lax.broadcasted_iota(jnp.int32, (4, W), 1) // B
    values = pattern.astype(jnp.float32)
    out = jnp.zeros((4, W), jnp.float32)
    for k in range(4):
        out = jnp.where(block == k, values[:, k : k + 1], out)
    return out


def kernel(
    r_in, d_in, l_in, pl_in, j_in, pj_in,
    xl, rs, left_x, left_r, right_e,
    gd, gl, gj0, gj1, gn, gp, rv, pat_l, pat_j, ml, mj, mn,
    left_d, left_dt, left_a, left_bt, left_c, left_j, left_e, left_m, left_g, left_w, left_v,
    right_rl, right_lt, right_f, right_b, right_x, right_p, right_q, right_g, right_u, right_c, right_n, right_xc, right_xe, right_xca,
    u, pt, pa, ct, cn, x0, xea, et, xlt, xct, xla, xca, gt, ga, wb, ht, c_in, e_in, c_out, e_out, ea_out,
    send_sem, recv_sem, local_sem, ready_sem,
):
    rhs, node = lax.axis_index("rhs"), lax.axis_index("node")
    x, zl, y = rhs // 8, (rhs // 4) % 2, rhs % 4
    after, before = node + 1, node - 1
    first, last = node == 0, node == NODES - 1
    chip, odd = node // 2, node % 2 == 1
    even = jnp.logical_not(odd)
    partner = node + 1 - 2 * (node % 2)
    two_after, two_before = node + 2, node - 2

    def device(px, pz, py):
        return (px * 8 + pz * 4 + py, node)

    sems = Sems(send_sem, recv_sem, local_sem)

    def load(source, target):
        copy = pltpu.make_async_copy(source, target, sems.one())
        copy.start()
        return copy

    barrier = pltpu.get_barrier_semaphore()
    peers = [device(x, 1 - zl, y)]
    peers += [device(x, zl, lax.rem(y + k, 4)) for k in (1, 2, 3)]
    peers += [device(lax.rem(x + k, 4), zl, y) for k in (1, 2, 3)]
    for peer in peers:
        pl.semaphore_signal(barrier, inc=1, device_id=peer, device_id_type=MESH_ID)
    for step in (1, 2):

        @pl.when(node + step < NODES)
        def _():
            pl.semaphore_signal(barrier, inc=1, device_id=(rhs, node + step), device_id_type=MESH_ID)

    for least in (0, 1, 2):

        @pl.when(node == least if least < 2 else node >= 2)
        def _():
            pl.semaphore_wait(barrier, len(peers) + least)

    for step in (1, 2):

        @pl.when(node >= step)
        def _():
            pl.semaphore_signal(ready_sem.at[step - 1], inc=1, device_id=(rhs, node - step), device_id_type=MESH_ID)

    gathers = [
        Gather(sems, gd, x, zl, y, device, True),
        Gather(sems, gl, x, zl, y, device, False),
    ]
    later = [
        Gather(sems, gj0, x, zl, y, device, True),
        Gather(sems, gj1, x, zl, y, device, False),
    ]

    def remote(source, target, pair, to):
        return pltpu.make_async_remote_copy(
            src_ref=source,
            dst_ref=target,
            send_sem=pair[0],
            recv_sem=pair[1],
            device_id=(rhs, to),
            device_id_type=MESH_ID,
        )

    for g, source in zip(gathers, (d_in, l_in)):
        g.start(source)
    border = [
        remote(ml.at[0], mn, sems.pair(), before),
        remote(gl.at[:, :, :, 0], gn, sems.pair(), before),
        remote(gd.at[:, :, :, 3], gp, sems.pair(), after),
    ]
    own_d = load(d_in, gd.at[x, zl, y])
    own_l = load(l_in, gl.at[x, zl, y])
    pat_loads = [load(pl_in, pat_l), load(pj_in, pat_j)]
    j_loads = []
    for h, gj in enumerate((gj0, gj1)):
        for s in range(2):
            for c in range(3):
                j_loads.append(load(j_in.at[2 * h + s, :, W * c : W * (c + 1)], gj.at[x, zl, y, 3 * s + c]))
    r_load = load(r_in, rv)
    own_d.wait()
    own_l.wait()
    for g in gathers:
        g.crossed()
    for q in (0, 1):
        for g in gathers:
            g.first.forward(q)
    def second_pieces():
        for g in gathers:
            g.second.direct(1)

    for q in (0, 1):
        for g in gathers:
            g.first.finish(q)
            if q == 0:
                g.second.direct(0)
    pl.when(even)(second_pieces)
    r_load.wait()
    for copy in pat_loads + j_loads:
        copy.wait()
    for s in range(4):
        ml[s] = rows_of(pat_l[s])
        for c in range(3):
            mj[s, :, W * c : W * (c + 1)] = rows_of(pat_j[s, :, 4 * c : 4 * (c + 1)])
    def stage(number):
        def run():
            if number < 2:
                for g in later:
                    (g.start, g.crossed)[number]()
                return
            for q in (0, 1):
                for g in later:
                    if number == 2:
                        g.first.forward(q)
                    elif number == 3:
                        g.first.finish(q)
                        g.second.direct(q)
                    else:
                        g.second.forward(q)

        return run

    early = chip > 1
    slow = chip < 2
    pl.when(early)(stage(0))
    for g in gathers:
        g.second.forward(0)
    pl.when(odd)(second_pieces)
    for g in gathers:
        g.second.forward(1)
    pl.when(early)(stage(1))
    for q in (0, 1):
        for g in gathers:
            g.second.finish(q)

    @pl.when(node > 0)
    def _():
        border[0].start()
        border[1].start()

    @pl.when(last)
    def _():
        mn[...] = jnp.zeros_like(mn)
        gn[...] = jnp.zeros_like(gn)

    @pl.when(first)
    def _():
        gp[...] = jnp.zeros_like(gp)


    pl.when(slow)(stage(0))
    pl.when(early)(stage(2))

    for s in range(4):
        d = jnp.concatenate(panel(gd, s), axis=0)
        put_left(left_d.at[s], d)
        low = masked_panel(gl, s, lambda k: ml[s, k : k + 1, :])
        right = right_rl.at[s]
        put_right(right, rv[W * s : W * (s + 1), :])
        put_right(right, low, W)
        both = dot(left_d[s], right[...])
        if s == 0:
            put_right(right_f.at[0], both[:, :W])
            put_right(right_f.at[0], -both[:, W:], W)
        else:
            u[s] = both[:, :W]
            put_left(left_a.at[s], -both[:, W:])
    for s in range(1, 4):
        both = dot(left_a[s], right_f[s - 1])
        fs = u[s] + both[:, :W]
        put_right(right_f.at[s], fs)
        put_right(right_f.at[s], both[:, W:], W)
        if s == 3:
            gt[...] = fs.T.reshape(CHUNKS, PART, W)
            pt[...] = both[:, W:].T

    chunks = [slice(PART * k, PART * (k + 1)) for k in range(CHUNKS)]
    down, fan_down, up, fan_up, join = [[sems.pair() for k in range(CHUNKS)] for _ in range(5)]
    hand = [
        remote(pt, pa, sems.pair(), partner),
        remote(xlt, xla, sems.pair(), partner),
        remote(xct, xca, sems.pair(), partner),
        remote(x0, xea, sems.pair(), partner),
    ]

    def send_g(k):
        return remote(gt.at[k], ga.at[k], join[k], partner)

    def send_down(k):
        return remote(c_out.at[k], c_in.at[k], down[k], two_after)

    def share_down(k):
        return remote(c_in.at[k], c_in.at[k], fan_down[k], partner)

    def send_up(k):
        return remote(e_out.at[k], e_in.at[k], up[k], two_before)

    def share_up(k):
        return remote(ea_out.at[k], e_in.at[k], fan_up[k], partner)

    for step in (1, 2):

        @pl.when(node + step < NODES)
        def _():
            pl.semaphore_wait(ready_sem.at[step - 1], 1)

    @pl.when(even)
    def _():
        for k in range(CHUNKS):
            send_g(k).start()
        hand[0].start()

    @pl.when(chip == 0)
    def _():
        c_in[...] = jnp.zeros_like(c_in)
        left_m[...] = jnp.zeros_like(left_m)

    @pl.when(slow)
    def _():
        stage(1)()
        stage(2)()

    pl.when(early)(stage(3))

    @pl.when(odd)
    def _():
        put_right(right_p, pt[...])
        for k, rows in enumerate(chunks):
            send_g(k).wait_recv()
            put_left(left_w.at[rows], ga[k])
            c_out[k] = gt[k] + dot(left_w[rows, :], right_p[...])

            @pl.when(chip == 0)
            def _():
                send_down(k).start()

        hand[0].wait_recv()
        put_left(left_g, pa[...])
        put_right(right_g, pa[...])
        put_right(right_q, dot(left_g[...], right_p[...]))

    def turn(k):
        rows = chunks[k]
        mine = ga[k] + dot(left_m[rows, :], right_g[...])
        ct[rows, :] = mine
        put_left(left_w.at[rows], mine)
        wb[k] = xlt[rows, :] + dot(left_w[rows, :], right_xc[...])
        put_left(left_v.at[rows], wb[k])
        head = xla[rows, :] + dot(left_m[rows, :], right_xca[...]) + dot(left_v[rows, :], right_xe[...])

        e_out[k] = head
        send_up(k).start()
        ea_out[k] = wb[k]
        share_up(k).start()

    def relay_down():
        for k, rows in enumerate(chunks):
            send_down(k).wait_recv()
            put_left(left_m.at[rows], c_in[k])

            @pl.when(chip < 3)
            def _():
                c_out[k] = c_out[k] + dot(left_m[rows, :], right_q[...])
                send_down(k).start()

            share_down(k).start()
            pl.when(chip == 3)(lambda: turn(k))

    pl.when(chip == 0)(stage(3))
    for s in range(4):
        put_left(left_dt.at[s], jnp.concatenate(panel(gd, s), axis=0).T)
        low = masked_panel(gl, s, lambda k: ml[s, k : k + 1, :])
        if s == 0:
            put_left(left_e.at[0], -low.T)
        else:
            put_right(right_lt.at[s - 1], low.T)
    for s in range(3):
        put_left(left_bt.at[s], -dot(left_dt[s], right_lt[s]))
    for s in range(3, -1, -1):
        both = dot(left_dt[s], right_f[s])
        if s < 3:
            both = both + dot(left_bt[s], right_b[...])
        if s > 0:
            put_right(right_b, both)
        xl[s] = both[:, :W]
        put_left(left_c.at[s], both[:, W:])
        if s == 0:
            xlt[...] = both[:, :W].T
            xct[...] = both[:, W:].T

    @pl.when(even)
    def _():
        hand[1].start()
        hand[2].start()

    @pl.when(odd)
    def _():
        put_right(right_xc, xct[...])

    pl.when(odd & (chip > 0) & (chip < 3))(relay_down)

    pl.when(chip == 1)(stage(3))

    @pl.when(jnp.logical_not(last))
    def _():
        border[0].wait_recv()
        border[1].wait_recv()

    nxt = masked_panel(gn, None, lambda k: mn[k : k + 1, :])
    put_right(right_lt.at[3], nxt.T)
    for s in range(3, -1, -1):
        if s == 3:
            xe = -dot(left_dt[3], right_lt[3])
        else:
            xe = dot(left_bt[s], right_x[3 * W * (s + 2) : 3 * W * (s + 3), W:])
        put_right(right_x, xe, W, 3 * W * (s + 1))
        put_left(left_x.at[s], xe)
        if s == 0:
            x0[...] = xe.T

    @pl.when(even)
    def _():
        hand[3].start()

    @pl.when(odd)
    def _():
        put_right(right_n, x0[...])
        put_left(left_g, x0[...])
        hand[1].wait_recv()
        hand[2].wait_recv()
        put_right(right_xca, xca[...])
        hand[3].wait_recv()
        put_right(right_xe, xea[...])
        put_right(right_u, dot(left_g[...], right_xe[...]))

    pl.when(odd & (chip == 3))(stage(4))
    pl.when(odd & (chip == 3))(relay_down)

    @pl.when(odd & (chip < 3))
    def _():
        mine = ga[...].reshape(W, W) + dot(left_m[...], right_g[...])
        ct[...] = mine
        put_left(left_w, mine)
        mine = xlt[...] + dot(left_w[...], right_xc[...])
        wb[...] = mine.reshape(CHUNKS, PART, W)
        put_left(left_v, mine)
        head = xla[...] + dot(left_m[...], right_xca[...]) + dot(left_v[...], right_xe[...])
        ht[...] = head.reshape(CHUNKS, PART, W)

    @pl.when(even)
    def _():
        @pl.when(chip > 0)
        def _():
            for k in range(CHUNKS):
                share_down(k).wait_recv()

        ct[...] = c_in[...].reshape(W, W)

    @pl.when(jnp.logical_not(last))
    def _():
        border[2].start()

    def prepare():
        cn[...] = ct[...].T
        put_right(right_c, cn[...])
        for s in range(4):
            xl[s] = xl[s] + dot(left_c[s], right_c[...])
            put_right(right_x, xl[s], 0, 3 * W * (s + 1))
        diagonal = lax.broadcasted_iota(jnp.int32, (W, W), 0) == lax.broadcasted_iota(jnp.int32, (W, W), 1)
        put_right(right_x, jnp.zeros((W, W), jnp.float32), 0, 15 * W)
        put_right(right_x, diagonal.astype(jnp.float32), W, 15 * W)
        pl.when(node > 0)(lambda: border[2].wait_recv())
        prev = jnp.concatenate(panel(gp, None), axis=0)
        put_left(left_e.at[1], prev.T)
        both = dot(left_e[0], right_x[3 * W : 6 * W, :])
        put_right(right_b, both[:, :W] + cn[...])
        put_right(right_b, both[:, W:], W)
        both = dot(left_e[1], right_b[...])
        put_right(right_x, jnp.where(first, 0.0, both))
        for q in (0, 1):
            for g in later:
                g.second.finish(q)
        for s in range(4):
            gj = (gj0, gj1)[s // 2]
            for c in range(3):
                block = masked_panel(gj, 3 * (s % 2) + c, lambda k: mj[s, k : k + 1, W * c : W * (c + 1)])
                put_left(left_j, block, 3 * W * c)
            both = dot(left_j[...], right_x[3 * W * s : 3 * W * (s + 3), :])
            rs[W * s : W * (s + 1), :] = rv[W * s : W * (s + 1), :] - both[:, :W]
            put_left(left_r.at[s], -both[:, W:])

    pl.when(even | (chip < 3))(stage(4))
    pl.when(even | (chip == 0))(prepare)

    @pl.when(odd & (chip < 3))
    def _():
        for k, rows in enumerate(chunks):
            send_up(k).wait_recv()
            put_left(left_v.at[rows], e_in[k])

            @pl.when(chip > 0)
            def _():
                e_out[k] = ht[k] + dot(left_v[rows, :], right_u[...])
                send_up(k).start()

            ea_out[k] = wb[k] + dot(left_v[rows, :], right_n[...])
            share_up(k).start()

    pl.when(odd & (chip > 0))(prepare)

    @pl.when(even)
    def _():
        for k in range(CHUNKS):
            share_up(k).wait_recv()

    @pl.when(last)
    def _():
        e_in[...] = jnp.zeros_like(e_in)

    put_right(right_e, e_in[...].reshape(W, W).T)
    for g in gathers + later:
        g.sent()

    @pl.when(node > 0)
    def _():
        border[0].wait_send()
        border[1].wait_send()

    @pl.when(jnp.logical_not(last))
    def _():
        border[2].wait_send()

    def sent(cond, *copies):
        @pl.when(cond)
        def _():
            for copy in copies:
                for k in range(CHUNKS):
                    copy(k).wait_send()

    sent(odd & (chip < 3), send_down)
    sent(odd & (chip > 0), share_down)
    sent(odd & (chip > 0), send_up)
    sent(odd, share_up)
    sent(even, send_g)

    @pl.when(even)
    def _():
        for copy in hand:
            copy.wait_send()


def last_kernel(xl, rs, left_x, left_r, right_e, sol_out, res_out, buf, sem):
    copies = []
    for s in range(4):
        rows = slice(W * s, W * (s + 1))
        for k, (base, left, out) in enumerate(((xl[s], left_x, sol_out), (rs[rows, :], left_r, res_out))):
            buf[k, rows, :] = base + dot(left[s], right_e[...])
            copies.append(pltpu.make_async_copy(buf.at[k, rows], out.at[rows], sem.at[k, s]))
            copies[-1].start()
    for copy in copies:
        copy.wait()


def on_device(*args):
    f32, bf16 = jnp.float32, jnp.bfloat16
    rows, columns = args[0].shape
    hbm, vmem = pl.BlockSpec(memory_space=pltpu.HBM), pltpu.VMEM
    held = pl.BlockSpec(memory_space=vmem)
    shape = jax.ShapeDtypeStruct
    parts = pl.pallas_call(
        kernel,
        out_shape=(
            shape((4, W, W), f32),
            shape((4 * W, W), f32),
            shape((4, W, 3 * W), bf16),
            shape((4, W, 3 * W), bf16),
            shape((3 * W, W), bf16),
        ),
        in_specs=[hbm] * 6,
        out_specs=(held,) * 5,
        scratch_shapes=[
            vmem((4, 2, 4, 4, 8, W), f32),
            vmem((4, 2, 4, 4, 8, W), f32),
            vmem((4, 2, 4, 6, 8, W), f32),
            vmem((4, 2, 4, 6, 8, W), f32),
            vmem((4, 2, 4, 8, W), f32),
            vmem((4, 2, 4, 8, W), f32),
            vmem((4 * W, W), f32),
            vmem((4, 4, 4), jnp.int32),
            vmem((4, 4, 12), jnp.int32),
            vmem((4, 4, W), f32),
            vmem((4, 4, 3 * W), f32),
            vmem((4, W), f32),
            vmem((4, W, 3 * W), bf16),
            vmem((4, W, 3 * W), bf16),
            vmem((4, W, 3 * W), bf16),
            vmem((3, W, 3 * W), bf16),
            vmem((4, W, 3 * W), bf16),
            vmem((W, 9 * W), bf16),
            vmem((2, W, 3 * W), bf16),
            vmem((W, 3 * W), bf16),
            vmem((W, 3 * W), bf16),
            vmem((W, 3 * W), bf16),
            vmem((W, 3 * W), bf16),
            vmem((4, 3 * W, 2 * W), bf16),
            vmem((4, 3 * W, W), bf16),
            vmem((4, 3 * W, 2 * W), bf16),
            vmem((3 * W, 2 * W), bf16),
            vmem((18 * W, 2 * W), bf16),
            vmem((3 * W, W), bf16),
            vmem((3 * W, W), bf16),
            vmem((3 * W, W), bf16),
            vmem((3 * W, W), bf16),
            vmem((3 * W, W), bf16),
            vmem((3 * W, W), bf16),
            vmem((3 * W, W), bf16),
            vmem((3 * W, W), bf16),
            vmem((3 * W, W), bf16),
            vmem((4, W, W), f32),
            vmem((W, W), f32),
            vmem((W, W), f32),
            vmem((W, W), f32),
            vmem((W, W), f32),
            vmem((W, W), f32),
            vmem((W, W), f32),
            vmem((W, W), f32),
            vmem((W, W), f32),
            vmem((W, W), f32),
            vmem((W, W), f32),
            vmem((W, W), f32),
            vmem((CHUNKS, PART, W), f32),
            vmem((CHUNKS, PART, W), f32),
            vmem((CHUNKS, PART, W), f32),
            vmem((CHUNKS, PART, W), f32),
            vmem((CHUNKS, PART, W), f32),
            vmem((CHUNKS, PART, W), f32),
            vmem((CHUNKS, PART, W), f32),
            vmem((CHUNKS, PART, W), f32),
            vmem((CHUNKS, PART, W), f32),
            pltpu.SemaphoreType.DMA((104,)),
            pltpu.SemaphoreType.DMA((104,)),
            pltpu.SemaphoreType.DMA((24,)),
            pltpu.SemaphoreType.REGULAR((2,)),
        ],
        compiler_params=pltpu.CompilerParams(
            collective_id=0, has_side_effects=True, vmem_limit_bytes=48 * 1024 * 1024
        ),
    )(*[pltpu.with_memory_space_constraint(a, pltpu.HBM) for a in args])
    out = shape((rows, columns), f32)
    return pl.pallas_call(
        last_kernel,
        out_shape=(out, out),
        in_specs=[held] * 5,
        out_specs=(hbm, hbm),
        scratch_shapes=[vmem((2, rows, columns), f32), pltpu.SemaphoreType.DMA((2, 4))],
        compiler_params=pltpu.CompilerParams(vmem_limit_bytes=16 * 1024 * 1024),
    )(*parts)


def solution(mesh):
    in_specs = (
        P("node", "rhs"),
        P("node", "rhs", None),
        P("node", "rhs", None),
        P("node", None, None),
        P("node", "rhs", None),
        P("node", None, None),
    )
    out_specs = (P("node", "rhs"), P("node", "rhs"))
    return jax.shard_map(on_device, mesh=mesh, in_specs=in_specs, out_specs=out_specs, check_vma=False)
```

```python
import jax
import jax.numpy as jnp
from jax import lax
from jax.experimental import pallas as pl
from jax.experimental.pallas import tpu as pltpu
from jax.sharding import PartitionSpec as P

MESH_ID = pl.DeviceIdType.MESH
B = 64
W = 256
NODES = 8
CHUNKS = 8
PART = W // CHUNKS


class Sems:
    def __init__(self, send, recv, local):
        self.send, self.recv, self.local = send, recv, local
        self.pairs = self.locals = 0

    def pair(self):
        k = self.pairs
        self.pairs += 1
        return self.send.at[k], self.recv.at[k]

    def one(self):
        k = self.locals
        self.locals += 1
        return self.local.at[k]


class Ring:
    def __init__(self, sems, where, pos, device_at, near=False):
        self.where, self.pos, self.near = where, pos, near
        self.opposite = device_at(lax.rem(pos + 2, 4))
        self.up, self.down = device_at(lax.rem(pos + 1, 4)), device_at(lax.rem(pos + 3, 4))
        self.sems = {key: sems.pair() for key in ("u0", "d0", "u1", "d1", "f0", "f1")}
        self.started = {}

    def at(self, q, step):
        return self.where(q, lax.rem(self.pos + step, 4))

    def copy(self, key, q, step, device, source=None):
        part = self.at(q, step)
        send, recv = self.sems[key]
        return pltpu.make_async_remote_copy(
            src_ref=part if source is None else source,
            dst_ref=part,
            send_sem=send,
            recv_sem=recv,
            device_id=device,
            device_id_type=MESH_ID,
        )

    def go(self, key, *args):
        self.started[key] = args
        self.copy(key, *args).start()

    def direct(self, q, source=None):
        if self.near and q == 1:
            self.go("f1", 1, 0, self.opposite, source)
        first, second = ("d", "u") if (q == 0) == self.near else ("u", "d")
        for way in (first, second):
            self.go(f"{way}{q}", q, 0, self.up if way == "u" else self.down, source)

    def arrived(self, key, q, step):
        self.copy(key, q, step, self.up).wait_recv()

    def forward(self, q):
        if self.near:
            if q == 0:
                self.arrived("d0", 0, 1)
                self.go("f0", 0, 1, self.down)
        elif q == 0:
            self.arrived("u0", 0, 3)
            self.go("f0", 0, 3, self.up)
        else:
            self.arrived("d1", 1, 1)
            self.go("f1", 1, 1, self.down)

    def finish(self, q):
        if self.near or q == 1:
            self.arrived(f"u{q}", q, 3)
        if (self.near and q == 1) or (not self.near and q == 0):
            self.arrived(f"d{q}", q, 1)
        self.arrived(f"f{q}", q, 2)

    def sent(self):
        for key, args in self.started.items():
            self.copy(key, *args).wait_send()


class Gather:
    def __init__(self, sems, buf, x, zl, y, device, y_first):
        self.own = buf.at[x, zl, y]

        def layer(q):
            return zl if q == 0 else 1 - zl

        if y_first:
            self.first = Ring(sems, lambda q, p: buf.at[x, layer(q), p], y, lambda p: device(x, zl, p), True)
            self.second = Ring(sems, lambda q, p: buf.at[p, layer(q)], x, lambda p: device(p, zl, y))
        else:
            self.first = Ring(sems, lambda q, p: buf.at[p, layer(q), y], x, lambda p: device(p, zl, y), True)
            self.second = Ring(sems, lambda q, p: buf.at[:, layer(q), p], y, lambda p: device(x, zl, p))
        send, recv = sems.pair()
        self.cross_sems = send, recv
        self.partner = device(x, 1 - zl, y)
        self.other = buf.at[x, 1 - zl, y]

    def cross(self, part, source):
        send, recv = self.cross_sems
        return pltpu.make_async_remote_copy(
            src_ref=source, dst_ref=part, send_sem=send, recv_sem=recv, device_id=self.partner, device_id_type=MESH_ID
        )

    def start(self, source=None):
        source = self.own if source is None else source
        self.sent_cross = self.cross(self.own, source)
        self.sent_cross.start()
        self.first.direct(0, source)

    def crossed(self):
        self.cross(self.other, self.other).wait_recv()
        self.first.direct(1)

    def sent(self):
        self.sent_cross.wait_send()
        self.first.sent()
        self.second.sent()


def split(value):
    high = value.astype(jnp.bfloat16)
    return high, (value - high.astype(jnp.float32)).astype(jnp.bfloat16)


def put_left(ref, value, at=0):
    high, low = split(value)
    for k, part in enumerate((high, low, high)):
        ref[:, at + k * W : at + (k + 1) * W] = part


def put_right(ref, value, col=0, row=0):
    high, low = split(value)
    cols = slice(col, col + value.shape[1])
    for k, part in enumerate((high, high, low)):
        ref[row + k * W : row + (k + 1) * W, cols] = part


def dot(left, right):
    return jnp.dot(left, right, preferred_element_type=jnp.float32)


def panel(buf, s):
    return [(buf[x] if s is None else buf[x, :, :, s]).reshape(B, W) for x in range(4)]


def masked_panel(buf, s, weights):
    return jnp.concatenate([part * weights(x) for x, part in enumerate(panel(buf, s))], axis=0)


def rows_of(pattern):
    block = lax.broadcasted_iota(jnp.int32, (4, W), 1) // B
    values = pattern.astype(jnp.float32)
    out = jnp.zeros((4, W), jnp.float32)
    for k in range(4):
        out = jnp.where(block == k, values[:, k : k + 1], out)
    return out


def kernel(
    r_in, d_in, l_in, pl_in, j_in, pj_in,
    xl, rs, left_x, left_r, right_e,
    gd, gl, gj0, gj1, gn, gp, rv, pat_l, pat_j, ml, mj, mn,
    left_d, left_dt, left_a, left_bt, left_c, left_j, left_e, left_m, left_g, left_w, left_v,
    right_rl, right_lt, right_f, right_b, right_x, right_p, right_q, right_g, right_u, right_c, right_n, right_xc, right_xe, right_xca,
    u, pt, pa, ct, cn, x0, xea, et, xlt, xct, xla, xca, gt, ga, wb, ht, c_in, e_in, c_out, e_out, ea_out,
    send_sem, recv_sem, local_sem, ready_sem,
):
    rhs, node = lax.axis_index("rhs"), lax.axis_index("node")
    x, zl, y = rhs // 8, (rhs // 4) % 2, rhs % 4
    after, before = node + 1, node - 1
    first, last = node == 0, node == NODES - 1
    chip, odd = node // 2, node % 2 == 1
    even = jnp.logical_not(odd)
    partner = node + 1 - 2 * (node % 2)
    two_after, two_before = node + 2, node - 2

    def device(px, pz, py):
        return (px * 8 + pz * 4 + py, node)

    sems = Sems(send_sem, recv_sem, local_sem)

    def load(source, target):
        copy = pltpu.make_async_copy(source, target, sems.one())
        copy.start()
        return copy

    owns = [load(d_in, gd.at[x, zl, y]), load(l_in, gl.at[x, zl, y])]
    barrier = pltpu.get_barrier_semaphore()
    peers = [device(x, 1 - zl, y)]
    peers += [device(x, zl, lax.rem(y + k, 4)) for k in (1, 2, 3)]
    peers += [device(lax.rem(x + k, 4), zl, y) for k in (1, 2, 3)]
    for peer in peers:
        pl.semaphore_signal(barrier, inc=1, device_id=peer, device_id_type=MESH_ID)
    for step in (1, 2):

        @pl.when(node + step < NODES)
        def _():
            pl.semaphore_signal(barrier, inc=1, device_id=(rhs, node + step), device_id_type=MESH_ID)

    for least in (0, 1, 2):

        @pl.when(node == least if least < 2 else node >= 2)
        def _():
            pl.semaphore_wait(barrier, len(peers) + least)

    for step in (1, 2):

        @pl.when(node >= step)
        def _():
            pl.semaphore_signal(ready_sem.at[step - 1], inc=1, device_id=(rhs, node - step), device_id_type=MESH_ID)

    gathers = [
        Gather(sems, gd, x, zl, y, device, True),
        Gather(sems, gl, x, zl, y, device, False),
    ]
    later = [
        Gather(sems, gj0, x, zl, y, device, True),
        Gather(sems, gj1, x, zl, y, device, False),
    ]

    def remote(source, target, pair, to):
        return pltpu.make_async_remote_copy(
            src_ref=source,
            dst_ref=target,
            send_sem=pair[0],
            recv_sem=pair[1],
            device_id=(rhs, to),
            device_id_type=MESH_ID,
        )

    for g, own in zip(gathers, owns):
        own.wait()
        g.start()
    border = [
        remote(ml.at[0], mn, sems.pair(), before),
        remote(gl.at[:, :, :, 0], gn, sems.pair(), before),
        remote(gd.at[:, :, :, 3], gp, sems.pair(), after),
    ]
    pat_loads = [load(pl_in, pat_l), load(pj_in, pat_j)]
    j_loads = []
    for h, gj in enumerate((gj0, gj1)):
        for s in range(2):
            for c in range(3):
                j_loads.append(load(j_in.at[2 * h + s, :, W * c : W * (c + 1)], gj.at[x, zl, y, 3 * s + c]))
    r_load = load(r_in, rv)
    for g in gathers:
        g.crossed()
    for q in (0, 1):
        for g in gathers:
            g.first.forward(q)
    def second_pieces():
        for g in gathers:
            g.second.direct(1)

    for q in (0, 1):
        for g in gathers:
            g.first.finish(q)
            if q == 0:
                g.second.direct(0)
    pl.when(even)(second_pieces)
    r_load.wait()
    for copy in pat_loads + j_loads:
        copy.wait()
    for s in range(4):
        ml[s] = rows_of(pat_l[s])
        for c in range(3):
            mj[s, :, W * c : W * (c + 1)] = rows_of(pat_j[s, :, 4 * c : 4 * (c + 1)])
    def stage(number):
        def run():
            if number < 2:
                for g in later:
                    (g.start, g.crossed)[number]()
                return
            for q in (0, 1):
                for g in later:
                    if number == 2:
                        g.first.forward(q)
                    elif number == 3:
                        g.first.finish(q)
                        g.second.direct(q)
                    else:
                        g.second.forward(q)

        return run

    early = chip > 1
    slow = chip < 2
    pl.when(early)(stage(0))
    for g in gathers:
        g.second.forward(0)
    pl.when(odd)(second_pieces)
    for g in gathers:
        g.second.forward(1)
    pl.when(early)(stage(1))
    for q in (0, 1):
        for g in gathers:
            g.second.finish(q)

    @pl.when(node > 0)
    def _():
        border[0].start()
        border[1].start()

    @pl.when(last)
    def _():
        mn[...] = jnp.zeros_like(mn)
        gn[...] = jnp.zeros_like(gn)

    @pl.when(first)
    def _():
        gp[...] = jnp.zeros_like(gp)


    pl.when(slow)(stage(0))
    pl.when(early)(stage(2))

    for s in range(4):
        d = jnp.concatenate(panel(gd, s), axis=0)
        put_left(left_d.at[s], d)
        low = masked_panel(gl, s, lambda k: ml[s, k : k + 1, :])
        right = right_rl.at[s]
        put_right(right, rv[W * s : W * (s + 1), :])
        put_right(right, low, W)
        both = dot(left_d[s], right[...])
        if s == 0:
            put_right(right_f.at[0], both[:, :W])
            put_right(right_f.at[0], -both[:, W:], W)
        else:
            u[s] = both[:, :W]
            put_left(left_a.at[s], -both[:, W:])
    for s in range(1, 4):
        both = dot(left_a[s], right_f[s - 1])
        fs = u[s] + both[:, :W]
        put_right(right_f.at[s], fs)
        put_right(right_f.at[s], both[:, W:], W)
        if s == 3:
            gt[...] = fs.T.reshape(CHUNKS, PART, W)
            pt[...] = both[:, W:].T

    chunks = [slice(PART * k, PART * (k + 1)) for k in range(CHUNKS)]
    down, fan_down, up, fan_up, join = [[sems.pair() for k in range(CHUNKS)] for _ in range(5)]
    hand = [
        remote(pt, pa, sems.pair(), partner),
        remote(xlt, xla, sems.pair(), partner),
        remote(xct, xca, sems.pair(), partner),
        remote(x0, xea, sems.pair(), partner),
    ]

    def send_g(k):
        return remote(gt.at[k], ga.at[k], join[k], partner)

    def send_down(k):
        return remote(c_out.at[k], c_in.at[k], down[k], two_after)

    def share_down(k):
        return remote(c_in.at[k], c_in.at[k], fan_down[k], partner)

    def send_up(k):
        return remote(e_out.at[k], e_in.at[k], up[k], two_before)

    def share_up(k):
        return remote(ea_out.at[k], e_in.at[k], fan_up[k], partner)

    for step in (1, 2):

        @pl.when(node + step < NODES)
        def _():
            pl.semaphore_wait(ready_sem.at[step - 1], 1)

    @pl.when(even)
    def _():
        for k in range(CHUNKS):
            send_g(k).start()
        hand[0].start()

    @pl.when(chip == 0)
    def _():
        c_in[...] = jnp.zeros_like(c_in)
        left_m[...] = jnp.zeros_like(left_m)

    @pl.when(slow)
    def _():
        stage(1)()
        stage(2)()

    pl.when(early)(stage(3))

    @pl.when(odd)
    def _():
        put_right(right_p, pt[...])
        for k, rows in enumerate(chunks):
            send_g(k).wait_recv()
            put_left(left_w.at[rows], ga[k])
            c_out[k] = gt[k] + dot(left_w[rows, :], right_p[...])

            @pl.when(chip == 0)
            def _():
                send_down(k).start()

        hand[0].wait_recv()
        put_left(left_g, pa[...])
        put_right(right_g, pa[...])
        put_right(right_q, dot(left_g[...], right_p[...]))

    def turn(k):
        rows = chunks[k]
        mine = ga[k] + dot(left_m[rows, :], right_g[...])
        ct[rows, :] = mine
        put_left(left_w.at[rows], mine)
        wb[k] = xlt[rows, :] + dot(left_w[rows, :], right_xc[...])
        put_left(left_v.at[rows], wb[k])
        head = xla[rows, :] + dot(left_m[rows, :], right_xca[...]) + dot(left_v[rows, :], right_xe[...])

        e_out[k] = head
        send_up(k).start()
        ea_out[k] = wb[k]
        share_up(k).start()

    def relay_down():
        for k, rows in enumerate(chunks):
            send_down(k).wait_recv()
            put_left(left_m.at[rows], c_in[k])

            @pl.when(chip < 3)
            def _():
                c_out[k] = c_out[k] + dot(left_m[rows, :], right_q[...])
                send_down(k).start()

            share_down(k).start()
            pl.when(chip == 3)(lambda: turn(k))

    pl.when(chip == 0)(stage(3))
    for s in range(4):
        put_left(left_dt.at[s], jnp.concatenate(panel(gd, s), axis=0).T)
        low = masked_panel(gl, s, lambda k: ml[s, k : k + 1, :])
        if s == 0:
            put_left(left_e.at[0], -low.T)
        else:
            put_right(right_lt.at[s - 1], low.T)
    for s in range(3):
        put_left(left_bt.at[s], -dot(left_dt[s], right_lt[s]))
    for s in range(3, -1, -1):
        both = dot(left_dt[s], right_f[s])
        if s < 3:
            both = both + dot(left_bt[s], right_b[...])
        if s > 0:
            put_right(right_b, both)
        xl[s] = both[:, :W]
        put_left(left_c.at[s], both[:, W:])
        if s == 0:
            xlt[...] = both[:, :W].T
            xct[...] = both[:, W:].T

    @pl.when(even)
    def _():
        hand[1].start()
        hand[2].start()

    @pl.when(odd)
    def _():
        put_right(right_xc, xct[...])

    pl.when(odd & (chip > 0) & (chip < 3))(relay_down)

    pl.when(chip == 1)(stage(3))

    @pl.when(jnp.logical_not(last))
    def _():
        border[0].wait_recv()
        border[1].wait_recv()

    nxt = masked_panel(gn, None, lambda k: mn[k : k + 1, :])
    put_right(right_lt.at[3], nxt.T)
    for s in range(3, -1, -1):
        if s == 3:
            xe = -dot(left_dt[3], right_lt[3])
        else:
            xe = dot(left_bt[s], right_x[3 * W * (s + 2) : 3 * W * (s + 3), W:])
        put_right(right_x, xe, W, 3 * W * (s + 1))
        put_left(left_x.at[s], xe)
        if s == 0:
            x0[...] = xe.T

    @pl.when(even)
    def _():
        hand[3].start()

    @pl.when(odd)
    def _():
        put_right(right_n, x0[...])
        put_left(left_g, x0[...])
        hand[1].wait_recv()
        hand[2].wait_recv()
        put_right(right_xca, xca[...])
        hand[3].wait_recv()
        put_right(right_xe, xea[...])
        put_right(right_u, dot(left_g[...], right_xe[...]))

    pl.when(odd & (chip == 3))(stage(4))
    pl.when(odd & (chip == 3))(relay_down)

    @pl.when(odd & (chip < 3))
    def _():
        mine = ga[...].reshape(W, W) + dot(left_m[...], right_g[...])
        ct[...] = mine
        put_left(left_w, mine)
        mine = xlt[...] + dot(left_w[...], right_xc[...])
        wb[...] = mine.reshape(CHUNKS, PART, W)
        put_left(left_v, mine)
        head = xla[...] + dot(left_m[...], right_xca[...]) + dot(left_v[...], right_xe[...])
        ht[...] = head.reshape(CHUNKS, PART, W)

    @pl.when(even)
    def _():
        @pl.when(chip > 0)
        def _():
            for k in range(CHUNKS):
                share_down(k).wait_recv()

        ct[...] = c_in[...].reshape(W, W)

    @pl.when(jnp.logical_not(last))
    def _():
        border[2].start()

    def prepare():
        cn[...] = ct[...].T
        put_right(right_c, cn[...])
        for s in range(4):
            xl[s] = xl[s] + dot(left_c[s], right_c[...])
            put_right(right_x, xl[s], 0, 3 * W * (s + 1))
        diagonal = lax.broadcasted_iota(jnp.int32, (W, W), 0) == lax.broadcasted_iota(jnp.int32, (W, W), 1)
        put_right(right_x, jnp.zeros((W, W), jnp.float32), 0, 15 * W)
        put_right(right_x, diagonal.astype(jnp.float32), W, 15 * W)
        pl.when(node > 0)(lambda: border[2].wait_recv())
        prev = jnp.concatenate(panel(gp, None), axis=0)
        put_left(left_e.at[1], prev.T)
        both = dot(left_e[0], right_x[3 * W : 6 * W, :])
        put_right(right_b, both[:, :W] + cn[...])
        put_right(right_b, both[:, W:], W)
        both = dot(left_e[1], right_b[...])
        put_right(right_x, jnp.where(first, 0.0, both))
        for q in (0, 1):
            for g in later:
                g.second.finish(q)
        for s in range(4):
            gj = (gj0, gj1)[s // 2]
            for c in range(3):
                block = masked_panel(gj, 3 * (s % 2) + c, lambda k: mj[s, k : k + 1, W * c : W * (c + 1)])
                put_left(left_j, block, 3 * W * c)
            both = dot(left_j[...], right_x[3 * W * s : 3 * W * (s + 3), :])
            rs[W * s : W * (s + 1), :] = rv[W * s : W * (s + 1), :] - both[:, :W]
            put_left(left_r.at[s], -both[:, W:])

    pl.when(even | (chip < 3))(stage(4))
    pl.when(even | (chip == 0))(prepare)

    @pl.when(odd & (chip < 3))
    def _():
        for k, rows in enumerate(chunks):
            send_up(k).wait_recv()
            put_left(left_v.at[rows], e_in[k])

            @pl.when(chip > 0)
            def _():
                e_out[k] = ht[k] + dot(left_v[rows, :], right_u[...])
                send_up(k).start()

            ea_out[k] = wb[k] + dot(left_v[rows, :], right_n[...])
            share_up(k).start()

    pl.when(odd & (chip > 0))(prepare)

    @pl.when(even)
    def _():
        for k in range(CHUNKS):
            share_up(k).wait_recv()

    @pl.when(last)
    def _():
        e_in[...] = jnp.zeros_like(e_in)

    put_right(right_e, e_in[...].reshape(W, W).T)
    for g in gathers + later:
        g.sent()

    @pl.when(node > 0)
    def _():
        border[0].wait_send()
        border[1].wait_send()

    @pl.when(jnp.logical_not(last))
    def _():
        border[2].wait_send()

    def sent(cond, *copies):
        @pl.when(cond)
        def _():
            for copy in copies:
                for k in range(CHUNKS):
                    copy(k).wait_send()

    sent(odd & (chip < 3), send_down)
    sent(odd & (chip > 0), share_down)
    sent(odd & (chip > 0), send_up)
    sent(odd, share_up)
    sent(even, send_g)

    @pl.when(even)
    def _():
        for copy in hand:
            copy.wait_send()


def last_kernel(xl, rs, left_x, left_r, right_e, sol_out, res_out, buf, sem):
    copies = []
    for s in range(4):
        rows = slice(W * s, W * (s + 1))
        for k, (base, left, out) in enumerate(((xl[s], left_x, sol_out), (rs[rows, :], left_r, res_out))):
            buf[k, rows, :] = base + dot(left[s], right_e[...])
            copies.append(pltpu.make_async_copy(buf.at[k, rows], out.at[rows], sem.at[k, s]))
            copies[-1].start()
    for copy in copies:
        copy.wait()


def on_device(*args):
    f32, bf16 = jnp.float32, jnp.bfloat16
    rows, columns = args[0].shape
    hbm, vmem = pl.BlockSpec(memory_space=pltpu.HBM), pltpu.VMEM
    held = pl.BlockSpec(memory_space=vmem)
    shape = jax.ShapeDtypeStruct
    parts = pl.pallas_call(
        kernel,
        out_shape=(
            shape((4, W, W), f32),
            shape((4 * W, W), f32),
            shape((4, W, 3 * W), bf16),
            shape((4, W, 3 * W), bf16),
            shape((3 * W, W), bf16),
        ),
        in_specs=[hbm] * 6,
        out_specs=(held,) * 5,
        scratch_shapes=[
            vmem((4, 2, 4, 4, 8, W), f32),
            vmem((4, 2, 4, 4, 8, W), f32),
            vmem((4, 2, 4, 6, 8, W), f32),
            vmem((4, 2, 4, 6, 8, W), f32),
            vmem((4, 2, 4, 8, W), f32),
            vmem((4, 2, 4, 8, W), f32),
            vmem((4 * W, W), f32),
            vmem((4, 4, 4), jnp.int32),
            vmem((4, 4, 12), jnp.int32),
            vmem((4, 4, W), f32),
            vmem((4, 4, 3 * W), f32),
            vmem((4, W), f32),
            vmem((4, W, 3 * W), bf16),
            vmem((4, W, 3 * W), bf16),
            vmem((4, W, 3 * W), bf16),
            vmem((3, W, 3 * W), bf16),
            vmem((4, W, 3 * W), bf16),
            vmem((W, 9 * W), bf16),
            vmem((2, W, 3 * W), bf16),
            vmem((W, 3 * W), bf16),
            vmem((W, 3 * W), bf16),
            vmem((W, 3 * W), bf16),
            vmem((W, 3 * W), bf16),
            vmem((4, 3 * W, 2 * W), bf16),
            vmem((4, 3 * W, W), bf16),
            vmem((4, 3 * W, 2 * W), bf16),
            vmem((3 * W, 2 * W), bf16),
            vmem((18 * W, 2 * W), bf16),
            vmem((3 * W, W), bf16),
            vmem((3 * W, W), bf16),
            vmem((3 * W, W), bf16),
            vmem((3 * W, W), bf16),
            vmem((3 * W, W), bf16),
            vmem((3 * W, W), bf16),
            vmem((3 * W, W), bf16),
            vmem((3 * W, W), bf16),
            vmem((3 * W, W), bf16),
            vmem((4, W, W), f32),
            vmem((W, W), f32),
            vmem((W, W), f32),
            vmem((W, W), f32),
            vmem((W, W), f32),
            vmem((W, W), f32),
            vmem((W, W), f32),
            vmem((W, W), f32),
            vmem((W, W), f32),
            vmem((W, W), f32),
            vmem((W, W), f32),
            vmem((W, W), f32),
            vmem((CHUNKS, PART, W), f32),
            vmem((CHUNKS, PART, W), f32),
            vmem((CHUNKS, PART, W), f32),
            vmem((CHUNKS, PART, W), f32),
            vmem((CHUNKS, PART, W), f32),
            vmem((CHUNKS, PART, W), f32),
            vmem((CHUNKS, PART, W), f32),
            vmem((CHUNKS, PART, W), f32),
            vmem((CHUNKS, PART, W), f32),
            pltpu.SemaphoreType.DMA((104,)),
            pltpu.SemaphoreType.DMA((104,)),
            pltpu.SemaphoreType.DMA((24,)),
            pltpu.SemaphoreType.REGULAR((2,)),
        ],
        compiler_params=pltpu.CompilerParams(
            collective_id=0, has_side_effects=True, vmem_limit_bytes=48 * 1024 * 1024
        ),
    )(*[pltpu.with_memory_space_constraint(a, pltpu.HBM) for a in args])
    out = shape((rows, columns), f32)
    return pl.pallas_call(
        last_kernel,
        out_shape=(out, out),
        in_specs=[held] * 5,
        out_specs=(hbm, hbm),
        scratch_shapes=[vmem((2, rows, columns), f32), pltpu.SemaphoreType.DMA((2, 4))],
        compiler_params=pltpu.CompilerParams(vmem_limit_bytes=16 * 1024 * 1024),
    )(*parts)


def solution(mesh):
    in_specs = (
        P("node", "rhs"),
        P("node", "rhs", None),
        P("node", "rhs", None),
        P("node", None, None),
        P("node", "rhs", None),
        P("node", None, None),
    )
    out_specs = (P("node", "rhs"), P("node", "rhs"))
    return jax.shard_map(on_device, mesh=mesh, in_specs=in_specs, out_specs=out_specs, check_vma=False)
```
